128 devices in a mesh: rows: 4 (over y_hi, core), cols: 32 (over z, y_lo, x).
Axes of the slice: x: 4, y: 4 (y_hi: 2, y_lo: 2; y = y_hi * 2 + y_lo), z: 4, core: 2. Of those that a mesh axis runs over, the one named last changes fastest.
Arguments:
- stem_out: bfloat16 [64, 128, 4096], P(None, 'rows', 'cols'), may hold values from -6 to 6
- tissue: int32 [2, 64], P(None, 'cols'), may hold values 0 or 1
- w_first: bfloat16 [64, 64], replicated, may hold values from -0.75 to 0.75
- w_reduce: bfloat16 [1, 256, 64], replicated, may hold values from -0.375 to 0.375
- w_mid: bfloat16 [2, 9, 64, 64], replicated, may hold values from -0.25 to 0.25
- w_expand: bfloat16 [2, 64, 256], replicated, may hold values from -0.75 to 0.75
- w_short: bfloat16 [64, 256], replicated, may hold values from -0.75 to 0.75
- gain_mid: float32 [2, 2, 64], replicated, may hold values from 0.5 to 1.5
- shift_mid: float32 [2, 2, 64], replicated, may hold values from -3 to 3
- gain_wide: float32 [2, 256], replicated, may hold values from 0.5 to 1.5
- shift_wide: float32 [2, 256], replicated, may hold values from -3 to 3
- upstream: bfloat16 [256, 128, 4096], P(None, 'rows', 'cols'), may hold values from -6 to 6
Outputs:
- stem_grad: bfloat16 [64, 128, 4096], P(None, 'rows', 'cols')
- param_grads: float32 [144896], replicated
The draws below stay inside these ranges and needn't reach their ends.
All inputs are finite; a program needn't handle non-finite values. No bound on the sum of `tissue` on one device may be relied on, other than what follows from the above.
Results may differ from the reference program's by a relative error of at most 0.017.
Values may be sent and summed in bfloat16 or wider, within the bound.
A program may use at most 128 MiB of HBM per device.

```python
import jax
import jax.numpy as jnp
from jax import lax

MID = 64
WIDE = 256
LEVELS = 2
BLOCK = 64
HEIGHT = 128
BREADTH = 4096


def plant(drawn, stream_key, least, largest):
    index_at = [jax.random.randint(jax.random.fold_in(stream_key, axis), (), 0, length) for axis, length in enumerate(drawn.shape)]
    widest = drawn.shape.index(max(drawn.shape))
    next_to = index_at[:widest] + [(index_at[widest] + 1) % drawn.shape[widest]] + index_at[widest + 1:]
    return drawn.at[tuple(index_at)].set(least).at[tuple(next_to)].set(largest)


def steps_of(stream_key, dims, cuts, smallest, high):
    level = 1.0
    for dim, parts in cuts:
        draws = jax.random.uniform(jax.random.fold_in(jax.random.fold_in(stream_key, 6), dim), (parts,), jnp.float32, smallest / len(cuts), high / len(cuts))
        level = level * jnp.repeat(jnp.exp(draws), dims[dim] // parts).reshape((-1,) + (1,) * (len(dims) - 1 - dim))
    return level


def scatter_about(key, extent, spread, limit, split=(), dtype=jnp.bfloat16):
    array = spread * jax.random.normal(key, extent, jnp.float32)
    if split:
        array = array * steps_of(key, extent, split, -0.22, 0.18)
    return jnp.clip(array, -limit, limit).astype(dtype)


def setup_inputs(seed: int = 0) -> dict:
    seeds = jax.random.split(jax.random.key(seed), 13)
    return {
        "stem_out": scatter_about(seeds[0], (MID, HEIGHT, BREADTH), 1.0, 6.0, ((1, 4), (2, 32))),
        "tissue": plant((jax.random.randint(seeds[1], (HEIGHT // BLOCK, BREADTH // BLOCK), 0, 3) < 2).astype(jnp.int32), jax.random.fold_in(seeds[1], 1), 0, 1),
        "w_first": scatter_about(seeds[2], (MID, MID), MID ** -0.5, 0.75),
        "w_reduce": scatter_about(seeds[3], (LEVELS - 1, WIDE, MID), WIDE ** -0.5, 0.375),
        "w_mid": scatter_about(seeds[4], (LEVELS, 9, MID, MID), (9 * MID) ** -0.5, 0.25),
        "w_expand": scatter_about(seeds[5], (LEVELS, MID, WIDE), MID ** -0.5, 0.75),
        "w_short": scatter_about(seeds[6], (MID, WIDE), MID ** -0.5, 0.75),
        "gain_mid": jnp.clip(1.0 + 0.1 * jax.random.normal(seeds[7], (LEVELS, 2, MID), jnp.float32), 0.5, 1.5),
        "shift_mid": scatter_about(seeds[8], (LEVELS, 2, MID), 0.3, 3.0, (), jnp.float32),
        "gain_wide": jnp.clip(1.0 + 0.1 * jax.random.normal(seeds[9], (LEVELS, WIDE), jnp.float32), 0.5, 1.5),
        "shift_wide": scatter_about(seeds[10], (LEVELS, WIDE), 0.3, 3.0, (), jnp.float32),
        "upstream": scatter_about(seeds[11], (WIDE, HEIGHT, BREADTH), 1.0, 6.0, ((1, 4), (2, 32))),
    }


def pointwise(weight, field):
    return jnp.einsum('cm,chw->mhw', weight.astype(jnp.float32), field.astype(jnp.float32))

def spatial_conv(kernel, padded, height, breadth):
    result = jnp.zeros((kernel.shape[2], height, breadth), jnp.float32)
    for tap_row in range(3):
        for tap_col in range(3):
            window = padded[:, tap_row:tap_row + height, tap_col:tap_col + breadth]
            result = result + pointwise(kernel[3 * tap_row + tap_col], window)
    return result

def per_channel(vector):
    return vector[:, None, None]

def smooth_act(value):
    return value * jax.nn.sigmoid(value)

def smooth_slope(value):
    sigma = jax.nn.sigmoid(value)
    return sigma * (1.0 + value * (1.0 - sigma))

def expand_mask(tissue):
    bands, tiles = tissue.shape
    values = tissue.astype(jnp.float32)[:, None, :, None]
    return jnp.broadcast_to(values, (bands, BLOCK, tiles, BLOCK)).reshape(bands * BLOCK, tiles * BLOCK)

def forward_block(block_index, feature, source, tissue_keep, params):
    w_first, w_reduce, w_mid, w_expand, w_short, gain_mid, shift_mid, gain_wide, shift_wide = params
    w_in = w_first if block_index == 0 else w_reduce[block_index - 1]
    height, breadth = (feature.shape[1], feature.shape[2])
    pre_one = pointwise(w_in, feature)
    act_one = smooth_act(per_channel(gain_mid[block_index, 0]) * pre_one + per_channel(shift_mid[block_index, 0])).astype(jnp.bfloat16)
    padded = jnp.pad(act_one, ((0, 0), (1, 1), (1, 1)))
    pre_two = spatial_conv(w_mid[block_index], padded, height, breadth)
    act_two = smooth_act(per_channel(gain_mid[block_index, 1]) * pre_two + per_channel(shift_mid[block_index, 1])).astype(jnp.bfloat16)
    pre_three = pointwise(w_expand[block_index], act_two)
    if block_index == 0:
        shortcut = pointwise(w_short, source)
    else:
        shortcut = feature.astype(jnp.float32)
    summed = per_channel(gain_wide[block_index]) * pre_three + per_channel(shift_wide[block_index]) + shortcut
    output = (smooth_act(summed) * tissue_keep).astype(jnp.bfloat16)
    return (output, (pre_one, act_one, padded, pre_two, act_two, pre_three, summed))

def reference(stem_out, tissue, w_first, w_reduce, w_mid, w_expand, w_short, gain_mid, shift_mid, gain_wide, shift_wide, upstream):
    params = (w_first, w_reduce, w_mid, w_expand, w_short, gain_mid, shift_mid, gain_wide, shift_wide)
    tissue_keep = expand_mask(tissue)
    height, breadth = (stem_out.shape[1], stem_out.shape[2])
    inputs = [stem_out]
    feature = stem_out
    for block_index in range(LEVELS):
        feature, unused = forward_block(block_index, feature, stem_out, tissue_keep, params)
        inputs.append(feature)
    gradient = upstream
    pieces = [None] * LEVELS
    g_short = None
    for block_index in range(LEVELS - 1, -1, -1):
        feature = inputs[block_index]
        unused, saved = forward_block(block_index, feature, stem_out, tissue_keep, params)
        pre_one, act_one, padded, pre_two, act_two, pre_three, summed = saved
        w_in = w_first if block_index == 0 else w_reduce[block_index - 1]
        d_sum = gradient.astype(jnp.float32) * tissue_keep * smooth_slope(summed)
        d_gain3 = lax.optimization_barrier(jnp.sum(d_sum * pre_three, axis=(1, 2)))
        d_shift3 = lax.optimization_barrier(jnp.sum(d_sum, axis=(1, 2)))
        d_pre3 = (per_channel(gain_wide[block_index]) * d_sum).astype(jnp.bfloat16)
        g_expand = jnp.einsum('mhw,ohw->mo', act_two.astype(jnp.float32), d_pre3.astype(jnp.float32))
        d_act2 = jnp.einsum('mo,ohw->mhw', w_expand[block_index].astype(jnp.float32), d_pre3.astype(jnp.float32))
        d_rel2 = d_act2 * smooth_slope(per_channel(gain_mid[block_index, 1]) * pre_two + per_channel(shift_mid[block_index, 1]))
        d_gain2 = lax.optimization_barrier(jnp.sum(d_rel2 * pre_two, axis=(1, 2)))
        d_shift2 = lax.optimization_barrier(jnp.sum(d_rel2, axis=(1, 2)))
        d_pre2 = (per_channel(gain_mid[block_index, 1]) * d_rel2).astype(jnp.bfloat16)
        taps = []
        for tap_row in range(3):
            for tap_col in range(3):
                window = padded[:, tap_row:tap_row + height, tap_col:tap_col + breadth]
                taps.append(jnp.einsum('chw,mhw->cm', window.astype(jnp.float32), d_pre2.astype(jnp.float32)))
        g_mid = jnp.stack(taps)
        grad_pad = jnp.pad(d_pre2, ((0, 0), (1, 1), (1, 1)))
        d_act1 = jnp.zeros((w_mid.shape[2], height, breadth), jnp.float32)
        for tap_row in range(3):
            for tap_col in range(3):
                window = grad_pad[:, 2 - tap_row:2 - tap_row + height, 2 - tap_col:2 - tap_col + breadth]
                d_act1 = d_act1 + jnp.einsum('cm,mhw->chw', w_mid[block_index, 3 * tap_row + tap_col].astype(jnp.float32), window.astype(jnp.float32))
        d_rel1 = d_act1 * smooth_slope(per_channel(gain_mid[block_index, 0]) * pre_one + per_channel(shift_mid[block_index, 0]))
        d_gain1 = lax.optimization_barrier(jnp.sum(d_rel1 * pre_one, axis=(1, 2)))
        d_shift1 = lax.optimization_barrier(jnp.sum(d_rel1, axis=(1, 2)))
        d_pre1 = (per_channel(gain_mid[block_index, 0]) * d_rel1).astype(jnp.bfloat16)
        g_in = jnp.einsum('chw,mhw->cm', feature.astype(jnp.float32), d_pre1.astype(jnp.float32))
        d_feature = jnp.einsum('cm,mhw->chw', w_in.astype(jnp.float32), d_pre1.astype(jnp.float32))
        if block_index == 0:
            d_short = d_sum.astype(jnp.bfloat16)
            g_short = jnp.einsum('chw,ohw->co', feature.astype(jnp.float32), d_short.astype(jnp.float32))
            d_feature = d_feature + jnp.einsum('co,ohw->chw', w_short.astype(jnp.float32), d_short.astype(jnp.float32))
        else:
            d_feature = d_feature + d_sum
        gradient = d_feature.astype(jnp.bfloat16)
        pieces[block_index] = [g_in, g_mid, g_expand, d_gain1, d_shift1, d_gain2, d_shift2, d_gain3, d_shift3]
    flat = []
    for block_index in range(LEVELS):
        for piece in pieces[block_index]:
            flat.append(piece.reshape(-1))
    flat.append(g_short.reshape(-1))
    scale = 1.0 / jnp.sqrt(jnp.float32(height * breadth))
    param_grads = jnp.concatenate(flat) * scale
    return (gradient, param_grads)
```

```python
import functools
import jax
import jax.numpy as jnp
from jax import lax
from jax.experimental import pallas as pl
from jax.experimental.pallas import tpu as pltpu
from jax.sharding import PartitionSpec as P

MESH = pl.DeviceIdType.MESH


def _sum_kernel(nr, nc, x_ref, o_ref, recv, gathered, mine, rs_send, rs_recv, ag_send, ag_recv, own_sem):
    n = nr * nc
    me = lax.axis_index("rows") * nc + lax.axis_index("cols")

    def dev(p):
        return (p // nc, p % nc)

    barrier = pltpu.get_barrier_semaphore()

    def greet(j, c):
        pl.semaphore_signal(barrier, inc=1, device_id=dev(lax.rem(me + j, n)), device_id_type=MESH)
        return c

    lax.fori_loop(1, n, greet, 0)
    pl.semaphore_wait(barrier, n - 1)

    def scatter_copy(p, s):
        return pltpu.make_async_remote_copy(
            src_ref=x_ref.at[p], dst_ref=recv.at[s], send_sem=rs_send.at[p],
            recv_sem=rs_recv.at[s], device_id=dev(p), device_id_type=MESH)

    def gather_copy(p, s):
        return pltpu.make_async_remote_copy(
            src_ref=gathered.at[s], dst_ref=gathered.at[s], send_sem=ag_send.at[p],
            recv_sem=ag_recv.at[s], device_id=dev(p), device_id_type=MESH)

    def start_scatter(j, c):
        scatter_copy(lax.rem(me + j, n), me).start()
        return c

    lax.fori_loop(1, n, start_scatter, 0)
    recv[me] = x_ref[me]

    def wait_scatter(j, c):
        scatter_copy(me, lax.rem(me + n - j, n)).wait_recv()
        return c

    lax.fori_loop(1, n, wait_scatter, 0)
    total = lax.fori_loop(0, n, lambda s, a: a + recv[s], jnp.zeros(recv.shape[1:], jnp.float32))
    mine[...] = total
    own = pltpu.make_async_copy(mine, gathered.at[me], own_sem)
    own.start()
    own.wait()

    def start_gather(j, c):
        gather_copy(lax.rem(me + j, n), me).start()
        return c

    lax.fori_loop(1, n, start_gather, 0)

    def wait_all(j, c):
        scatter_copy(lax.rem(me + j, n), me).wait_send()
        gather_copy(me, lax.rem(me + n - j, n)).wait_recv()
        gather_copy(lax.rem(me + j, n), me).wait_send()
        return c

    lax.fori_loop(1, n, wait_all, 0)
    o_ref[...] = gathered[...]


def all_sum(vector, nr, nc):
    n = nr * nc
    length = vector.shape[0]
    rows = -(-length // (n * 128))
    blocks = jnp.pad(vector, (0, n * rows * 128 - length)).reshape(n, rows, 128)
    chunk = (n, rows, 128)
    out = pl.pallas_call(
        functools.partial(_sum_kernel, nr, nc),
        out_shape=jax.ShapeDtypeStruct(chunk, jnp.float32),
        in_specs=[pl.BlockSpec(memory_space=pltpu.VMEM)],
        out_specs=pl.BlockSpec(memory_space=pltpu.VMEM),
        scratch_shapes=[
            pltpu.VMEM(chunk, jnp.float32),
            pltpu.VMEM(chunk, jnp.float32),
            pltpu.VMEM((rows, 128), jnp.float32),
            pltpu.SemaphoreType.DMA((n,)),
            pltpu.SemaphoreType.DMA((n,)),
            pltpu.SemaphoreType.DMA((n,)),
            pltpu.SemaphoreType.DMA((n,)),
            pltpu.SemaphoreType.DMA(()),
        ],
        compiler_params=pltpu.CompilerParams(collective_id=0, has_side_effects=True),
    )(blocks)
    return out.reshape(-1)[:length]


BLOCK = 64


def padded_2(cells, sides, width):
    for axis, dim in sides:
        count = lax.axis_size(axis)
        ends = count - 1
        head = lax.slice_in_dim(cells, 0, width, axis=dim)
        tail = lax.slice_in_dim(cells, cells.shape[dim] - width, cells.shape[dim], axis=dim)
        cells = jnp.concatenate(
            [
                lax.ppermute(tail, axis, [(i, (i + 1) % count) for i in range(ends)]),
                cells,
                lax.ppermute(head, axis, [((i + 1) % count, i) for i in range(ends)]),
            ],
            axis=dim,
        )
    return cells


def pointwise(weight, field):
    return jnp.einsum("cm,chw->mhw", weight, field, preferred_element_type=jnp.float32)


def per_channel(vector):
    return vector[:, None, None]


def smooth_act(value):
    return value * jax.nn.sigmoid(value)


def smooth_slope(value):
    sigma = jax.nn.sigmoid(value)
    return sigma * (1.0 + value * (1.0 - sigma))


def spatial_conv(kernel, padded, height, breadth):
    result = jnp.zeros((kernel.shape[2], height, breadth), jnp.float32)
    for tap_row in range(3):
        for tap_col in range(3):
            window = padded[:, tap_row : tap_row + height, tap_col : tap_col + breadth]
            result = result + pointwise(kernel[3 * tap_row + tap_col], window)
    return result


def per_device(
    stem_out,
    tissue,
    w_first,
    w_reduce,
    w_mid,
    w_expand,
    w_short,
    gain_mid,
    shift_mid,
    gain_wide,
    shift_wide,
    upstream,
):
    height, breadth = (stem_out.shape[1], stem_out.shape[2])
    bands, tiles = tissue.shape
    values = tissue.astype(jnp.float32)[:, None, :, None]
    band_keep = jnp.broadcast_to(values, (bands, BLOCK, tiles, BLOCK)).reshape(
        bands * BLOCK, tiles * BLOCK
    )
    row_start = lax.axis_index("rows") * height
    tissue_keep = lax.dynamic_slice_in_dim(band_keep, row_start, height, 0)
    levels = w_mid.shape[0]
    saved_all = []
    feature = stem_out
    for block_index in range(levels):
        w_in = w_first if block_index == 0 else w_reduce[block_index - 1]
        pre_one = pointwise(w_in, feature)
        act_one = smooth_act(
            per_channel(gain_mid[block_index, 0]) * pre_one + per_channel(shift_mid[block_index, 0])
        ).astype(jnp.bfloat16)
        padded = padded_2(act_one, (("rows", 1), ("cols", 2)), 1)
        pre_two = spatial_conv(w_mid[block_index], padded, height, breadth)
        act_two = smooth_act(
            per_channel(gain_mid[block_index, 1]) * pre_two + per_channel(shift_mid[block_index, 1])
        ).astype(jnp.bfloat16)
        pre_three = pointwise(w_expand[block_index], act_two)
        if block_index == 0:
            shortcut = pointwise(w_short, stem_out)
        else:
            shortcut = feature.astype(jnp.float32)
        summed = (
            per_channel(gain_wide[block_index]) * pre_three
            + per_channel(shift_wide[block_index])
            + shortcut
        )
        stored = padded
        saved_all.append((feature, pre_one, stored, pre_two, act_two, pre_three, summed))
        feature = (smooth_act(summed) * tissue_keep).astype(jnp.bfloat16)
    gradient = upstream
    pieces = [None] * levels
    g_short = None
    for block_index in range(levels - 1, -1, -1):
        feature, pre_one, stored, pre_two, act_two, pre_three, summed = saved_all[block_index]
        w_in = w_first if block_index == 0 else w_reduce[block_index - 1]
        d_sum = gradient.astype(jnp.float32) * tissue_keep * smooth_slope(summed)
        d_gain3 = jnp.sum(d_sum * pre_three, axis=(1, 2))
        d_shift3 = jnp.sum(d_sum, axis=(1, 2))
        d_pre3 = (per_channel(gain_wide[block_index]) * d_sum).astype(jnp.bfloat16)
        g_expand = jnp.einsum("mhw,ohw->mo", act_two, d_pre3, preferred_element_type=jnp.float32)
        d_act2 = jnp.einsum(
            "mo,ohw->mhw", w_expand[block_index], d_pre3, preferred_element_type=jnp.float32
        )
        d_rel2 = d_act2 * smooth_slope(
            per_channel(gain_mid[block_index, 1]) * pre_two + per_channel(shift_mid[block_index, 1])
        )
        d_gain2 = jnp.sum(d_rel2 * pre_two, axis=(1, 2))
        d_shift2 = jnp.sum(d_rel2, axis=(1, 2))
        d_pre2 = (per_channel(gain_mid[block_index, 1]) * d_rel2).astype(jnp.bfloat16)
        padded = stored
        taps = []
        for tap_row in range(3):
            for tap_col in range(3):
                window = padded[:, tap_row : tap_row + height, tap_col : tap_col + breadth]
                taps.append(
                    jnp.einsum("chw,mhw->cm", window, d_pre2, preferred_element_type=jnp.float32)
                )
        g_mid = jnp.stack(taps)
        grad_pad = padded_2(d_pre2, (("rows", 1), ("cols", 2)), 1)
        d_act1 = jnp.zeros((w_mid.shape[2], height, breadth), jnp.float32)
        for tap_row in range(3):
            for tap_col in range(3):
                window = grad_pad[
                    :, 2 - tap_row : 2 - tap_row + height, 2 - tap_col : 2 - tap_col + breadth
                ]
                d_act1 = d_act1 + jnp.einsum(
                    "cm,mhw->chw",
                    w_mid[block_index, 3 * tap_row + tap_col],
                    window,
                    preferred_element_type=jnp.float32,
                )
        d_rel1 = d_act1 * smooth_slope(
            per_channel(gain_mid[block_index, 0]) * pre_one + per_channel(shift_mid[block_index, 0])
        )
        d_gain1 = jnp.sum(d_rel1 * pre_one, axis=(1, 2))
        d_shift1 = jnp.sum(d_rel1, axis=(1, 2))
        d_pre1 = (per_channel(gain_mid[block_index, 0]) * d_rel1).astype(jnp.bfloat16)
        g_in = jnp.einsum("chw,mhw->cm", feature, d_pre1, preferred_element_type=jnp.float32)
        d_feature = jnp.einsum("cm,mhw->chw", w_in, d_pre1, preferred_element_type=jnp.float32)
        if block_index == 0:
            d_short = d_sum.astype(jnp.bfloat16)
            g_short = jnp.einsum(
                "chw,ohw->co", feature, d_short, preferred_element_type=jnp.float32
            )
            d_feature = d_feature + jnp.einsum(
                "co,ohw->chw", w_short, d_short, preferred_element_type=jnp.float32
            )
        else:
            d_feature = d_feature + d_sum
        gradient = d_feature.astype(jnp.bfloat16)
        pieces[block_index] = [
            g_in,
            g_mid,
            g_expand,
            d_gain1,
            d_shift1,
            d_gain2,
            d_shift2,
            d_gain3,
            d_shift3,
        ]
    flat = []
    for block_index in range(levels):
        for piece in pieces[block_index]:
            flat.append(piece.reshape(-1))
    flat.append(g_short.reshape(-1))
    partial_vector = jnp.concatenate(flat)
    totals = all_sum(partial_vector, lax.axis_size("rows"), lax.axis_size("cols"))
    pixel_count = height * breadth * lax.axis_size("rows") * lax.axis_size("cols")
    scale = 1.0 / jnp.sqrt(jnp.float32(pixel_count))
    return (gradient, totals * scale)


def solution(mesh):
    in_specs = (
        P(None, "rows", "cols"),
        P(None, "cols"),
        P(),
        P(),
        P(),
        P(),
        P(),
        P(),
        P(),
        P(),
        P(),
        P(None, "rows", "cols"),
    )
    out_specs = (P(None, "rows", "cols"), P())
    return jax.shard_map(
        per_device, mesh=mesh, in_specs=in_specs, out_specs=out_specs, check_vma=False
    )
```

```python
import functools
import jax
import jax.numpy as jnp
from jax import lax
from jax.experimental import pallas as pl
from jax.experimental.pallas import tpu as pltpu
from jax.sharding import PartitionSpec as P

MESH = pl.DeviceIdType.MESH


_TOWARD = ((-1, 0), (1, 0), (0, -1), (0, 1), (-1, -1), (-1, 1), (1, -1), (1, 1))


def _halo_kernel(nr, nc, e_ref, o_ref, send_sem, recv_sem):
    my_r = lax.axis_index("rows")
    my_c = lax.axis_index("cols")

    def present(dr, dc):
        ok = True
        if dr:
            ok = jnp.logical_and(ok, jnp.logical_and(my_r + dr >= 0, my_r + dr < nr))
        if dc:
            ok = jnp.logical_and(ok, jnp.logical_and(my_c + dc >= 0, my_c + dc < nc))
        return ok

    barrier = pltpu.get_barrier_semaphore()
    count = 0
    for dr, dc in _TOWARD:
        there = present(dr, dc)
        count = count + there.astype(jnp.int32)

        @pl.when(there)
        def _():
            pl.semaphore_signal(barrier, inc=1, device_id=(my_r + dr, my_c + dc), device_id_type=MESH)

    pl.semaphore_wait(barrier, count)

    def copy(k, dr, dc):
        return pltpu.make_async_remote_copy(
            src_ref=e_ref.at[k], dst_ref=o_ref.at[k], send_sem=send_sem.at[k],
            recv_sem=recv_sem.at[k], device_id=(my_r + dr, my_c + dc), device_id_type=MESH)

    for k, (dr, dc) in enumerate(_TOWARD):
        @pl.when(present(dr, dc))
        def _():
            copy(k, dr, dc).start()

        @pl.when(jnp.logical_not(present(-dr, -dc)))
        def _():
            o_ref[k] = jnp.zeros(o_ref.shape[1:], o_ref.dtype)

    for k, (dr, dc) in enumerate(_TOWARD):
        @pl.when(present(-dr, -dc))
        def _():
            copy(k, -dr, -dc).wait_recv()

        @pl.when(present(dr, dc))
        def _():
            copy(k, dr, dc).wait_send()


def exchange(cells, nr, nc):
    ch, h, w = cells.shape
    lanes = max(w, -(-h // 128) * 128)

    def wide(v):
        return jnp.pad(v, ((0, 0), (0, lanes - v.shape[1])))

    top, bottom = cells[:, 0, :], cells[:, h - 1, :]
    left, right = cells[:, :, 0], cells[:, :, w - 1]
    pieces = jnp.stack([
        wide(top), wide(bottom), wide(left), wide(right),
        wide(top[:, :1]), wide(top[:, w - 1:]), wide(bottom[:, :1]), wide(bottom[:, w - 1:]),
    ])
    got = pl.pallas_call(
        functools.partial(_halo_kernel, nr, nc),
        out_shape=jax.ShapeDtypeStruct(pieces.shape, pieces.dtype),
        in_specs=[pl.BlockSpec(memory_space=pltpu.VMEM)],
        out_specs=pl.BlockSpec(memory_space=pltpu.VMEM),
        scratch_shapes=[pltpu.SemaphoreType.DMA((8,)), pltpu.SemaphoreType.DMA((8,))],
        compiler_params=pltpu.CompilerParams(collective_id=1, has_side_effects=True),
    )(pieces)
    above = got[1, :, :w]
    below = got[0, :, :w]
    from_left = got[3, :, :h]
    from_right = got[2, :, :h]
    top_row = jnp.concatenate([got[7, :, :1], above, got[6, :, :1]], axis=1)
    bottom_row = jnp.concatenate([got[5, :, :1], below, got[4, :, :1]], axis=1)
    middle = jnp.concatenate([from_left[:, :, None], cells, from_right[:, :, None]], axis=2)
    return jnp.concatenate([top_row[:, None, :], middle, bottom_row[:, None, :]], axis=1)


def _sum_kernel(nr, nc, x_ref, o_ref, recv, gathered, mine, rs_send, rs_recv, ag_send, ag_recv, own_sem):
    n = nr * nc
    me = lax.axis_index("rows") * nc + lax.axis_index("cols")

    def dev(p):
        return (p // nc, p % nc)

    barrier = pltpu.get_barrier_semaphore()

    def greet(j, c):
        pl.semaphore_signal(barrier, inc=1, device_id=dev(lax.rem(me + j, n)), device_id_type=MESH)
        return c

    lax.fori_loop(1, n, greet, 0)
    pl.semaphore_wait(barrier, n - 1)

    def scatter_copy(p, s):
        return pltpu.make_async_remote_copy(
            src_ref=x_ref.at[p], dst_ref=recv.at[s], send_sem=rs_send.at[p],
            recv_sem=rs_recv.at[s], device_id=dev(p), device_id_type=MESH)

    def gather_copy(p, s):
        return pltpu.make_async_remote_copy(
            src_ref=gathered.at[s], dst_ref=gathered.at[s], send_sem=ag_send.at[p],
            recv_sem=ag_recv.at[s], device_id=dev(p), device_id_type=MESH)

    def start_scatter(j, c):
        scatter_copy(lax.rem(me + j, n), me).start()
        return c

    lax.fori_loop(1, n, start_scatter, 0)
    recv[me] = x_ref[me]

    def wait_scatter(j, c):
        scatter_copy(me, lax.rem(me + n - j, n)).wait_recv()
        return c

    lax.fori_loop(1, n, wait_scatter, 0)
    total = lax.fori_loop(0, n, lambda s, a: a + recv[s], jnp.zeros(recv.shape[1:], jnp.float32))
    mine[...] = total
    own = pltpu.make_async_copy(mine, gathered.at[me], own_sem)
    own.start()
    own.wait()

    def start_gather(j, c):
        gather_copy(lax.rem(me + j, n), me).start()
        return c

    lax.fori_loop(1, n, start_gather, 0)

    def wait_all(j, c):
        scatter_copy(lax.rem(me + j, n), me).wait_send()
        gather_copy(me, lax.rem(me + n - j, n)).wait_recv()
        gather_copy(lax.rem(me + j, n), me).wait_send()
        return c

    lax.fori_loop(1, n, wait_all, 0)
    o_ref[...] = gathered[...]


def all_sum(vector, nr, nc):
    n = nr * nc
    length = vector.shape[0]
    rows = -(-length // (n * 128))
    blocks = jnp.pad(vector, (0, n * rows * 128 - length)).reshape(n, rows, 128)
    chunk = (n, rows, 128)
    out = pl.pallas_call(
        functools.partial(_sum_kernel, nr, nc),
        out_shape=jax.ShapeDtypeStruct(chunk, jnp.float32),
        in_specs=[pl.BlockSpec(memory_space=pltpu.VMEM)],
        out_specs=pl.BlockSpec(memory_space=pltpu.VMEM),
        scratch_shapes=[
            pltpu.VMEM(chunk, jnp.float32),
            pltpu.VMEM(chunk, jnp.float32),
            pltpu.VMEM((rows, 128), jnp.float32),
            pltpu.SemaphoreType.DMA((n,)),
            pltpu.SemaphoreType.DMA((n,)),
            pltpu.SemaphoreType.DMA((n,)),
            pltpu.SemaphoreType.DMA((n,)),
            pltpu.SemaphoreType.DMA(()),
        ],
        compiler_params=pltpu.CompilerParams(collective_id=0, has_side_effects=True),
    )(blocks)
    return out.reshape(-1)[:length]


BLOCK = 64


def padded_2(cells, sides, width):
    for axis, dim in sides:
        count = lax.axis_size(axis)
        ends = count - 1
        head = lax.slice_in_dim(cells, 0, width, axis=dim)
        tail = lax.slice_in_dim(cells, cells.shape[dim] - width, cells.shape[dim], axis=dim)
        cells = jnp.concatenate(
            [
                lax.ppermute(tail, axis, [(i, (i + 1) % count) for i in range(ends)]),
                cells,
                lax.ppermute(head, axis, [((i + 1) % count, i) for i in range(ends)]),
            ],
            axis=dim,
        )
    return cells


def pointwise(weight, field):
    return jnp.einsum("cm,chw->mhw", weight, field, preferred_element_type=jnp.float32)


def per_channel(vector):
    return vector[:, None, None]


def smooth_act(value):
    return value * jax.nn.sigmoid(value)


def smooth_slope(value):
    sigma = jax.nn.sigmoid(value)
    return sigma * (1.0 + value * (1.0 - sigma))


def spatial_conv(kernel, padded, height, breadth):
    result = jnp.zeros((kernel.shape[2], height, breadth), jnp.float32)
    for tap_row in range(3):
        for tap_col in range(3):
            window = padded[:, tap_row : tap_row + height, tap_col : tap_col + breadth]
            result = result + pointwise(kernel[3 * tap_row + tap_col], window)
    return result


def per_device(
    stem_out,
    tissue,
    w_first,
    w_reduce,
    w_mid,
    w_expand,
    w_short,
    gain_mid,
    shift_mid,
    gain_wide,
    shift_wide,
    upstream,
):
    height, breadth = (stem_out.shape[1], stem_out.shape[2])
    bands, tiles = tissue.shape
    values = tissue.astype(jnp.float32)[:, None, :, None]
    band_keep = jnp.broadcast_to(values, (bands, BLOCK, tiles, BLOCK)).reshape(
        bands * BLOCK, tiles * BLOCK
    )
    row_start = lax.axis_index("rows") * height
    tissue_keep = lax.dynamic_slice_in_dim(band_keep, row_start, height, 0)
    levels = w_mid.shape[0]
    saved_all = []
    feature = stem_out
    for block_index in range(levels):
        w_in = w_first if block_index == 0 else w_reduce[block_index - 1]
        pre_one = pointwise(w_in, feature)
        act_one = smooth_act(
            per_channel(gain_mid[block_index, 0]) * pre_one + per_channel(shift_mid[block_index, 0])
        ).astype(jnp.bfloat16)
        padded = exchange(act_one, lax.axis_size("rows"), lax.axis_size("cols"))
        pre_two = spatial_conv(w_mid[block_index], padded, height, breadth)
        act_two = smooth_act(
            per_channel(gain_mid[block_index, 1]) * pre_two + per_channel(shift_mid[block_index, 1])
        ).astype(jnp.bfloat16)
        pre_three = pointwise(w_expand[block_index], act_two)
        if block_index == 0:
            shortcut = pointwise(w_short, stem_out)
        else:
            shortcut = feature.astype(jnp.float32)
        summed = (
            per_channel(gain_wide[block_index]) * pre_three
            + per_channel(shift_wide[block_index])
            + shortcut
        )
        stored = padded
        saved_all.append((feature, pre_one, stored, pre_two, act_two, pre_three, summed))
        feature = (smooth_act(summed) * tissue_keep).astype(jnp.bfloat16)
    gradient = upstream
    pieces = [None] * levels
    g_short = None
    for block_index in range(levels - 1, -1, -1):
        feature, pre_one, stored, pre_two, act_two, pre_three, summed = saved_all[block_index]
        w_in = w_first if block_index == 0 else w_reduce[block_index - 1]
        d_sum = gradient.astype(jnp.float32) * tissue_keep * smooth_slope(summed)
        d_gain3 = jnp.sum(d_sum * pre_three, axis=(1, 2))
        d_shift3 = jnp.sum(d_sum, axis=(1, 2))
        d_pre3 = (per_channel(gain_wide[block_index]) * d_sum).astype(jnp.bfloat16)
        g_expand = jnp.einsum("mhw,ohw->mo", act_two, d_pre3, preferred_element_type=jnp.float32)
        d_act2 = jnp.einsum(
            "mo,ohw->mhw", w_expand[block_index], d_pre3, preferred_element_type=jnp.float32
        )
        d_rel2 = d_act2 * smooth_slope(
            per_channel(gain_mid[block_index, 1]) * pre_two + per_channel(shift_mid[block_index, 1])
        )
        d_gain2 = jnp.sum(d_rel2 * pre_two, axis=(1, 2))
        d_shift2 = jnp.sum(d_rel2, axis=(1, 2))
        d_pre2 = (per_channel(gain_mid[block_index, 1]) * d_rel2).astype(jnp.bfloat16)
        padded = stored
        taps = []
        for tap_row in range(3):
            for tap_col in range(3):
                window = padded[:, tap_row : tap_row + height, tap_col : tap_col + breadth]
                taps.append(
                    jnp.einsum("chw,mhw->cm", window, d_pre2, preferred_element_type=jnp.float32)
                )
        g_mid = jnp.stack(taps)
        grad_pad = exchange(d_pre2, lax.axis_size("rows"), lax.axis_size("cols"))
        d_act1 = jnp.zeros((w_mid.shape[2], height, breadth), jnp.float32)
        for tap_row in range(3):
            for tap_col in range(3):
                window = grad_pad[
                    :, 2 - tap_row : 2 - tap_row + height, 2 - tap_col : 2 - tap_col + breadth
                ]
                d_act1 = d_act1 + jnp.einsum(
                    "cm,mhw->chw",
                    w_mid[block_index, 3 * tap_row + tap_col],
                    window,
                    preferred_element_type=jnp.float32,
                )
        d_rel1 = d_act1 * smooth_slope(
            per_channel(gain_mid[block_index, 0]) * pre_one + per_channel(shift_mid[block_index, 0])
        )
        d_gain1 = jnp.sum(d_rel1 * pre_one, axis=(1, 2))
        d_shift1 = jnp.sum(d_rel1, axis=(1, 2))
        d_pre1 = (per_channel(gain_mid[block_index, 0]) * d_rel1).astype(jnp.bfloat16)
        g_in = jnp.einsum("chw,mhw->cm", feature, d_pre1, preferred_element_type=jnp.float32)
        d_feature = jnp.einsum("cm,mhw->chw", w_in, d_pre1, preferred_element_type=jnp.float32)
        if block_index == 0:
            d_short = d_sum.astype(jnp.bfloat16)
            g_short = jnp.einsum(
                "chw,ohw->co", feature, d_short, preferred_element_type=jnp.float32
            )
            d_feature = d_feature + jnp.einsum(
                "co,ohw->chw", w_short, d_short, preferred_element_type=jnp.float32
            )
        else:
            d_feature = d_feature + d_sum
        gradient = d_feature.astype(jnp.bfloat16)
        pieces[block_index] = [
            g_in,
            g_mid,
            g_expand,
            d_gain1,
            d_shift1,
            d_gain2,
            d_shift2,
            d_gain3,
            d_shift3,
        ]
    flat = []
    for block_index in range(levels):
        for piece in pieces[block_index]:
            flat.append(piece.reshape(-1))
    flat.append(g_short.reshape(-1))
    partial_vector = jnp.concatenate(flat)
    totals = all_sum(partial_vector, lax.axis_size("rows"), lax.axis_size("cols"))
    pixel_count = height * breadth * lax.axis_size("rows") * lax.axis_size("cols")
    scale = 1.0 / jnp.sqrt(jnp.float32(pixel_count))
    return (gradient, totals * scale)


def solution(mesh):
    in_specs = (
        P(None, "rows", "cols"),
        P(None, "cols"),
        P(),
        P(),
        P(),
        P(),
        P(),
        P(),
        P(),
        P(),
        P(),
        P(None, "rows", "cols"),
    )
    out_specs = (P(None, "rows", "cols"), P())
    return jax.shard_map(
        per_device, mesh=mesh, in_specs=in_specs, out_specs=out_specs, check_vma=False
    )
```

```python
import functools
import jax
import jax.numpy as jnp
from jax import lax
from jax.experimental import pallas as pl
from jax.experimental.pallas import tpu as pltpu
from jax.sharding import PartitionSpec as P

MESH = pl.DeviceIdType.MESH


_TOWARD = ((-1, 0), (1, 0), (0, -1), (0, 1), (-1, -1), (-1, 1), (1, -1), (1, 1))


def _halo_kernel(nr, nc, e_ref, o_ref, send_sem, recv_sem):
    my_r = lax.axis_index("rows")
    my_c = lax.axis_index("cols")

    def present(dr, dc):
        ok = True
        if dr:
            ok = jnp.logical_and(ok, jnp.logical_and(my_r + dr >= 0, my_r + dr < nr))
        if dc:
            ok = jnp.logical_and(ok, jnp.logical_and(my_c + dc >= 0, my_c + dc < nc))
        return ok

    barrier = pltpu.get_barrier_semaphore()
    count = 0
    for dr, dc in _TOWARD:
        there = present(dr, dc)
        count = count + there.astype(jnp.int32)

        @pl.when(there)
        def _():
            pl.semaphore_signal(barrier, inc=1, device_id=(my_r + dr, my_c + dc), device_id_type=MESH)

    pl.semaphore_wait(barrier, count)

    def copy(k, dr, dc):
        return pltpu.make_async_remote_copy(
            src_ref=e_ref.at[k], dst_ref=o_ref.at[k], send_sem=send_sem.at[k],
            recv_sem=recv_sem.at[k], device_id=(my_r + dr, my_c + dc), device_id_type=MESH)

    for k, (dr, dc) in enumerate(_TOWARD):
        @pl.when(present(dr, dc))
        def _():
            copy(k, dr, dc).start()

        @pl.when(jnp.logical_not(present(-dr, -dc)))
        def _():
            o_ref[k] = jnp.zeros(o_ref.shape[1:], o_ref.dtype)

    for k, (dr, dc) in enumerate(_TOWARD):
        @pl.when(present(-dr, -dc))
        def _():
            copy(k, -dr, -dc).wait_recv()

        @pl.when(present(dr, dc))
        def _():
            copy(k, dr, dc).wait_send()


def exchange(cells, nr, nc):
    ch, h, w = cells.shape
    lanes = max(w, -(-h // 128) * 128)

    def wide(v):
        return jnp.pad(v, ((0, 0), (0, lanes - v.shape[1])))

    top, bottom = cells[:, 0, :], cells[:, h - 1, :]
    left, right = cells[:, :, 0], cells[:, :, w - 1]
    pieces = jnp.stack([
        wide(top), wide(bottom), wide(left), wide(right),
        wide(top[:, :1]), wide(top[:, w - 1:]), wide(bottom[:, :1]), wide(bottom[:, w - 1:]),
    ])
    got = pl.pallas_call(
        functools.partial(_halo_kernel, nr, nc),
        out_shape=jax.ShapeDtypeStruct(pieces.shape, pieces.dtype),
        in_specs=[pl.BlockSpec(memory_space=pltpu.VMEM)],
        out_specs=pl.BlockSpec(memory_space=pltpu.VMEM),
        scratch_shapes=[pltpu.SemaphoreType.DMA((8,)), pltpu.SemaphoreType.DMA((8,))],
        compiler_params=pltpu.CompilerParams(collective_id=1, has_side_effects=True),
    )(pieces)
    above = got[1, :, :w]
    below = got[0, :, :w]
    from_left = got[3, :, :h]
    from_right = got[2, :, :h]
    top_row = jnp.concatenate([got[7, :, :1], above, got[6, :, :1]], axis=1)
    bottom_row = jnp.concatenate([got[5, :, :1], below, got[4, :, :1]], axis=1)
    middle = jnp.concatenate([from_left[:, :, None], cells, from_right[:, :, None]], axis=2)
    return jnp.concatenate([top_row[:, None, :], middle, bottom_row[:, None, :]], axis=1)


def _sum_kernel(nr, nc, x_ref, o_ref, recv, gathered, mine, rs_send, rs_recv, ag_send, ag_recv, own_sem):
    n = nr * nc
    me = lax.axis_index("rows") * nc + lax.axis_index("cols")

    def dev(p):
        return (p // nc, p % nc)

    barrier = pltpu.get_barrier_semaphore()

    def greet(j, c):
        pl.semaphore_signal(barrier, inc=1, device_id=dev(lax.rem(me + j, n)), device_id_type=MESH)
        return c

    lax.fori_loop(1, n, greet, 0)
    pl.semaphore_wait(barrier, n - 1)

    def scatter_copy(p, s):
        return pltpu.make_async_remote_copy(
            src_ref=x_ref.at[p], dst_ref=recv.at[s], send_sem=rs_send.at[p],
            recv_sem=rs_recv.at[s], device_id=dev(p), device_id_type=MESH)

    def gather_copy(p, s):
        return pltpu.make_async_remote_copy(
            src_ref=gathered.at[s], dst_ref=gathered.at[s], send_sem=ag_send.at[p],
            recv_sem=ag_recv.at[s], device_id=dev(p), device_id_type=MESH)

    def start_scatter(j, c):
        scatter_copy(lax.rem(me + j, n), me).start()
        return c

    lax.fori_loop(1, n, start_scatter, 0)
    recv[me] = x_ref[me]

    def wait_scatter(j, c):
        scatter_copy(me, lax.rem(me + n - j, n)).wait_recv()
        return c

    lax.fori_loop(1, n, wait_scatter, 0)
    total = lax.fori_loop(0, n, lambda s, a: a + recv[s], jnp.zeros(recv.shape[1:], jnp.float32))
    mine[...] = total
    own = pltpu.make_async_copy(mine, gathered.at[me], own_sem)
    own.start()
    own.wait()

    def start_gather(j, c):
        gather_copy(lax.rem(me + j, n), me).start()
        return c

    lax.fori_loop(1, n, start_gather, 0)

    def wait_all(j, c):
        scatter_copy(lax.rem(me + j, n), me).wait_send()
        gather_copy(me, lax.rem(me + n - j, n)).wait_recv()
        gather_copy(lax.rem(me + j, n), me).wait_send()
        return c

    lax.fori_loop(1, n, wait_all, 0)
    o_ref[...] = gathered[...]


def all_sum(vector, nr, nc):
    n = nr * nc
    length = vector.shape[0]
    rows = -(-length // (n * 128))
    blocks = jnp.pad(vector, (0, n * rows * 128 - length)).reshape(n, rows, 128)
    chunk = (n, rows, 128)
    out = pl.pallas_call(
        functools.partial(_sum_kernel, nr, nc),
        out_shape=jax.ShapeDtypeStruct(chunk, jnp.float32),
        in_specs=[pl.BlockSpec(memory_space=pltpu.VMEM)],
        out_specs=pl.BlockSpec(memory_space=pltpu.VMEM),
        scratch_shapes=[
            pltpu.VMEM(chunk, jnp.float32),
            pltpu.VMEM(chunk, jnp.float32),
            pltpu.VMEM((rows, 128), jnp.float32),
            pltpu.SemaphoreType.DMA((n,)),
            pltpu.SemaphoreType.DMA((n,)),
            pltpu.SemaphoreType.DMA((n,)),
            pltpu.SemaphoreType.DMA((n,)),
            pltpu.SemaphoreType.DMA(()),
        ],
        compiler_params=pltpu.CompilerParams(collective_id=0, has_side_effects=True),
    )(blocks)
    return out.reshape(-1)[:length]


BLOCK = 64


def padded_2(cells, sides, width):
    for axis, dim in sides:
        count = lax.axis_size(axis)
        ends = count - 1
        head = lax.slice_in_dim(cells, 0, width, axis=dim)
        tail = lax.slice_in_dim(cells, cells.shape[dim] - width, cells.shape[dim], axis=dim)
        cells = jnp.concatenate(
            [
                lax.ppermute(tail, axis, [(i, (i + 1) % count) for i in range(ends)]),
                cells,
                lax.ppermute(head, axis, [((i + 1) % count, i) for i in range(ends)]),
            ],
            axis=dim,
        )
    return cells


def pointwise(weight, field):
    return jnp.einsum("cm,chw->mhw", weight, field, preferred_element_type=jnp.float32)


def per_channel(vector):
    return vector[:, None, None]


def smooth_act(value):
    return value * jax.nn.sigmoid(value)


def smooth_slope(value):
    sigma = jax.nn.sigmoid(value)
    return sigma * (1.0 + value * (1.0 - sigma))


def spatial_conv(kernel, padded, height, breadth):
    result = jnp.zeros((kernel.shape[2], height, breadth), jnp.float32)
    for tap_row in range(3):
        for tap_col in range(3):
            window = padded[:, tap_row : tap_row + height, tap_col : tap_col + breadth]
            result = result + pointwise(kernel[3 * tap_row + tap_col], window)
    return result


def conv3(kernel_hwio, padded):
    out = lax.conv_general_dilated(
        padded[None], kernel_hwio, (1, 1), "VALID",
        dimension_numbers=("NCHW", "HWIO", "NCHW"), preferred_element_type=jnp.float32,
    )
    return out[0]


def conv_weight_grad(padded, grad):
    out = lax.conv_general_dilated(
        padded[None], grad[None], (1, 1), "VALID",
        dimension_numbers=("CNHW", "IOHW", "NCHW"), preferred_element_type=jnp.float32,
    )
    return jnp.transpose(out, (2, 3, 0, 1)).reshape(9, padded.shape[0], grad.shape[0])


def per_device(
    stem_out,
    tissue,
    w_first,
    w_reduce,
    w_mid,
    w_expand,
    w_short,
    gain_mid,
    shift_mid,
    gain_wide,
    shift_wide,
    upstream,
):
    height, breadth = (stem_out.shape[1], stem_out.shape[2])
    bands, tiles = tissue.shape
    values = tissue.astype(jnp.float32)[:, None, :, None]
    band_keep = jnp.broadcast_to(values, (bands, BLOCK, tiles, BLOCK)).reshape(
        bands * BLOCK, tiles * BLOCK
    )
    row_start = lax.axis_index("rows") * height
    tissue_keep = lax.dynamic_slice_in_dim(band_keep, row_start, height, 0)
    levels = w_mid.shape[0]
    saved_all = []
    feature = stem_out
    for block_index in range(levels):
        w_in = w_first if block_index == 0 else w_reduce[block_index - 1]
        pre_one = pointwise(w_in, feature)
        act_one = smooth_act(
            per_channel(gain_mid[block_index, 0]) * pre_one + per_channel(shift_mid[block_index, 0])
        ).astype(jnp.bfloat16)
        padded = exchange(act_one, lax.axis_size("rows"), lax.axis_size("cols"))
        pre_two = conv3(w_mid[block_index].reshape(3, 3, w_mid.shape[2], w_mid.shape[3]), padded)
        act_two = smooth_act(
            per_channel(gain_mid[block_index, 1]) * pre_two + per_channel(shift_mid[block_index, 1])
        ).astype(jnp.bfloat16)
        pre_three = pointwise(w_expand[block_index], act_two)
        if block_index == 0:
            shortcut = pointwise(w_short, stem_out)
        else:
            shortcut = feature.astype(jnp.float32)
        summed = (
            per_channel(gain_wide[block_index]) * pre_three
            + per_channel(shift_wide[block_index])
            + shortcut
        )
        stored = padded
        saved_all.append((feature, pre_one, stored, pre_two, act_two, pre_three, summed))
        feature = (smooth_act(summed) * tissue_keep).astype(jnp.bfloat16)
    gradient = upstream
    pieces = [None] * levels
    g_short = None
    for block_index in range(levels - 1, -1, -1):
        feature, pre_one, stored, pre_two, act_two, pre_three, summed = saved_all[block_index]
        w_in = w_first if block_index == 0 else w_reduce[block_index - 1]
        d_sum = gradient.astype(jnp.float32) * tissue_keep * smooth_slope(summed)
        d_gain3 = jnp.sum(d_sum * pre_three, axis=(1, 2))
        d_shift3 = jnp.sum(d_sum, axis=(1, 2))
        d_pre3 = (per_channel(gain_wide[block_index]) * d_sum).astype(jnp.bfloat16)
        g_expand = jnp.einsum("mhw,ohw->mo", act_two, d_pre3, preferred_element_type=jnp.float32)
        d_act2 = jnp.einsum(
            "mo,ohw->mhw", w_expand[block_index], d_pre3, preferred_element_type=jnp.float32
        )
        d_rel2 = d_act2 * smooth_slope(
            per_channel(gain_mid[block_index, 1]) * pre_two + per_channel(shift_mid[block_index, 1])
        )
        d_gain2 = jnp.sum(d_rel2 * pre_two, axis=(1, 2))
        d_shift2 = jnp.sum(d_rel2, axis=(1, 2))
        d_pre2 = (per_channel(gain_mid[block_index, 1]) * d_rel2).astype(jnp.bfloat16)
        padded = stored
        g_mid = conv_weight_grad(padded, d_pre2)
        grad_pad = exchange(d_pre2, lax.axis_size("rows"), lax.axis_size("cols"))
        flipped = w_mid[block_index].reshape(3, 3, w_mid.shape[2], w_mid.shape[3])[::-1, ::-1]
        d_act1 = conv3(jnp.swapaxes(flipped, 2, 3), grad_pad)
        d_rel1 = d_act1 * smooth_slope(
            per_channel(gain_mid[block_index, 0]) * pre_one + per_channel(shift_mid[block_index, 0])
        )
        d_gain1 = jnp.sum(d_rel1 * pre_one, axis=(1, 2))
        d_shift1 = jnp.sum(d_rel1, axis=(1, 2))
        d_pre1 = (per_channel(gain_mid[block_index, 0]) * d_rel1).astype(jnp.bfloat16)
        g_in = jnp.einsum("chw,mhw->cm", feature, d_pre1, preferred_element_type=jnp.float32)
        d_feature = jnp.einsum("cm,mhw->chw", w_in, d_pre1, preferred_element_type=jnp.float32)
        if block_index == 0:
            d_short = d_sum.astype(jnp.bfloat16)
            g_short = jnp.einsum(
                "chw,ohw->co", feature, d_short, preferred_element_type=jnp.float32
            )
            d_feature = d_feature + jnp.einsum(
                "co,ohw->chw", w_short, d_short, preferred_element_type=jnp.float32
            )
        else:
            d_feature = d_feature + d_sum
        gradient = d_feature.astype(jnp.bfloat16)
        pieces[block_index] = [
            g_in,
            g_mid,
            g_expand,
            d_gain1,
            d_shift1,
            d_gain2,
            d_shift2,
            d_gain3,
            d_shift3,
        ]
    flat = []
    for block_index in range(levels):
        for piece in pieces[block_index]:
            flat.append(piece.reshape(-1))
    flat.append(g_short.reshape(-1))
    partial_vector = jnp.concatenate(flat)
    totals = all_sum(partial_vector, lax.axis_size("rows"), lax.axis_size("cols"))
    pixel_count = height * breadth * lax.axis_size("rows") * lax.axis_size("cols")
    scale = 1.0 / jnp.sqrt(jnp.float32(pixel_count))
    return (gradient, totals * scale)


def solution(mesh):
    in_specs = (
        P(None, "rows", "cols"),
        P(None, "cols"),
        P(),
        P(),
        P(),
        P(),
        P(),
        P(),
        P(),
        P(),
        P(),
        P(None, "rows", "cols"),
    )
    out_specs = (P(None, "rows", "cols"), P())
    return jax.shard_map(
        per_device, mesh=mesh, in_specs=in_specs, out_specs=out_specs, check_vma=False
    )
```

```python
import functools
import jax
import jax.numpy as jnp
from jax import lax
from jax.experimental import pallas as pl
from jax.experimental.pallas import tpu as pltpu
from jax.sharding import PartitionSpec as P

MESH = pl.DeviceIdType.MESH


_TOWARD = ((-1, 0), (1, 0), (0, -1), (0, 1), (-1, -1), (-1, 1), (1, -1), (1, 1))


def _halo_kernel(nr, nc, e_ref, o_ref, send_sem, recv_sem):
    my_r = lax.axis_index("rows")
    my_c = lax.axis_index("cols")

    def present(dr, dc):
        ok = True
        if dr:
            ok = jnp.logical_and(ok, jnp.logical_and(my_r + dr >= 0, my_r + dr < nr))
        if dc:
            ok = jnp.logical_and(ok, jnp.logical_and(my_c + dc >= 0, my_c + dc < nc))
        return ok

    barrier = pltpu.get_barrier_semaphore()
    count = 0
    for dr, dc in _TOWARD:
        there = present(dr, dc)
        count = count + there.astype(jnp.int32)

        @pl.when(there)
        def _():
            pl.semaphore_signal(barrier, inc=1, device_id=(my_r + dr, my_c + dc), device_id_type=MESH)

    pl.semaphore_wait(barrier, count)

    def copy(k, dr, dc):
        return pltpu.make_async_remote_copy(
            src_ref=e_ref.at[k], dst_ref=o_ref.at[k], send_sem=send_sem.at[k],
            recv_sem=recv_sem.at[k], device_id=(my_r + dr, my_c + dc), device_id_type=MESH)

    for k, (dr, dc) in enumerate(_TOWARD):
        @pl.when(present(dr, dc))
        def _():
            copy(k, dr, dc).start()

        @pl.when(jnp.logical_not(present(-dr, -dc)))
        def _():
            o_ref[k] = jnp.zeros(o_ref.shape[1:], o_ref.dtype)

    for k, (dr, dc) in enumerate(_TOWARD):
        @pl.when(present(-dr, -dc))
        def _():
            copy(k, -dr, -dc).wait_recv()

        @pl.when(present(dr, dc))
        def _():
            copy(k, dr, dc).wait_send()


def exchange(cells, nr, nc):
    ch, h, w = cells.shape
    lanes = max(w, -(-h // 128) * 128)

    def wide(v):
        return jnp.pad(v, ((0, 0), (0, lanes - v.shape[1])))

    top, bottom = cells[:, 0, :], cells[:, h - 1, :]
    left, right = cells[:, :, 0], cells[:, :, w - 1]
    pieces = jnp.stack([
        wide(top), wide(bottom), wide(left), wide(right),
        wide(top[:, :1]), wide(top[:, w - 1:]), wide(bottom[:, :1]), wide(bottom[:, w - 1:]),
    ])
    got = pl.pallas_call(
        functools.partial(_halo_kernel, nr, nc),
        out_shape=jax.ShapeDtypeStruct(pieces.shape, pieces.dtype),
        in_specs=[pl.BlockSpec(memory_space=pltpu.VMEM)],
        out_specs=pl.BlockSpec(memory_space=pltpu.VMEM),
        scratch_shapes=[pltpu.SemaphoreType.DMA((8,)), pltpu.SemaphoreType.DMA((8,))],
        compiler_params=pltpu.CompilerParams(collective_id=1, has_side_effects=True),
    )(pieces)
    above = got[1, :, :w]
    below = got[0, :, :w]
    from_left = got[3, :, :h]
    from_right = got[2, :, :h]
    top_row = jnp.concatenate([got[7, :, :1], above, got[6, :, :1]], axis=1)
    bottom_row = jnp.concatenate([got[5, :, :1], below, got[4, :, :1]], axis=1)
    middle = jnp.concatenate([from_left[:, :, None], cells, from_right[:, :, None]], axis=2)
    return jnp.concatenate([top_row[:, None, :], middle, bottom_row[:, None, :]], axis=1)


def _sum_kernel(nr, nc, x_ref, o_ref, recv, gathered, mine, rs_send, rs_recv, ag_send, ag_recv, own_sem):
    n = nr * nc
    me = lax.axis_index("rows") * nc + lax.axis_index("cols")

    def dev(p):
        return (p // nc, p % nc)

    barrier = pltpu.get_barrier_semaphore()

    def greet(j, c):
        pl.semaphore_signal(barrier, inc=1, device_id=dev(lax.rem(me + j, n)), device_id_type=MESH)
        return c

    lax.fori_loop(1, n, greet, 0)
    pl.semaphore_wait(barrier, n - 1)

    def scatter_copy(p, s):
        return pltpu.make_async_remote_copy(
            src_ref=x_ref.at[p], dst_ref=recv.at[s], send_sem=rs_send.at[p],
            recv_sem=rs_recv.at[s], device_id=dev(p), device_id_type=MESH)

    def gather_copy(p, s):
        return pltpu.make_async_remote_copy(
            src_ref=gathered.at[s], dst_ref=gathered.at[s], send_sem=ag_send.at[p],
            recv_sem=ag_recv.at[s], device_id=dev(p), device_id_type=MESH)

    def start_scatter(j, c):
        scatter_copy(lax.rem(me + j, n), me).start()
        return c

    lax.fori_loop(1, n, start_scatter, 0)
    recv[me] = x_ref[me]

    def wait_scatter(j, c):
        scatter_copy(me, lax.rem(me + n - j, n)).wait_recv()
        return c

    lax.fori_loop(1, n, wait_scatter, 0)
    total = lax.fori_loop(0, n, lambda s, a: a + recv[s], jnp.zeros(recv.shape[1:], jnp.float32))
    mine[...] = total
    own = pltpu.make_async_copy(mine, gathered.at[me], own_sem)
    own.start()
    own.wait()

    def start_gather(j, c):
        gather_copy(lax.rem(me + j, n), me).start()
        return c

    lax.fori_loop(1, n, start_gather, 0)

    def wait_all(j, c):
        scatter_copy(lax.rem(me + j, n), me).wait_send()
        gather_copy(me, lax.rem(me + n - j, n)).wait_recv()
        gather_copy(lax.rem(me + j, n), me).wait_send()
        return c

    lax.fori_loop(1, n, wait_all, 0)
    o_ref[...] = gathered[...]


def all_sum(vector, nr, nc):
    n = nr * nc
    length = vector.shape[0]
    rows = -(-length // (n * 128))
    blocks = jnp.pad(vector, (0, n * rows * 128 - length)).reshape(n, rows, 128)
    chunk = (n, rows, 128)
    out = pl.pallas_call(
        functools.partial(_sum_kernel, nr, nc),
        out_shape=jax.ShapeDtypeStruct(chunk, jnp.float32),
        in_specs=[pl.BlockSpec(memory_space=pltpu.VMEM)],
        out_specs=pl.BlockSpec(memory_space=pltpu.VMEM),
        scratch_shapes=[
            pltpu.VMEM(chunk, jnp.float32),
            pltpu.VMEM(chunk, jnp.float32),
            pltpu.VMEM((rows, 128), jnp.float32),
            pltpu.SemaphoreType.DMA((n,)),
            pltpu.SemaphoreType.DMA((n,)),
            pltpu.SemaphoreType.DMA((n,)),
            pltpu.SemaphoreType.DMA((n,)),
            pltpu.SemaphoreType.DMA(()),
        ],
        compiler_params=pltpu.CompilerParams(collective_id=0, has_side_effects=True),
    )(blocks)
    return out.reshape(-1)[:length]


BLOCK = 64


def padded_2(cells, sides, width):
    for axis, dim in sides:
        count = lax.axis_size(axis)
        ends = count - 1
        head = lax.slice_in_dim(cells, 0, width, axis=dim)
        tail = lax.slice_in_dim(cells, cells.shape[dim] - width, cells.shape[dim], axis=dim)
        cells = jnp.concatenate(
            [
                lax.ppermute(tail, axis, [(i, (i + 1) % count) for i in range(ends)]),
                cells,
                lax.ppermute(head, axis, [((i + 1) % count, i) for i in range(ends)]),
            ],
            axis=dim,
        )
    return cells


def pointwise(weight, field):
    return jnp.einsum("cm,chw->mhw", weight, field, preferred_element_type=jnp.float32)


def per_channel(vector):
    return vector[:, None, None]


def smooth_act(value):
    return value * jax.nn.sigmoid(value)


def smooth_slope(value):
    sigma = jax.nn.sigmoid(value)
    return sigma * (1.0 + value * (1.0 - sigma))


def spatial_conv(kernel, padded, height, breadth):
    result = jnp.zeros((kernel.shape[2], height, breadth), jnp.float32)
    for tap_row in range(3):
        for tap_col in range(3):
            window = padded[:, tap_row : tap_row + height, tap_col : tap_col + breadth]
            result = result + pointwise(kernel[3 * tap_row + tap_col], window)
    return result


def windows(padded, height, breadth, flip):
    taps = []
    for tap_row in range(3):
        for tap_col in range(3):
            i, j = (2 - tap_row, 2 - tap_col) if flip else (tap_row, tap_col)
            taps.append(padded[:, i : i + height, j : j + breadth])
    return jnp.concatenate(taps, axis=0)


def per_device(
    stem_out,
    tissue,
    w_first,
    w_reduce,
    w_mid,
    w_expand,
    w_short,
    gain_mid,
    shift_mid,
    gain_wide,
    shift_wide,
    upstream,
):
    height, breadth = (stem_out.shape[1], stem_out.shape[2])
    bands, tiles = tissue.shape
    values = tissue.astype(jnp.float32)[:, None, :, None]
    band_keep = jnp.broadcast_to(values, (bands, BLOCK, tiles, BLOCK)).reshape(
        bands * BLOCK, tiles * BLOCK
    )
    row_start = lax.axis_index("rows") * height
    tissue_keep = lax.dynamic_slice_in_dim(band_keep, row_start, height, 0)
    levels = w_mid.shape[0]
    saved_all = []
    feature = stem_out
    for block_index in range(levels):
        w_in = w_first if block_index == 0 else w_reduce[block_index - 1]
        pre_one = pointwise(w_in, feature)
        act_one = smooth_act(
            per_channel(gain_mid[block_index, 0]) * pre_one + per_channel(shift_mid[block_index, 0])
        ).astype(jnp.bfloat16)
        padded = exchange(act_one, lax.axis_size("rows"), lax.axis_size("cols"))
        stacked = windows(padded, height, breadth, False)
        pre_two = jnp.einsum(
            "km,khw->mhw", w_mid[block_index].reshape(-1, w_mid.shape[3]), stacked,
            preferred_element_type=jnp.float32,
        )
        act_two = smooth_act(
            per_channel(gain_mid[block_index, 1]) * pre_two + per_channel(shift_mid[block_index, 1])
        ).astype(jnp.bfloat16)
        pre_three = pointwise(w_expand[block_index], act_two)
        if block_index == 0:
            shortcut = pointwise(w_short, stem_out)
        else:
            shortcut = feature.astype(jnp.float32)
        summed = (
            per_channel(gain_wide[block_index]) * pre_three
            + per_channel(shift_wide[block_index])
            + shortcut
        )
        stored = stacked
        saved_all.append((feature, pre_one, stored, pre_two, act_two, pre_three, summed))
        feature = (smooth_act(summed) * tissue_keep).astype(jnp.bfloat16)
    gradient = upstream
    pieces = [None] * levels
    g_short = None
    for block_index in range(levels - 1, -1, -1):
        feature, pre_one, stored, pre_two, act_two, pre_three, summed = saved_all[block_index]
        w_in = w_first if block_index == 0 else w_reduce[block_index - 1]
        d_sum = gradient.astype(jnp.float32) * tissue_keep * smooth_slope(summed)
        d_gain3 = jnp.sum(d_sum * pre_three, axis=(1, 2))
        d_shift3 = jnp.sum(d_sum, axis=(1, 2))
        d_pre3 = (per_channel(gain_wide[block_index]) * d_sum).astype(jnp.bfloat16)
        g_expand = jnp.einsum("mhw,ohw->mo", act_two, d_pre3, preferred_element_type=jnp.float32)
        d_act2 = jnp.einsum(
            "mo,ohw->mhw", w_expand[block_index], d_pre3, preferred_element_type=jnp.float32
        )
        d_rel2 = d_act2 * smooth_slope(
            per_channel(gain_mid[block_index, 1]) * pre_two + per_channel(shift_mid[block_index, 1])
        )
        d_gain2 = jnp.sum(d_rel2 * pre_two, axis=(1, 2))
        d_shift2 = jnp.sum(d_rel2, axis=(1, 2))
        d_pre2 = (per_channel(gain_mid[block_index, 1]) * d_rel2).astype(jnp.bfloat16)
        g_mid = jnp.einsum(
            "khw,mhw->km", stored, d_pre2, preferred_element_type=jnp.float32
        ).reshape(w_mid.shape[1:])
        grad_pad = exchange(d_pre2, lax.axis_size("rows"), lax.axis_size("cols"))
        d_act1 = jnp.einsum(
            "km,khw->mhw",
            jnp.swapaxes(w_mid[block_index], 1, 2).reshape(-1, w_mid.shape[2]),
            windows(grad_pad, height, breadth, True),
            preferred_element_type=jnp.float32,
        )
        d_rel1 = d_act1 * smooth_slope(
            per_channel(gain_mid[block_index, 0]) * pre_one + per_channel(shift_mid[block_index, 0])
        )
        d_gain1 = jnp.sum(d_rel1 * pre_one, axis=(1, 2))
        d_shift1 = jnp.sum(d_rel1, axis=(1, 2))
        d_pre1 = (per_channel(gain_mid[block_index, 0]) * d_rel1).astype(jnp.bfloat16)
        g_in = jnp.einsum("chw,mhw->cm", feature, d_pre1, preferred_element_type=jnp.float32)
        d_feature = jnp.einsum("cm,mhw->chw", w_in, d_pre1, preferred_element_type=jnp.float32)
        if block_index == 0:
            d_short = d_sum.astype(jnp.bfloat16)
            g_short = jnp.einsum(
                "chw,ohw->co", feature, d_short, preferred_element_type=jnp.float32
            )
            d_feature = d_feature + jnp.einsum(
                "co,ohw->chw", w_short, d_short, preferred_element_type=jnp.float32
            )
        else:
            d_feature = d_feature + d_sum
        gradient = d_feature.astype(jnp.bfloat16)
        pieces[block_index] = [
            g_in,
            g_mid,
            g_expand,
            d_gain1,
            d_shift1,
            d_gain2,
            d_shift2,
            d_gain3,
            d_shift3,
        ]
    flat = []
    for block_index in range(levels):
        for piece in pieces[block_index]:
            flat.append(piece.reshape(-1))
    flat.append(g_short.reshape(-1))
    partial_vector = jnp.concatenate(flat)
    totals = all_sum(partial_vector, lax.axis_size("rows"), lax.axis_size("cols"))
    pixel_count = height * breadth * lax.axis_size("rows") * lax.axis_size("cols")
    scale = 1.0 / jnp.sqrt(jnp.float32(pixel_count))
    return (gradient, totals * scale)


def solution(mesh):
    in_specs = (
        P(None, "rows", "cols"),
        P(None, "cols"),
        P(),
        P(),
        P(),
        P(),
        P(),
        P(),
        P(),
        P(),
        P(),
        P(None, "rows", "cols"),
    )
    out_specs = (P(None, "rows", "cols"), P())
    return jax.shard_map(
        per_device, mesh=mesh, in_specs=in_specs, out_specs=out_specs, check_vma=False
    )
```

```python
import functools
import jax
import jax.numpy as jnp
from jax import lax
from jax.experimental import pallas as pl
from jax.experimental.pallas import tpu as pltpu
from jax.sharding import PartitionSpec as P

MESH = pl.DeviceIdType.MESH

BLOCK = 64


_TOWARD = ((-1, 0), (1, 0), (0, -1), (0, 1), (-1, -1), (-1, 1), (1, -1), (1, 1))


def _halo_kernel(nr, nc, e_ref, o_ref, send_sem, recv_sem):
    my_r = lax.axis_index("rows")
    my_c = lax.axis_index("cols")

    def present(dr, dc):
        ok = True
        if dr:
            ok = jnp.logical_and(ok, jnp.logical_and(my_r + dr >= 0, my_r + dr < nr))
        if dc:
            ok = jnp.logical_and(ok, jnp.logical_and(my_c + dc >= 0, my_c + dc < nc))
        return ok

    barrier = pltpu.get_barrier_semaphore()
    count = 0
    for dr, dc in _TOWARD:
        there = present(dr, dc)
        count = count + there.astype(jnp.int32)

        @pl.when(there)
        def _():
            pl.semaphore_signal(barrier, inc=1, device_id=(my_r + dr, my_c + dc), device_id_type=MESH)

    pl.semaphore_wait(barrier, count)

    def copy(k, dr, dc):
        return pltpu.make_async_remote_copy(
            src_ref=e_ref.at[k], dst_ref=o_ref.at[k], send_sem=send_sem.at[k],
            recv_sem=recv_sem.at[k], device_id=(my_r + dr, my_c + dc), device_id_type=MESH)

    for k, (dr, dc) in enumerate(_TOWARD):
        @pl.when(present(dr, dc))
        def _():
            copy(k, dr, dc).start()

        @pl.when(jnp.logical_not(present(-dr, -dc)))
        def _():
            o_ref[k] = jnp.zeros(o_ref.shape[1:], o_ref.dtype)

    for k, (dr, dc) in enumerate(_TOWARD):
        @pl.when(present(-dr, -dc))
        def _():
            copy(k, -dr, -dc).wait_recv()

        @pl.when(present(dr, dc))
        def _():
            copy(k, dr, dc).wait_send()


def exchange(cells, nr, nc):
    ch, h, w = cells.shape
    lanes = max(w, -(-h // 128) * 128)

    def wide(v):
        return jnp.pad(v, ((0, 0), (0, lanes - v.shape[1])))

    top, bottom = cells[:, 0, :], cells[:, h - 1, :]
    left, right = cells[:, :, 0], cells[:, :, w - 1]
    pieces = jnp.stack([
        wide(top), wide(bottom), wide(left), wide(right),
        wide(top[:, :1]), wide(top[:, w - 1:]), wide(bottom[:, :1]), wide(bottom[:, w - 1:]),
    ])
    got = pl.pallas_call(
        functools.partial(_halo_kernel, nr, nc),
        out_shape=jax.ShapeDtypeStruct(pieces.shape, pieces.dtype),
        in_specs=[pl.BlockSpec(memory_space=pltpu.VMEM)],
        out_specs=pl.BlockSpec(memory_space=pltpu.VMEM),
        scratch_shapes=[pltpu.SemaphoreType.DMA((8,)), pltpu.SemaphoreType.DMA((8,))],
        compiler_params=pltpu.CompilerParams(collective_id=1, has_side_effects=True),
    )(pieces)
    above = got[1, :, :w]
    below = got[0, :, :w]
    from_left = got[3, :, :h]
    from_right = got[2, :, :h]
    top_row = jnp.concatenate([got[7, :, :1], above, got[6, :, :1]], axis=1)
    bottom_row = jnp.concatenate([got[5, :, :1], below, got[4, :, :1]], axis=1)
    middle = jnp.concatenate([from_left[:, :, None], cells, from_right[:, :, None]], axis=2)
    return jnp.concatenate([top_row[:, None, :], middle, bottom_row[:, None, :]], axis=1)


def _sum_kernel(nr, nc, x_ref, o_ref, cpart, rpart, csum, rsum, gathered_r, sems, cs_send, cs_recv, rs_send, rs_recv, rg_send, rg_recv, cg_send, cg_recv):
    my_r = lax.axis_index("rows")
    my_c = lax.axis_index("cols")

    def col_peer(j):
        return lax.rem(my_c + j, nc)

    def row_peer(j):
        return lax.rem(my_r + j, nr)

    barrier = pltpu.get_barrier_semaphore()

    def greet_c(j, c):
        pl.semaphore_signal(barrier, inc=1, device_id=(my_r, col_peer(j)), device_id_type=MESH)
        return c

    lax.fori_loop(1, nc, greet_c, 0)

    def greet_r(j, c):
        pl.semaphore_signal(barrier, inc=1, device_id=(row_peer(j), my_c), device_id_type=MESH)
        return c

    lax.fori_loop(1, nr, greet_r, 0)
    pl.semaphore_wait(barrier, nc + nr - 2)

    def c_scatter(p, s):
        return pltpu.make_async_remote_copy(
            src_ref=x_ref.at[p], dst_ref=cpart.at[s], send_sem=cs_send.at[p],
            recv_sem=cs_recv.at[s], device_id=(my_r, p), device_id_type=MESH)

    def start_cs(j, c):
        c_scatter(col_peer(j), my_c).start()
        return c

    lax.fori_loop(1, nc, start_cs, 0)
    cpart[my_c] = x_ref[my_c]

    def wait_cs(j, c):
        c_scatter(my_c, col_peer(j)).wait_recv()
        return c

    lax.fori_loop(1, nc, wait_cs, 0)
    csum[0] = lax.fori_loop(0, nc, lambda s, a: a + cpart[s], jnp.zeros(cpart.shape[1:], jnp.float32))
    own = pltpu.make_async_copy(csum.at[0], csum.at[1], sems.at[0])
    own.start()
    own.wait()

    def r_scatter(q, s):
        return pltpu.make_async_remote_copy(
            src_ref=csum.at[1, q], dst_ref=rpart.at[s], send_sem=rs_send.at[q],
            recv_sem=rs_recv.at[s], device_id=(q, my_c), device_id_type=MESH)

    def start_rs(j, c):
        r_scatter(row_peer(j), my_r).start()
        return c

    lax.fori_loop(1, nr, start_rs, 0)
    rpart[my_r] = csum[1, my_r]

    def wait_rs(j, c):
        r_scatter(my_r, row_peer(j)).wait_recv()
        return c

    lax.fori_loop(1, nr, wait_rs, 0)
    rsum[...] = lax.fori_loop(0, nr, lambda s, a: a + rpart[s], jnp.zeros(rpart.shape[1:], jnp.float32))
    own = pltpu.make_async_copy(rsum, gathered_r.at[my_r], sems.at[1])
    own.start()
    own.wait()

    def r_gather(q, s):
        return pltpu.make_async_remote_copy(
            src_ref=gathered_r.at[s], dst_ref=gathered_r.at[s], send_sem=rg_send.at[q],
            recv_sem=rg_recv.at[s], device_id=(q, my_c), device_id_type=MESH)

    def start_rg(j, c):
        r_gather(row_peer(j), my_r).start()
        return c

    lax.fori_loop(1, nr, start_rg, 0)

    def wait_rg(j, c):
        r_gather(my_r, row_peer(j)).wait_recv()
        return c

    lax.fori_loop(1, nr, wait_rg, 0)
    own = pltpu.make_async_copy(gathered_r, o_ref.at[my_c], sems.at[2])
    own.start()
    own.wait()

    def c_gather(p, s):
        return pltpu.make_async_remote_copy(
            src_ref=o_ref.at[s], dst_ref=o_ref.at[s], send_sem=cg_send.at[p],
            recv_sem=cg_recv.at[s], device_id=(my_r, p), device_id_type=MESH)

    def start_cg(j, c):
        c_gather(col_peer(j), my_c).start()
        return c

    lax.fori_loop(1, nc, start_cg, 0)

    def wait_c(j, c):
        c_scatter(col_peer(j), my_c).wait_send()
        c_gather(my_c, col_peer(j)).wait_recv()
        c_gather(col_peer(j), my_c).wait_send()
        return c

    lax.fori_loop(1, nc, wait_c, 0)

    def wait_r(j, c):
        r_scatter(row_peer(j), my_r).wait_send()
        r_gather(row_peer(j), my_r).wait_send()
        return c

    lax.fori_loop(1, nr, wait_r, 0)


def all_sum(vector, nr, nc):
    length = vector.shape[0]
    rows = -(-length // (nr * nc * 128))
    blocks = jnp.pad(vector, (0, nr * nc * rows * 128 - length)).reshape(nc, nr, rows, 128)
    sem = pltpu.SemaphoreType.DMA
    out = pl.pallas_call(
        functools.partial(_sum_kernel, nr, nc),
        out_shape=jax.ShapeDtypeStruct(blocks.shape, jnp.float32),
        in_specs=[pl.BlockSpec(memory_space=pltpu.VMEM)],
        out_specs=pl.BlockSpec(memory_space=pltpu.VMEM),
        scratch_shapes=[
            pltpu.VMEM((nc, nr, rows, 128), jnp.float32),
            pltpu.VMEM((nr, rows, 128), jnp.float32),
            pltpu.VMEM((2, nr, rows, 128), jnp.float32),
            pltpu.VMEM((rows, 128), jnp.float32),
            pltpu.VMEM((nr, rows, 128), jnp.float32),
            sem((3,)),
            sem((nc,)), sem((nc,)), sem((nr,)), sem((nr,)),
            sem((nr,)), sem((nr,)), sem((nc,)), sem((nc,)),
        ],
        compiler_params=pltpu.CompilerParams(collective_id=0, has_side_effects=True),
    )(blocks)
    return out.reshape(-1)[:length]


def padded_2(cells, sides, width):
    for axis, dim in sides:
        count = lax.axis_size(axis)
        ends = count - 1
        head = lax.slice_in_dim(cells, 0, width, axis=dim)
        tail = lax.slice_in_dim(cells, cells.shape[dim] - width, cells.shape[dim], axis=dim)
        cells = jnp.concatenate(
            [
                lax.ppermute(tail, axis, [(i, (i + 1) % count) for i in range(ends)]),
                cells,
                lax.ppermute(head, axis, [((i + 1) % count, i) for i in range(ends)]),
            ],
            axis=dim,
        )
    return cells


def pointwise(weight, field):
    return jnp.einsum("cm,chw->mhw", weight, field, preferred_element_type=jnp.float32)


def per_channel(vector):
    return vector[:, None, None]


def smooth_act(value):
    return value * jax.nn.sigmoid(value)


def smooth_slope(value):
    sigma = jax.nn.sigmoid(value)
    return sigma * (1.0 + value * (1.0 - sigma))


def spatial_conv(kernel, padded, height, breadth):
    result = jnp.zeros((kernel.shape[2], height, breadth), jnp.float32)
    for tap_row in range(3):
        for tap_col in range(3):
            window = padded[:, tap_row : tap_row + height, tap_col : tap_col + breadth]
            result = result + pointwise(kernel[3 * tap_row + tap_col], window)
    return result


def windows(padded, height, breadth, flip):
    taps = []
    for tap_row in range(3):
        for tap_col in range(3):
            i, j = (2 - tap_row, 2 - tap_col) if flip else (tap_row, tap_col)
            taps.append(padded[:, i : i + height, j : j + breadth])
    return jnp.concatenate(taps, axis=0)


def per_device(
    stem_out,
    tissue,
    w_first,
    w_reduce,
    w_mid,
    w_expand,
    w_short,
    gain_mid,
    shift_mid,
    gain_wide,
    shift_wide,
    upstream,
):
    height, breadth = (stem_out.shape[1], stem_out.shape[2])
    bands, tiles = tissue.shape
    values = tissue.astype(jnp.float32)[:, None, :, None]
    band_keep = jnp.broadcast_to(values, (bands, BLOCK, tiles, BLOCK)).reshape(
        bands * BLOCK, tiles * BLOCK
    )
    row_start = lax.axis_index("rows") * height
    tissue_keep = lax.dynamic_slice_in_dim(band_keep, row_start, height, 0)
    levels = w_mid.shape[0]
    saved_all = []
    feature = stem_out
    for block_index in range(levels):
        w_in = w_first if block_index == 0 else w_reduce[block_index - 1]
        pre_one = pointwise(w_in, feature)
        act_one = smooth_act(
            per_channel(gain_mid[block_index, 0]) * pre_one + per_channel(shift_mid[block_index, 0])
        ).astype(jnp.bfloat16)
        padded = exchange(act_one, lax.axis_size("rows"), lax.axis_size("cols"))
        stacked = windows(padded, height, breadth, False)
        pre_two = jnp.einsum(
            "km,khw->mhw", w_mid[block_index].reshape(-1, w_mid.shape[3]), stacked,
            preferred_element_type=jnp.float32,
        )
        act_two = smooth_act(
            per_channel(gain_mid[block_index, 1]) * pre_two + per_channel(shift_mid[block_index, 1])
        ).astype(jnp.bfloat16)
        pre_three = pointwise(w_expand[block_index], act_two)
        if block_index == 0:
            shortcut = pointwise(w_short, stem_out)
        else:
            shortcut = feature.astype(jnp.float32)
        summed = (
            per_channel(gain_wide[block_index]) * pre_three
            + per_channel(shift_wide[block_index])
            + shortcut
        )
        stored = stacked
        saved_all.append((feature, pre_one, stored, pre_two, act_two, pre_three, summed))
        feature = (smooth_act(summed) * tissue_keep).astype(jnp.bfloat16)
    gradient = upstream
    pieces = [None] * levels
    g_short = None
    for block_index in range(levels - 1, -1, -1):
        feature, pre_one, stored, pre_two, act_two, pre_three, summed = saved_all[block_index]
        w_in = w_first if block_index == 0 else w_reduce[block_index - 1]
        d_sum = gradient.astype(jnp.float32) * tissue_keep * smooth_slope(summed)
        d_gain3 = jnp.sum(d_sum * pre_three, axis=(1, 2))
        d_shift3 = jnp.sum(d_sum, axis=(1, 2))
        d_pre3 = (per_channel(gain_wide[block_index]) * d_sum).astype(jnp.bfloat16)
        g_expand = jnp.einsum("mhw,ohw->mo", act_two, d_pre3, preferred_element_type=jnp.float32)
        d_act2 = jnp.einsum(
            "mo,ohw->mhw", w_expand[block_index], d_pre3, preferred_element_type=jnp.float32
        )
        d_rel2 = d_act2 * smooth_slope(
            per_channel(gain_mid[block_index, 1]) * pre_two + per_channel(shift_mid[block_index, 1])
        )
        d_gain2 = jnp.sum(d_rel2 * pre_two, axis=(1, 2))
        d_shift2 = jnp.sum(d_rel2, axis=(1, 2))
        d_pre2 = (per_channel(gain_mid[block_index, 1]) * d_rel2).astype(jnp.bfloat16)
        g_mid = jnp.einsum(
            "khw,mhw->km", stored, d_pre2, preferred_element_type=jnp.float32
        ).reshape(w_mid.shape[1:])
        grad_pad = exchange(d_pre2, lax.axis_size("rows"), lax.axis_size("cols"))
        d_act1 = jnp.einsum(
            "km,khw->mhw",
            jnp.swapaxes(w_mid[block_index], 1, 2).reshape(-1, w_mid.shape[2]),
            windows(grad_pad, height, breadth, True),
            preferred_element_type=jnp.float32,
        )
        d_rel1 = d_act1 * smooth_slope(
            per_channel(gain_mid[block_index, 0]) * pre_one + per_channel(shift_mid[block_index, 0])
        )
        d_gain1 = jnp.sum(d_rel1 * pre_one, axis=(1, 2))
        d_shift1 = jnp.sum(d_rel1, axis=(1, 2))
        d_pre1 = (per_channel(gain_mid[block_index, 0]) * d_rel1).astype(jnp.bfloat16)
        g_in = jnp.einsum("chw,mhw->cm", feature, d_pre1, preferred_element_type=jnp.float32)
        d_feature = jnp.einsum("cm,mhw->chw", w_in, d_pre1, preferred_element_type=jnp.float32)
        if block_index == 0:
            d_short = d_sum.astype(jnp.bfloat16)
            g_short = jnp.einsum(
                "chw,ohw->co", feature, d_short, preferred_element_type=jnp.float32
            )
            d_feature = d_feature + jnp.einsum(
                "co,ohw->chw", w_short, d_short, preferred_element_type=jnp.float32
            )
        else:
            d_feature = d_feature + d_sum
        gradient = d_feature.astype(jnp.bfloat16)
        pieces[block_index] = [
            g_in,
            g_mid,
            g_expand,
            d_gain1,
            d_shift1,
            d_gain2,
            d_shift2,
            d_gain3,
            d_shift3,
        ]
    flat = []
    for block_index in range(levels):
        for piece in pieces[block_index]:
            flat.append(piece.reshape(-1))
    flat.append(g_short.reshape(-1))
    partial_vector = jnp.concatenate(flat)
    totals = all_sum(partial_vector, lax.axis_size("rows"), lax.axis_size("cols"))
    pixel_count = height * breadth * lax.axis_size("rows") * lax.axis_size("cols")
    scale = 1.0 / jnp.sqrt(jnp.float32(pixel_count))
    return (gradient, totals * scale)


def solution(mesh):
    in_specs = (
        P(None, "rows", "cols"),
        P(None, "cols"),
        P(),
        P(),
        P(),
        P(),
        P(),
        P(),
        P(),
        P(),
        P(),
        P(None, "rows", "cols"),
    )
    out_specs = (P(None, "rows", "cols"), P())
    return jax.shard_map(
        per_device, mesh=mesh, in_specs=in_specs, out_specs=out_specs, check_vma=False
    )
```

```python
import functools
import jax
import jax.numpy as jnp
from jax import lax
from jax.experimental import pallas as pl
from jax.experimental.pallas import tpu as pltpu
from jax.sharding import PartitionSpec as P

MESH = pl.DeviceIdType.MESH

BLOCK = 64


_TOWARD = ((-1, 0), (1, 0), (0, -1), (0, 1), (-1, -1), (-1, 1), (1, -1), (1, 1))


def _halo_kernel(nr, nc, e_ref, o_ref, send_sem, recv_sem):
    my_r = lax.axis_index("rows")
    my_c = lax.axis_index("cols")

    def present(dr, dc):
        ok = True
        if dr:
            ok = jnp.logical_and(ok, jnp.logical_and(my_r + dr >= 0, my_r + dr < nr))
        if dc:
            ok = jnp.logical_and(ok, jnp.logical_and(my_c + dc >= 0, my_c + dc < nc))
        return ok

    barrier = pltpu.get_barrier_semaphore()
    count = 0
    for dr, dc in _TOWARD:
        there = present(dr, dc)
        count = count + there.astype(jnp.int32)

        @pl.when(there)
        def _():
            pl.semaphore_signal(barrier, inc=1, device_id=(my_r + dr, my_c + dc), device_id_type=MESH)

    pl.semaphore_wait(barrier, count)

    def copy(k, dr, dc):
        return pltpu.make_async_remote_copy(
            src_ref=e_ref.at[k], dst_ref=o_ref.at[k], send_sem=send_sem.at[k],
            recv_sem=recv_sem.at[k], device_id=(my_r + dr, my_c + dc), device_id_type=MESH)

    for k, (dr, dc) in enumerate(_TOWARD):
        @pl.when(present(dr, dc))
        def _():
            copy(k, dr, dc).start()

        @pl.when(jnp.logical_not(present(-dr, -dc)))
        def _():
            o_ref[k] = jnp.zeros(o_ref.shape[1:], o_ref.dtype)

    for k, (dr, dc) in enumerate(_TOWARD):
        @pl.when(present(-dr, -dc))
        def _():
            copy(k, -dr, -dc).wait_recv()

        @pl.when(present(dr, dc))
        def _():
            copy(k, dr, dc).wait_send()


def exchange(cells, nr, nc):
    ch, h, w = cells.shape
    lanes = max(w, -(-h // 128) * 128)

    def wide(v):
        return jnp.pad(v, ((0, 0), (0, lanes - v.shape[1])))

    top, bottom = cells[:, 0, :], cells[:, h - 1, :]
    left, right = cells[:, :, 0], cells[:, :, w - 1]
    pieces = jnp.stack([
        wide(top), wide(bottom), wide(left), wide(right),
        wide(top[:, :1]), wide(top[:, w - 1:]), wide(bottom[:, :1]), wide(bottom[:, w - 1:]),
    ])
    got = pl.pallas_call(
        functools.partial(_halo_kernel, nr, nc),
        out_shape=jax.ShapeDtypeStruct(pieces.shape, pieces.dtype),
        in_specs=[pl.BlockSpec(memory_space=pltpu.VMEM)],
        out_specs=pl.BlockSpec(memory_space=pltpu.VMEM),
        scratch_shapes=[pltpu.SemaphoreType.DMA((8,)), pltpu.SemaphoreType.DMA((8,))],
        compiler_params=pltpu.CompilerParams(collective_id=1, has_side_effects=True),
    )(pieces)
    above = got[1, :, :w]
    below = got[0, :, :w]
    from_left = got[3, :, :h]
    from_right = got[2, :, :h]
    top_row = jnp.concatenate([got[7, :, :1], above, got[6, :, :1]], axis=1)
    bottom_row = jnp.concatenate([got[5, :, :1], below, got[4, :, :1]], axis=1)
    middle = jnp.concatenate([from_left[:, :, None], cells, from_right[:, :, None]], axis=2)
    return jnp.concatenate([top_row[:, None, :], middle, bottom_row[:, None, :]], axis=1)


def _sum_kernel(nr, nc, x_ref, o_ref, cpart, rpart, mine, sems, cs_send, cs_recv, r_send, r_recv, cg_send, cg_recv):
    my_r = lax.axis_index("rows")
    my_c = lax.axis_index("cols")

    def col_peer(j):
        return lax.rem(my_c + j, nc)

    def row_peer(j):
        return lax.rem(my_r + j, nr)

    barrier = pltpu.get_barrier_semaphore()

    def greet_c(j, c):
        pl.semaphore_signal(barrier, inc=1, device_id=(my_r, col_peer(j)), device_id_type=MESH)
        return c

    lax.fori_loop(1, nc, greet_c, 0)

    def greet_r(j, c):
        pl.semaphore_signal(barrier, inc=1, device_id=(row_peer(j), my_c), device_id_type=MESH)
        return c

    lax.fori_loop(1, nr, greet_r, 0)
    pl.semaphore_wait(barrier, nc + nr - 2)

    def c_scatter(p, s):
        return pltpu.make_async_remote_copy(
            src_ref=x_ref.at[p], dst_ref=cpart.at[s], send_sem=cs_send.at[p],
            recv_sem=cs_recv.at[s], device_id=(my_r, p), device_id_type=MESH)

    def start_cs(j, c):
        c_scatter(col_peer(j), my_c).start()
        return c

    lax.fori_loop(1, nc, start_cs, 0)
    cpart[my_c] = x_ref[my_c]

    def wait_cs(j, c):
        c_scatter(my_c, col_peer(j)).wait_recv()
        return c

    lax.fori_loop(1, nc, wait_cs, 0)
    mine[0] = lax.fori_loop(0, nc, lambda s, a: a + cpart[s], jnp.zeros(cpart.shape[1:], jnp.float32))
    own = pltpu.make_async_copy(mine.at[0], rpart.at[my_r], sems.at[0])
    own.start()
    own.wait()

    def r_share(q, s):
        return pltpu.make_async_remote_copy(
            src_ref=rpart.at[s], dst_ref=rpart.at[s], send_sem=r_send.at[q],
            recv_sem=r_recv.at[s], device_id=(q, my_c), device_id_type=MESH)

    def start_r(j, c):
        r_share(row_peer(j), my_r).start()
        return c

    lax.fori_loop(1, nr, start_r, 0)

    def wait_r(j, c):
        r_share(my_r, row_peer(j)).wait_recv()
        return c

    lax.fori_loop(1, nr, wait_r, 0)
    mine[1] = lax.fori_loop(0, nr, lambda s, a: a + rpart[s], jnp.zeros(rpart.shape[1:], jnp.float32))
    own = pltpu.make_async_copy(mine.at[1], o_ref.at[my_c], sems.at[1])
    own.start()
    own.wait()

    def c_gather(p, s):
        return pltpu.make_async_remote_copy(
            src_ref=o_ref.at[s], dst_ref=o_ref.at[s], send_sem=cg_send.at[p],
            recv_sem=cg_recv.at[s], device_id=(my_r, p), device_id_type=MESH)

    def start_cg(j, c):
        c_gather(col_peer(j), my_c).start()
        return c

    lax.fori_loop(1, nc, start_cg, 0)

    def wait_c(j, c):
        c_scatter(col_peer(j), my_c).wait_send()
        c_gather(my_c, col_peer(j)).wait_recv()
        c_gather(col_peer(j), my_c).wait_send()
        return c

    lax.fori_loop(1, nc, wait_c, 0)

    def wait_rs(j, c):
        r_share(row_peer(j), my_r).wait_send()
        return c

    lax.fori_loop(1, nr, wait_rs, 0)


def all_sum(vector, nr, nc):
    length = vector.shape[0]
    rows = -(-length // (nc * 128 * 8)) * 8
    blocks = jnp.pad(vector, (0, nc * rows * 128 - length)).reshape(nc, rows, 128)
    sem = pltpu.SemaphoreType.DMA
    out = pl.pallas_call(
        functools.partial(_sum_kernel, nr, nc),
        out_shape=jax.ShapeDtypeStruct(blocks.shape, jnp.float32),
        in_specs=[pl.BlockSpec(memory_space=pltpu.VMEM)],
        out_specs=pl.BlockSpec(memory_space=pltpu.VMEM),
        scratch_shapes=[
            pltpu.VMEM((nc, rows, 128), jnp.float32),
            pltpu.VMEM((nr, rows, 128), jnp.float32),
            pltpu.VMEM((2, rows, 128), jnp.float32),
            sem((2,)),
            sem((nc,)), sem((nc,)), sem((nr,)), sem((nr,)), sem((nc,)), sem((nc,)),
        ],
        compiler_params=pltpu.CompilerParams(collective_id=0, has_side_effects=True),
    )(blocks)
    return out.reshape(-1)[:length]


def padded_2(cells, sides, width):
    for axis, dim in sides:
        count = lax.axis_size(axis)
        ends = count - 1
        head = lax.slice_in_dim(cells, 0, width, axis=dim)
        tail = lax.slice_in_dim(cells, cells.shape[dim] - width, cells.shape[dim], axis=dim)
        cells = jnp.concatenate(
            [
                lax.ppermute(tail, axis, [(i, (i + 1) % count) for i in range(ends)]),
                cells,
                lax.ppermute(head, axis, [((i + 1) % count, i) for i in range(ends)]),
            ],
            axis=dim,
        )
    return cells


def pointwise(weight, field):
    return jnp.einsum("cm,chw->mhw", weight, field, preferred_element_type=jnp.float32)


def per_channel(vector):
    return vector[:, None, None]


def smooth_act(value):
    return value * jax.nn.sigmoid(value)


def smooth_slope(value):
    sigma = jax.nn.sigmoid(value)
    return sigma * (1.0 + value * (1.0 - sigma))


def spatial_conv(kernel, padded, height, breadth):
    result = jnp.zeros((kernel.shape[2], height, breadth), jnp.float32)
    for tap_row in range(3):
        for tap_col in range(3):
            window = padded[:, tap_row : tap_row + height, tap_col : tap_col + breadth]
            result = result + pointwise(kernel[3 * tap_row + tap_col], window)
    return result


def windows(padded, height, breadth, flip):
    taps = []
    for tap_row in range(3):
        for tap_col in range(3):
            i, j = (2 - tap_row, 2 - tap_col) if flip else (tap_row, tap_col)
            taps.append(padded[:, i : i + height, j : j + breadth])
    return jnp.concatenate(taps, axis=0)


def per_device(
    stem_out,
    tissue,
    w_first,
    w_reduce,
    w_mid,
    w_expand,
    w_short,
    gain_mid,
    shift_mid,
    gain_wide,
    shift_wide,
    upstream,
):
    height, breadth = (stem_out.shape[1], stem_out.shape[2])
    bands, tiles = tissue.shape
    values = tissue.astype(jnp.float32)[:, None, :, None]
    band_keep = jnp.broadcast_to(values, (bands, BLOCK, tiles, BLOCK)).reshape(
        bands * BLOCK, tiles * BLOCK
    )
    row_start = lax.axis_index("rows") * height
    tissue_keep = lax.dynamic_slice_in_dim(band_keep, row_start, height, 0)
    levels = w_mid.shape[0]
    saved_all = []
    feature = stem_out
    for block_index in range(levels):
        w_in = w_first if block_index == 0 else w_reduce[block_index - 1]
        pre_one = pointwise(w_in, feature)
        act_one = smooth_act(
            per_channel(gain_mid[block_index, 0]) * pre_one + per_channel(shift_mid[block_index, 0])
        ).astype(jnp.bfloat16)
        padded = exchange(act_one, lax.axis_size("rows"), lax.axis_size("cols"))
        stacked = windows(padded, height, breadth, False)
        pre_two = jnp.einsum(
            "km,khw->mhw", w_mid[block_index].reshape(-1, w_mid.shape[3]), stacked,
            preferred_element_type=jnp.float32,
        )
        act_two = smooth_act(
            per_channel(gain_mid[block_index, 1]) * pre_two + per_channel(shift_mid[block_index, 1])
        ).astype(jnp.bfloat16)
        pre_three = pointwise(w_expand[block_index], act_two)
        if block_index == 0:
            shortcut = pointwise(w_short, stem_out)
        else:
            shortcut = feature.astype(jnp.float32)
        summed = (
            per_channel(gain_wide[block_index]) * pre_three
            + per_channel(shift_wide[block_index])
            + shortcut
        )
        stored = stacked
        saved_all.append((feature, pre_one, stored, pre_two, act_two, pre_three, summed))
        feature = (smooth_act(summed) * tissue_keep).astype(jnp.bfloat16)
    gradient = upstream
    pieces = [None] * levels
    g_short = None
    for block_index in range(levels - 1, -1, -1):
        feature, pre_one, stored, pre_two, act_two, pre_three, summed = saved_all[block_index]
        w_in = w_first if block_index == 0 else w_reduce[block_index - 1]
        d_sum = gradient.astype(jnp.float32) * tissue_keep * smooth_slope(summed)
        d_gain3 = jnp.sum(d_sum * pre_three, axis=(1, 2))
        d_shift3 = jnp.sum(d_sum, axis=(1, 2))
        d_pre3 = (per_channel(gain_wide[block_index]) * d_sum).astype(jnp.bfloat16)
        g_expand = jnp.einsum("mhw,ohw->mo", act_two, d_pre3, preferred_element_type=jnp.float32)
        d_act2 = jnp.einsum(
            "mo,ohw->mhw", w_expand[block_index], d_pre3, preferred_element_type=jnp.float32
        )
        d_rel2 = d_act2 * smooth_slope(
            per_channel(gain_mid[block_index, 1]) * pre_two + per_channel(shift_mid[block_index, 1])
        )
        d_gain2 = jnp.sum(d_rel2 * pre_two, axis=(1, 2))
        d_shift2 = jnp.sum(d_rel2, axis=(1, 2))
        d_pre2 = (per_channel(gain_mid[block_index, 1]) * d_rel2).astype(jnp.bfloat16)
        g_mid = jnp.einsum(
            "khw,mhw->km", stored, d_pre2, preferred_element_type=jnp.float32
        ).reshape(w_mid.shape[1:])
        grad_pad = exchange(d_pre2, lax.axis_size("rows"), lax.axis_size("cols"))
        d_act1 = jnp.einsum(
            "km,khw->mhw",
            jnp.swapaxes(w_mid[block_index], 1, 2).reshape(-1, w_mid.shape[2]),
            windows(grad_pad, height, breadth, True),
            preferred_element_type=jnp.float32,
        )
        d_rel1 = d_act1 * smooth_slope(
            per_channel(gain_mid[block_index, 0]) * pre_one + per_channel(shift_mid[block_index, 0])
        )
        d_gain1 = jnp.sum(d_rel1 * pre_one, axis=(1, 2))
        d_shift1 = jnp.sum(d_rel1, axis=(1, 2))
        d_pre1 = (per_channel(gain_mid[block_index, 0]) * d_rel1).astype(jnp.bfloat16)
        g_in = jnp.einsum("chw,mhw->cm", feature, d_pre1, preferred_element_type=jnp.float32)
        d_feature = jnp.einsum("cm,mhw->chw", w_in, d_pre1, preferred_element_type=jnp.float32)
        if block_index == 0:
            d_short = d_sum.astype(jnp.bfloat16)
            g_short = jnp.einsum(
                "chw,ohw->co", feature, d_short, preferred_element_type=jnp.float32
            )
            d_feature = d_feature + jnp.einsum(
                "co,ohw->chw", w_short, d_short, preferred_element_type=jnp.float32
            )
        else:
            d_feature = d_feature + d_sum
        gradient = d_feature.astype(jnp.bfloat16)
        pieces[block_index] = [
            g_in,
            g_mid,
            g_expand,
            d_gain1,
            d_shift1,
            d_gain2,
            d_shift2,
            d_gain3,
            d_shift3,
        ]
    flat = []
    for block_index in range(levels):
        for piece in pieces[block_index]:
            flat.append(piece.reshape(-1))
    flat.append(g_short.reshape(-1))
    partial_vector = jnp.concatenate(flat)
    totals = all_sum(partial_vector, lax.axis_size("rows"), lax.axis_size("cols"))
    pixel_count = height * breadth * lax.axis_size("rows") * lax.axis_size("cols")
    scale = 1.0 / jnp.sqrt(jnp.float32(pixel_count))
    return (gradient, totals * scale)


def solution(mesh):
    in_specs = (
        P(None, "rows", "cols"),
        P(None, "cols"),
        P(),
        P(),
        P(),
        P(),
        P(),
        P(),
        P(),
        P(),
        P(),
        P(None, "rows", "cols"),
    )
    out_specs = (P(None, "rows", "cols"), P())
    return jax.shard_map(
        per_device, mesh=mesh, in_specs=in_specs, out_specs=out_specs, check_vma=False
    )
```

```python
import functools
import jax
import jax.numpy as jnp
from jax import lax
from jax.experimental import pallas as pl
from jax.experimental.pallas import tpu as pltpu
from jax.sharding import PartitionSpec as P

MESH = pl.DeviceIdType.MESH

BLOCK = 64


_TOWARD = ((-1, 0), (1, 0), (0, -1), (0, 1), (-1, -1), (-1, 1), (1, -1), (1, 1))


def _halo_kernel(nr, nc, *refs):
    pieces, got, (send_sem, recv_sem) = refs[:8], refs[8:16], refs[16:]
    my_r = lax.axis_index("rows")
    my_c = lax.axis_index("cols")

    def present(dr, dc):
        ok = True
        if dr:
            ok = jnp.logical_and(ok, jnp.logical_and(my_r + dr >= 0, my_r + dr < nr))
        if dc:
            ok = jnp.logical_and(ok, jnp.logical_and(my_c + dc >= 0, my_c + dc < nc))
        return ok

    barrier = pltpu.get_barrier_semaphore()
    count = 0
    for dr, dc in _TOWARD:
        there = present(dr, dc)
        count = count + there.astype(jnp.int32)

        @pl.when(there)
        def _():
            pl.semaphore_signal(barrier, inc=1, device_id=(my_r + dr, my_c + dc), device_id_type=MESH)

    pl.semaphore_wait(barrier, count)

    def copy(k, dr, dc):
        return pltpu.make_async_remote_copy(
            src_ref=pieces[k], dst_ref=got[k], send_sem=send_sem.at[k],
            recv_sem=recv_sem.at[k], device_id=(my_r + dr, my_c + dc), device_id_type=MESH)

    for k, (dr, dc) in enumerate(_TOWARD):
        @pl.when(present(dr, dc))
        def _():
            copy(k, dr, dc).start()

        @pl.when(jnp.logical_not(present(-dr, -dc)))
        def _():
            got[k][...] = jnp.zeros(got[k].shape, got[k].dtype)

    for k, (dr, dc) in enumerate(_TOWARD):
        @pl.when(present(-dr, -dc))
        def _():
            copy(k, -dr, -dc).wait_recv()

        @pl.when(present(dr, dc))
        def _():
            copy(k, dr, dc).wait_send()


def exchange(cells, nr, nc):
    ch, h, w = cells.shape
    top, bottom = cells[:, 0, :], cells[:, h - 1, :]
    left, right = cells[:, :, 0], cells[:, :, w - 1]
    pieces = [top, bottom, left, right, top[:, :1], top[:, w - 1 :], bottom[:, :1], bottom[:, w - 1 :]]
    vmem = pl.BlockSpec(memory_space=pltpu.VMEM)
    got = pl.pallas_call(
        functools.partial(_halo_kernel, nr, nc),
        out_shape=[jax.ShapeDtypeStruct(p.shape, p.dtype) for p in pieces],
        in_specs=[vmem] * 8,
        out_specs=[vmem] * 8,
        scratch_shapes=[pltpu.SemaphoreType.DMA((8,)), pltpu.SemaphoreType.DMA((8,))],
        compiler_params=pltpu.CompilerParams(collective_id=1, has_side_effects=True),
    )(*pieces)
    top_row = jnp.concatenate([got[7], got[1], got[6]], axis=1)
    bottom_row = jnp.concatenate([got[5], got[0], got[4]], axis=1)
    middle = jnp.concatenate([got[3][:, :, None], cells, got[2][:, :, None]], axis=2)
    return jnp.concatenate([top_row[:, None, :], middle, bottom_row[:, None, :]], axis=1)


def _sum_kernel(nr, nc, x_ref, o_ref, cpart, rpart, mine, sems, cs_send, cs_recv, r_send, r_recv, cg_send, cg_recv):
    my_r = lax.axis_index("rows")
    my_c = lax.axis_index("cols")

    def col_peer(j):
        return lax.rem(my_c + j, nc)

    def row_peer(j):
        return lax.rem(my_r + j, nr)

    barrier = pltpu.get_barrier_semaphore()

    def greet_c(j, c):
        pl.semaphore_signal(barrier, inc=1, device_id=(my_r, col_peer(j)), device_id_type=MESH)
        return c

    lax.fori_loop(1, nc, greet_c, 0)

    def greet_r(j, c):
        pl.semaphore_signal(barrier, inc=1, device_id=(row_peer(j), my_c), device_id_type=MESH)
        return c

    lax.fori_loop(1, nr, greet_r, 0)
    pl.semaphore_wait(barrier, nc + nr - 2)

    def c_scatter(p, s):
        return pltpu.make_async_remote_copy(
            src_ref=x_ref.at[p], dst_ref=cpart.at[s], send_sem=cs_send.at[p],
            recv_sem=cs_recv.at[s], device_id=(my_r, p), device_id_type=MESH)

    def start_cs(j, c):
        c_scatter(col_peer(j), my_c).start()
        return c

    lax.fori_loop(1, nc, start_cs, 0)
    cpart[my_c] = x_ref[my_c]

    def wait_cs(j, c):
        c_scatter(my_c, col_peer(j)).wait_recv()
        return c

    lax.fori_loop(1, nc, wait_cs, 0)
    mine[0] = lax.fori_loop(0, nc, lambda s, a: a + cpart[s], jnp.zeros(cpart.shape[1:], jnp.float32))
    own = pltpu.make_async_copy(mine.at[0], rpart.at[my_r], sems.at[0])
    own.start()
    own.wait()

    def r_share(q, s):
        return pltpu.make_async_remote_copy(
            src_ref=rpart.at[s], dst_ref=rpart.at[s], send_sem=r_send.at[q],
            recv_sem=r_recv.at[s], device_id=(q, my_c), device_id_type=MESH)

    def start_r(j, c):
        r_share(row_peer(j), my_r).start()
        return c

    lax.fori_loop(1, nr, start_r, 0)

    def wait_r(j, c):
        r_share(my_r, row_peer(j)).wait_recv()
        return c

    lax.fori_loop(1, nr, wait_r, 0)
    mine[1] = lax.fori_loop(0, nr, lambda s, a: a + rpart[s], jnp.zeros(rpart.shape[1:], jnp.float32))
    own = pltpu.make_async_copy(mine.at[1], o_ref.at[my_c], sems.at[1])
    own.start()
    own.wait()

    def c_gather(p, s):
        return pltpu.make_async_remote_copy(
            src_ref=o_ref.at[s], dst_ref=o_ref.at[s], send_sem=cg_send.at[p],
            recv_sem=cg_recv.at[s], device_id=(my_r, p), device_id_type=MESH)

    def start_cg(j, c):
        c_gather(col_peer(j), my_c).start()
        return c

    lax.fori_loop(1, nc, start_cg, 0)

    def wait_c(j, c):
        c_scatter(col_peer(j), my_c).wait_send()
        c_gather(my_c, col_peer(j)).wait_recv()
        c_gather(col_peer(j), my_c).wait_send()
        return c

    lax.fori_loop(1, nc, wait_c, 0)

    def wait_rs(j, c):
        r_share(row_peer(j), my_r).wait_send()
        return c

    lax.fori_loop(1, nr, wait_rs, 0)


def all_sum(vector, nr, nc):
    length = vector.shape[0]
    rows = -(-length // (nc * 128 * 8)) * 8
    blocks = jnp.pad(vector, (0, nc * rows * 128 - length)).reshape(nc, rows, 128)
    sem = pltpu.SemaphoreType.DMA
    out = pl.pallas_call(
        functools.partial(_sum_kernel, nr, nc),
        out_shape=jax.ShapeDtypeStruct(blocks.shape, jnp.float32),
        in_specs=[pl.BlockSpec(memory_space=pltpu.VMEM)],
        out_specs=pl.BlockSpec(memory_space=pltpu.VMEM),
        scratch_shapes=[
            pltpu.VMEM((nc, rows, 128), jnp.float32),
            pltpu.VMEM((nr, rows, 128), jnp.float32),
            pltpu.VMEM((2, rows, 128), jnp.float32),
            sem((2,)),
            sem((nc,)), sem((nc,)), sem((nr,)), sem((nr,)), sem((nc,)), sem((nc,)),
        ],
        compiler_params=pltpu.CompilerParams(collective_id=0, has_side_effects=True),
    )(blocks)
    return out.reshape(-1)[:length]


def padded_2(cells, sides, width):
    for axis, dim in sides:
        count = lax.axis_size(axis)
        ends = count - 1
        head = lax.slice_in_dim(cells, 0, width, axis=dim)
        tail = lax.slice_in_dim(cells, cells.shape[dim] - width, cells.shape[dim], axis=dim)
        cells = jnp.concatenate(
            [
                lax.ppermute(tail, axis, [(i, (i + 1) % count) for i in range(ends)]),
                cells,
                lax.ppermute(head, axis, [((i + 1) % count, i) for i in range(ends)]),
            ],
            axis=dim,
        )
    return cells


def pointwise(weight, field):
    return jnp.einsum("cm,chw->mhw", weight, field, preferred_element_type=jnp.float32)


def per_channel(vector):
    return vector[:, None, None]


def smooth_act(value):
    return value * jax.nn.sigmoid(value)


def smooth_slope(value):
    sigma = jax.nn.sigmoid(value)
    return sigma * (1.0 + value * (1.0 - sigma))


def spatial_conv(kernel, padded, height, breadth):
    result = jnp.zeros((kernel.shape[2], height, breadth), jnp.float32)
    for tap_row in range(3):
        for tap_col in range(3):
            window = padded[:, tap_row : tap_row + height, tap_col : tap_col + breadth]
            result = result + pointwise(kernel[3 * tap_row + tap_col], window)
    return result


def windows(padded, height, breadth, flip):
    taps = []
    for tap_row in range(3):
        for tap_col in range(3):
            i, j = (2 - tap_row, 2 - tap_col) if flip else (tap_row, tap_col)
            taps.append(padded[:, i : i + height, j : j + breadth])
    return jnp.concatenate(taps, axis=0)


def per_device(
    stem_out,
    tissue,
    w_first,
    w_reduce,
    w_mid,
    w_expand,
    w_short,
    gain_mid,
    shift_mid,
    gain_wide,
    shift_wide,
    upstream,
):
    height, breadth = (stem_out.shape[1], stem_out.shape[2])
    bands, tiles = tissue.shape
    values = tissue.astype(jnp.float32)[:, None, :, None]
    band_keep = jnp.broadcast_to(values, (bands, BLOCK, tiles, BLOCK)).reshape(
        bands * BLOCK, tiles * BLOCK
    )
    row_start = lax.axis_index("rows") * height
    tissue_keep = lax.dynamic_slice_in_dim(band_keep, row_start, height, 0)
    levels = w_mid.shape[0]
    saved_all = []
    feature = stem_out
    for block_index in range(levels):
        w_in = w_first if block_index == 0 else w_reduce[block_index - 1]
        pre_one = pointwise(w_in, feature)
        act_one = smooth_act(
            per_channel(gain_mid[block_index, 0]) * pre_one + per_channel(shift_mid[block_index, 0])
        ).astype(jnp.bfloat16)
        padded = exchange(act_one, lax.axis_size("rows"), lax.axis_size("cols"))
        stacked = windows(padded, height, breadth, False)
        pre_two = jnp.einsum(
            "km,khw->mhw", w_mid[block_index].reshape(-1, w_mid.shape[3]), stacked,
            preferred_element_type=jnp.float32,
        )
        act_two = smooth_act(
            per_channel(gain_mid[block_index, 1]) * pre_two + per_channel(shift_mid[block_index, 1])
        ).astype(jnp.bfloat16)
        pre_three = pointwise(w_expand[block_index], act_two)
        if block_index == 0:
            shortcut = pointwise(w_short, stem_out)
        else:
            shortcut = feature.astype(jnp.float32)
        summed = (
            per_channel(gain_wide[block_index]) * pre_three
            + per_channel(shift_wide[block_index])
            + shortcut
        )
        stored = stacked
        saved_all.append((feature, pre_one, stored, pre_two, act_two, pre_three, summed))
        feature = (smooth_act(summed) * tissue_keep).astype(jnp.bfloat16)
    gradient = upstream
    pieces = [None] * levels
    g_short = None
    for block_index in range(levels - 1, -1, -1):
        feature, pre_one, stored, pre_two, act_two, pre_three, summed = saved_all[block_index]
        w_in = w_first if block_index == 0 else w_reduce[block_index - 1]
        d_sum = gradient.astype(jnp.float32) * tissue_keep * smooth_slope(summed)
        d_gain3 = jnp.sum(d_sum * pre_three, axis=(1, 2))
        d_shift3 = jnp.sum(d_sum, axis=(1, 2))
        d_pre3 = (per_channel(gain_wide[block_index]) * d_sum).astype(jnp.bfloat16)
        g_expand = jnp.einsum("mhw,ohw->mo", act_two, d_pre3, preferred_element_type=jnp.float32)
        d_act2 = jnp.einsum(
            "mo,ohw->mhw", w_expand[block_index], d_pre3, preferred_element_type=jnp.float32
        )
        d_rel2 = d_act2 * smooth_slope(
            per_channel(gain_mid[block_index, 1]) * pre_two + per_channel(shift_mid[block_index, 1])
        )
        d_gain2 = jnp.sum(d_rel2 * pre_two, axis=(1, 2))
        d_shift2 = jnp.sum(d_rel2, axis=(1, 2))
        d_pre2 = (per_channel(gain_mid[block_index, 1]) * d_rel2).astype(jnp.bfloat16)
        g_mid = jnp.einsum(
            "khw,mhw->km", stored, d_pre2, preferred_element_type=jnp.float32
        ).reshape(w_mid.shape[1:])
        grad_pad = exchange(d_pre2, lax.axis_size("rows"), lax.axis_size("cols"))
        d_act1 = jnp.einsum(
            "km,khw->mhw",
            jnp.swapaxes(w_mid[block_index], 1, 2).reshape(-1, w_mid.shape[2]),
            windows(grad_pad, height, breadth, True),
            preferred_element_type=jnp.float32,
        )
        d_rel1 = d_act1 * smooth_slope(
            per_channel(gain_mid[block_index, 0]) * pre_one + per_channel(shift_mid[block_index, 0])
        )
        d_gain1 = jnp.sum(d_rel1 * pre_one, axis=(1, 2))
        d_shift1 = jnp.sum(d_rel1, axis=(1, 2))
        d_pre1 = (per_channel(gain_mid[block_index, 0]) * d_rel1).astype(jnp.bfloat16)
        g_in = jnp.einsum("chw,mhw->cm", feature, d_pre1, preferred_element_type=jnp.float32)
        d_feature = jnp.einsum("cm,mhw->chw", w_in, d_pre1, preferred_element_type=jnp.float32)
        if block_index == 0:
            d_short = d_sum.astype(jnp.bfloat16)
            g_short = jnp.einsum(
                "chw,ohw->co", feature, d_short, preferred_element_type=jnp.float32
            )
            d_feature = d_feature + jnp.einsum(
                "co,ohw->chw", w_short, d_short, preferred_element_type=jnp.float32
            )
        else:
            d_feature = d_feature + d_sum
        gradient = d_feature.astype(jnp.bfloat16)
        pieces[block_index] = [
            g_in,
            g_mid,
            g_expand,
            d_gain1,
            d_shift1,
            d_gain2,
            d_shift2,
            d_gain3,
            d_shift3,
        ]
    flat = []
    for block_index in range(levels):
        for piece in pieces[block_index]:
            flat.append(piece.reshape(-1))
    flat.append(g_short.reshape(-1))
    partial_vector = jnp.concatenate(flat)
    totals = all_sum(partial_vector, lax.axis_size("rows"), lax.axis_size("cols"))
    pixel_count = height * breadth * lax.axis_size("rows") * lax.axis_size("cols")
    scale = 1.0 / jnp.sqrt(jnp.float32(pixel_count))
    return (gradient, totals * scale)


def solution(mesh):
    in_specs = (
        P(None, "rows", "cols"),
        P(None, "cols"),
        P(),
        P(),
        P(),
        P(),
        P(),
        P(),
        P(),
        P(),
        P(),
        P(None, "rows", "cols"),
    )
    out_specs = (P(None, "rows", "cols"), P())
    return jax.shard_map(
        per_device, mesh=mesh, in_specs=in_specs, out_specs=out_specs, check_vma=False
    )
```

```python
import functools
import jax
import jax.numpy as jnp
from jax import lax
from jax.experimental import pallas as pl
from jax.experimental.pallas import tpu as pltpu
from jax.sharding import PartitionSpec as P

MESH = pl.DeviceIdType.MESH

BLOCK = 64


_TOWARD = ((-1, 0), (1, 0), (0, -1), (0, 1), (-1, -1), (-1, 1), (1, -1), (1, 1))


def _halo_kernel(nr, nc, e_ref, o_ref, send_sem, recv_sem):
    my_r = lax.axis_index("rows")
    my_c = lax.axis_index("cols")

    def present(dr, dc):
        ok = True
        if dr:
            ok = jnp.logical_and(ok, jnp.logical_and(my_r + dr >= 0, my_r + dr < nr))
        if dc:
            ok = jnp.logical_and(ok, jnp.logical_and(my_c + dc >= 0, my_c + dc < nc))
        return ok

    barrier = pltpu.get_barrier_semaphore()
    count = 0
    for dr, dc in _TOWARD:
        there = present(dr, dc)
        count = count + there.astype(jnp.int32)

        @pl.when(there)
        def _():
            pl.semaphore_signal(barrier, inc=1, device_id=(my_r + dr, my_c + dc), device_id_type=MESH)

    pl.semaphore_wait(barrier, count)

    def copy(k, dr, dc):
        return pltpu.make_async_remote_copy(
            src_ref=e_ref.at[k], dst_ref=o_ref.at[k], send_sem=send_sem.at[k],
            recv_sem=recv_sem.at[k], device_id=(my_r + dr, my_c + dc), device_id_type=MESH)

    for k, (dr, dc) in enumerate(_TOWARD):
        @pl.when(present(dr, dc))
        def _():
            copy(k, dr, dc).start()

        @pl.when(jnp.logical_not(present(-dr, -dc)))
        def _():
            o_ref[k] = jnp.zeros(o_ref.shape[1:], o_ref.dtype)

    for k, (dr, dc) in enumerate(_TOWARD):
        @pl.when(present(-dr, -dc))
        def _():
            copy(k, -dr, -dc).wait_recv()

        @pl.when(present(dr, dc))
        def _():
            copy(k, dr, dc).wait_send()


def exchange(cells, nr, nc):
    ch, h, w = cells.shape
    lanes = max(w, -(-h // 128) * 128)

    def wide(v):
        return jnp.pad(v, ((0, 0), (0, lanes - v.shape[1])))

    top, bottom = cells[:, 0, :], cells[:, h - 1, :]
    left, right = cells[:, :, 0], cells[:, :, w - 1]
    pieces = jnp.stack([
        wide(top), wide(bottom), wide(left), wide(right),
        wide(top[:, :1]), wide(top[:, w - 1:]), wide(bottom[:, :1]), wide(bottom[:, w - 1:]),
    ])
    got = pl.pallas_call(
        functools.partial(_halo_kernel, nr, nc),
        out_shape=jax.ShapeDtypeStruct(pieces.shape, pieces.dtype),
        in_specs=[pl.BlockSpec(memory_space=pltpu.VMEM)],
        out_specs=pl.BlockSpec(memory_space=pltpu.VMEM),
        scratch_shapes=[pltpu.SemaphoreType.DMA((8,)), pltpu.SemaphoreType.DMA((8,))],
        compiler_params=pltpu.CompilerParams(collective_id=1, has_side_effects=True),
    )(pieces)
    above = got[1, :, :w]
    below = got[0, :, :w]
    from_left = got[3, :, :h]
    from_right = got[2, :, :h]
    top_row = jnp.concatenate([got[7, :, :1], above, got[6, :, :1]], axis=1)
    bottom_row = jnp.concatenate([got[5, :, :1], below, got[4, :, :1]], axis=1)
    middle = jnp.concatenate([from_left[:, :, None], cells, from_right[:, :, None]], axis=2)
    return jnp.concatenate([top_row[:, None, :], middle, bottom_row[:, None, :]], axis=1)


def _sum_kernel(nr, nc, x_ref, o_ref, cpart, rpart, mine, sems, cs_send, cs_recv, r_send, r_recv, cg_send, cg_recv):
    my_r = lax.axis_index("rows")
    my_c = lax.axis_index("cols")

    def col_peer(j):
        return lax.rem(my_c + j, nc)

    def row_peer(j):
        return lax.rem(my_r + j, nr)

    barrier = pltpu.get_barrier_semaphore()

    def greet_c(j, c):
        pl.semaphore_signal(barrier, inc=1, device_id=(my_r, col_peer(j)), device_id_type=MESH)
        return c

    lax.fori_loop(1, nc, greet_c, 0)

    def greet_r(j, c):
        pl.semaphore_signal(barrier, inc=1, device_id=(row_peer(j), my_c), device_id_type=MESH)
        return c

    lax.fori_loop(1, nr, greet_r, 0)
    pl.semaphore_wait(barrier, nc + nr - 2)

    def c_scatter(p, s):
        return pltpu.make_async_remote_copy(
            src_ref=x_ref.at[p], dst_ref=cpart.at[s], send_sem=cs_send.at[p],
            recv_sem=cs_recv.at[s], device_id=(my_r, p), device_id_type=MESH)

    def start_cs(j, c):
        c_scatter(col_peer(j), my_c).start()
        return c

    lax.fori_loop(1, nc, start_cs, 0)
    cpart[my_c] = x_ref[my_c]

    def wait_cs(j, c):
        c_scatter(my_c, col_peer(j)).wait_recv()
        return c

    lax.fori_loop(1, nc, wait_cs, 0)
    mine[0] = lax.fori_loop(0, nc, lambda s, a: a + cpart[s], jnp.zeros(cpart.shape[1:], jnp.float32))
    own = pltpu.make_async_copy(mine.at[0], rpart.at[my_r], sems.at[0])
    own.start()
    own.wait()

    def r_share(q, s):
        return pltpu.make_async_remote_copy(
            src_ref=rpart.at[s], dst_ref=rpart.at[s], send_sem=r_send.at[q],
            recv_sem=r_recv.at[s], device_id=(q, my_c), device_id_type=MESH)

    def start_r(j, c):
        r_share(row_peer(j), my_r).start()
        return c

    lax.fori_loop(1, nr, start_r, 0)

    def wait_r(j, c):
        r_share(my_r, row_peer(j)).wait_recv()
        return c

    lax.fori_loop(1, nr, wait_r, 0)
    mine[1] = lax.fori_loop(0, nr, lambda s, a: a + rpart[s], jnp.zeros(rpart.shape[1:], jnp.float32))
    own = pltpu.make_async_copy(mine.at[1], o_ref.at[my_c], sems.at[1])
    own.start()
    own.wait()

    def c_gather(p, s):
        return pltpu.make_async_remote_copy(
            src_ref=o_ref.at[s], dst_ref=o_ref.at[s], send_sem=cg_send.at[p],
            recv_sem=cg_recv.at[s], device_id=(my_r, p), device_id_type=MESH)

    def start_cg(j, c):
        c_gather(col_peer(j), my_c).start()
        return c

    lax.fori_loop(1, nc, start_cg, 0)

    def wait_c(j, c):
        c_scatter(col_peer(j), my_c).wait_send()
        c_gather(my_c, col_peer(j)).wait_recv()
        c_gather(col_peer(j), my_c).wait_send()
        return c

    lax.fori_loop(1, nc, wait_c, 0)

    def wait_rs(j, c):
        r_share(row_peer(j), my_r).wait_send()
        return c

    lax.fori_loop(1, nr, wait_rs, 0)


def all_sum(vector, nr, nc):
    length = vector.shape[0]
    rows = -(-length // (nc * 128 * 8)) * 8
    blocks = jnp.pad(vector, (0, nc * rows * 128 - length)).reshape(nc, rows, 128)
    sem = pltpu.SemaphoreType.DMA
    out = pl.pallas_call(
        functools.partial(_sum_kernel, nr, nc),
        out_shape=jax.ShapeDtypeStruct(blocks.shape, jnp.float32),
        in_specs=[pl.BlockSpec(memory_space=pltpu.VMEM)],
        out_specs=pl.BlockSpec(memory_space=pltpu.VMEM),
        scratch_shapes=[
            pltpu.VMEM((nc, rows, 128), jnp.float32),
            pltpu.VMEM((nr, rows, 128), jnp.float32),
            pltpu.VMEM((2, rows, 128), jnp.float32),
            sem((2,)),
            sem((nc,)), sem((nc,)), sem((nr,)), sem((nr,)), sem((nc,)), sem((nc,)),
        ],
        compiler_params=pltpu.CompilerParams(collective_id=0, has_side_effects=True),
    )(blocks)
    return out.reshape(-1)[:length]


def padded_2(cells, sides, width):
    for axis, dim in sides:
        count = lax.axis_size(axis)
        ends = count - 1
        head = lax.slice_in_dim(cells, 0, width, axis=dim)
        tail = lax.slice_in_dim(cells, cells.shape[dim] - width, cells.shape[dim], axis=dim)
        cells = jnp.concatenate(
            [
                lax.ppermute(tail, axis, [(i, (i + 1) % count) for i in range(ends)]),
                cells,
                lax.ppermute(head, axis, [((i + 1) % count, i) for i in range(ends)]),
            ],
            axis=dim,
        )
    return cells


def pointwise(weight, field):
    return jnp.einsum("cm,chw->mhw", weight, field, preferred_element_type=jnp.float32)


def per_channel(vector):
    return vector[:, None, None]


def smooth_act(value):
    return value * jax.nn.sigmoid(value)


def smooth_slope(value):
    sigma = jax.nn.sigmoid(value)
    return sigma * (1.0 + value * (1.0 - sigma))


def spatial_conv(kernel, padded, height, breadth):
    result = jnp.zeros((kernel.shape[2], height, breadth), jnp.float32)
    for tap_row in range(3):
        for tap_col in range(3):
            window = padded[:, tap_row : tap_row + height, tap_col : tap_col + breadth]
            result = result + pointwise(kernel[3 * tap_row + tap_col], window)
    return result


def windows(padded, height, breadth, flip):
    taps = []
    for tap_row in range(3):
        for tap_col in range(3):
            i, j = (2 - tap_row, 2 - tap_col) if flip else (tap_row, tap_col)
            taps.append(padded[:, i : i + height, j : j + breadth])
    return jnp.concatenate(taps, axis=0)


def per_device(
    stem_out,
    tissue,
    w_first,
    w_reduce,
    w_mid,
    w_expand,
    w_short,
    gain_mid,
    shift_mid,
    gain_wide,
    shift_wide,
    upstream,
):
    height, breadth = (stem_out.shape[1], stem_out.shape[2])
    bands, tiles = tissue.shape
    values = tissue.astype(jnp.float32)[:, None, :, None]
    band_keep = jnp.broadcast_to(values, (bands, BLOCK, tiles, BLOCK)).reshape(
        bands * BLOCK, tiles * BLOCK
    )
    row_start = lax.axis_index("rows") * height
    tissue_keep = lax.dynamic_slice_in_dim(band_keep, row_start, height, 0)
    levels = w_mid.shape[0]
    saved_all = []
    feature = stem_out
    for block_index in range(levels):
        w_in = w_first if block_index == 0 else w_reduce[block_index - 1]
        pre_one = pointwise(w_in, feature)
        act_one = smooth_act(
            per_channel(gain_mid[block_index, 0]) * pre_one + per_channel(shift_mid[block_index, 0])
        ).astype(jnp.bfloat16)
        padded = exchange(act_one, lax.axis_size("rows"), lax.axis_size("cols"))
        stacked = windows(padded, height, breadth, False)
        pre_two = jnp.einsum(
            "km,khw->mhw", w_mid[block_index].reshape(-1, w_mid.shape[3]), stacked,
            preferred_element_type=jnp.float32,
        )
        act_two = smooth_act(
            per_channel(gain_mid[block_index, 1]) * pre_two + per_channel(shift_mid[block_index, 1])
        ).astype(jnp.bfloat16)
        pre_three = pointwise(w_expand[block_index], act_two)
        if block_index == 0:
            shortcut = pointwise(w_short, stem_out)
        else:
            shortcut = feature.astype(jnp.float32)
        summed = (
            per_channel(gain_wide[block_index]) * pre_three
            + per_channel(shift_wide[block_index])
            + shortcut
        )
        stored = stacked
        saved_all.append((feature, pre_one, stored, pre_two, act_two))
        feature = (smooth_act(summed) * tissue_keep).astype(jnp.bfloat16)
    gradient = upstream
    pieces = [None] * levels
    g_short = None
    for block_index in range(levels - 1, -1, -1):
        feature, pre_one, stored, pre_two, act_two = saved_all[block_index]
        again_two, again_feature = lax.optimization_barrier((act_two, feature))
        pre_three = pointwise(w_expand[block_index], again_two)
        if block_index == 0:
            shortcut = pointwise(w_short, again_feature)
        else:
            shortcut = again_feature.astype(jnp.float32)
        summed = (
            per_channel(gain_wide[block_index]) * pre_three
            + per_channel(shift_wide[block_index])
            + shortcut
        )
        w_in = w_first if block_index == 0 else w_reduce[block_index - 1]
        d_sum = gradient.astype(jnp.float32) * tissue_keep * smooth_slope(summed)
        d_gain3 = jnp.sum(d_sum * pre_three, axis=(1, 2))
        d_shift3 = jnp.sum(d_sum, axis=(1, 2))
        d_pre3 = (per_channel(gain_wide[block_index]) * d_sum).astype(jnp.bfloat16)
        g_expand = jnp.einsum("mhw,ohw->mo", act_two, d_pre3, preferred_element_type=jnp.float32)
        d_act2 = jnp.einsum(
            "mo,ohw->mhw", w_expand[block_index], d_pre3, preferred_element_type=jnp.float32
        )
        d_rel2 = d_act2 * smooth_slope(
            per_channel(gain_mid[block_index, 1]) * pre_two + per_channel(shift_mid[block_index, 1])
        )
        d_gain2 = jnp.sum(d_rel2 * pre_two, axis=(1, 2))
        d_shift2 = jnp.sum(d_rel2, axis=(1, 2))
        d_pre2 = (per_channel(gain_mid[block_index, 1]) * d_rel2).astype(jnp.bfloat16)
        g_mid = jnp.einsum(
            "khw,mhw->km", stored, d_pre2, preferred_element_type=jnp.float32
        ).reshape(w_mid.shape[1:])
        grad_pad = exchange(d_pre2, lax.axis_size("rows"), lax.axis_size("cols"))
        d_act1 = jnp.einsum(
            "km,khw->mhw",
            jnp.swapaxes(w_mid[block_index], 1, 2).reshape(-1, w_mid.shape[2]),
            windows(grad_pad, height, breadth, True),
            preferred_element_type=jnp.float32,
        )
        d_rel1 = d_act1 * smooth_slope(
            per_channel(gain_mid[block_index, 0]) * pre_one + per_channel(shift_mid[block_index, 0])
        )
        d_gain1 = jnp.sum(d_rel1 * pre_one, axis=(1, 2))
        d_shift1 = jnp.sum(d_rel1, axis=(1, 2))
        d_pre1 = (per_channel(gain_mid[block_index, 0]) * d_rel1).astype(jnp.bfloat16)
        g_in = jnp.einsum("chw,mhw->cm", feature, d_pre1, preferred_element_type=jnp.float32)
        d_feature = jnp.einsum("cm,mhw->chw", w_in, d_pre1, preferred_element_type=jnp.float32)
        if block_index == 0:
            d_short = d_sum.astype(jnp.bfloat16)
            g_short = jnp.einsum(
                "chw,ohw->co", feature, d_short, preferred_element_type=jnp.float32
            )
            d_feature = d_feature + jnp.einsum(
                "co,ohw->chw", w_short, d_short, preferred_element_type=jnp.float32
            )
        else:
            d_feature = d_feature + d_sum
        gradient = d_feature.astype(jnp.bfloat16)
        pieces[block_index] = [
            g_in,
            g_mid,
            g_expand,
            d_gain1,
            d_shift1,
            d_gain2,
            d_shift2,
            d_gain3,
            d_shift3,
        ]
    flat = []
    for block_index in range(levels):
        for piece in pieces[block_index]:
            flat.append(piece.reshape(-1))
    flat.append(g_short.reshape(-1))
    partial_vector = jnp.concatenate(flat)
    totals = all_sum(partial_vector, lax.axis_size("rows"), lax.axis_size("cols"))
    pixel_count = height * breadth * lax.axis_size("rows") * lax.axis_size("cols")
    scale = 1.0 / jnp.sqrt(jnp.float32(pixel_count))
    return (gradient, totals * scale)


def solution(mesh):
    in_specs = (
        P(None, "rows", "cols"),
        P(None, "cols"),
        P(),
        P(),
        P(),
        P(),
        P(),
        P(),
        P(),
        P(),
        P(),
        P(None, "rows", "cols"),
    )
    out_specs = (P(None, "rows", "cols"), P())
    return jax.shard_map(
        per_device, mesh=mesh, in_specs=in_specs, out_specs=out_specs, check_vma=False
    )
```

```python
import functools
import jax
import jax.numpy as jnp
from jax import lax
from jax.experimental import pallas as pl
from jax.experimental.pallas import tpu as pltpu
from jax.sharding import PartitionSpec as P

MESH = pl.DeviceIdType.MESH

BLOCK = 64


_TOWARD = ((-1, 0), (1, 0), (0, -1), (0, 1), (-1, -1), (-1, 1), (1, -1), (1, 1))


def _halo_kernel(nr, nc, e_ref, o_ref, send_sem, recv_sem):
    my_r = lax.axis_index("rows")
    my_c = lax.axis_index("cols")

    def present(dr, dc):
        ok = True
        if dr:
            ok = jnp.logical_and(ok, jnp.logical_and(my_r + dr >= 0, my_r + dr < nr))
        if dc:
            ok = jnp.logical_and(ok, jnp.logical_and(my_c + dc >= 0, my_c + dc < nc))
        return ok

    barrier = pltpu.get_barrier_semaphore()
    count = 0
    for dr, dc in _TOWARD:
        there = present(dr, dc)
        count = count + there.astype(jnp.int32)

        @pl.when(there)
        def _():
            pl.semaphore_signal(barrier, inc=1, device_id=(my_r + dr, my_c + dc), device_id_type=MESH)

    pl.semaphore_wait(barrier, count)

    def copy(k, dr, dc):
        return pltpu.make_async_remote_copy(
            src_ref=e_ref.at[k], dst_ref=o_ref.at[k], send_sem=send_sem.at[k],
            recv_sem=recv_sem.at[k], device_id=(my_r + dr, my_c + dc), device_id_type=MESH)

    for k, (dr, dc) in enumerate(_TOWARD):
        @pl.when(present(dr, dc))
        def _():
            copy(k, dr, dc).start()

        @pl.when(jnp.logical_not(present(-dr, -dc)))
        def _():
            o_ref[k] = jnp.zeros(o_ref.shape[1:], o_ref.dtype)

    for k, (dr, dc) in enumerate(_TOWARD):
        @pl.when(present(-dr, -dc))
        def _():
            copy(k, -dr, -dc).wait_recv()

        @pl.when(present(dr, dc))
        def _():
            copy(k, dr, dc).wait_send()


def exchange(cells, nr, nc):
    ch, h, w = cells.shape
    lanes = max(w, -(-h // 128) * 128)

    def wide(v):
        return jnp.pad(v, ((0, 0), (0, lanes - v.shape[1])))

    top, bottom = cells[:, 0, :], cells[:, h - 1, :]
    left, right = cells[:, :, 0], cells[:, :, w - 1]
    pieces = jnp.stack([
        wide(top), wide(bottom), wide(left), wide(right),
        wide(top[:, :1]), wide(top[:, w - 1:]), wide(bottom[:, :1]), wide(bottom[:, w - 1:]),
    ])
    got = pl.pallas_call(
        functools.partial(_halo_kernel, nr, nc),
        out_shape=jax.ShapeDtypeStruct(pieces.shape, pieces.dtype),
        in_specs=[pl.BlockSpec(memory_space=pltpu.VMEM)],
        out_specs=pl.BlockSpec(memory_space=pltpu.VMEM),
        scratch_shapes=[pltpu.SemaphoreType.DMA((8,)), pltpu.SemaphoreType.DMA((8,))],
        compiler_params=pltpu.CompilerParams(collective_id=1, has_side_effects=True),
    )(pieces)
    above = got[1, :, :w]
    below = got[0, :, :w]
    from_left = got[3, :, :h]
    from_right = got[2, :, :h]
    top_row = jnp.concatenate([got[7, :, :1], above, got[6, :, :1]], axis=1)
    bottom_row = jnp.concatenate([got[5, :, :1], below, got[4, :, :1]], axis=1)
    middle = jnp.concatenate([from_left[:, :, None], cells, from_right[:, :, None]], axis=2)
    return jnp.concatenate([top_row[:, None, :], middle, bottom_row[:, None, :]], axis=1)


def _sum_kernel(nr, nc, x_ref, o_ref, cpart, rpart, mine, sems, cs_send, cs_recv, r_send, r_recv, cg_send, cg_recv):
    my_r = lax.axis_index("rows")
    my_c = lax.axis_index("cols")

    def col_peer(j):
        return lax.rem(my_c + j, nc)

    def row_peer(j):
        return lax.rem(my_r + j, nr)

    barrier = pltpu.get_barrier_semaphore()

    def greet_c(j, c):
        pl.semaphore_signal(barrier, inc=1, device_id=(my_r, col_peer(j)), device_id_type=MESH)
        return c

    lax.fori_loop(1, nc, greet_c, 0)

    def greet_r(j, c):
        pl.semaphore_signal(barrier, inc=1, device_id=(row_peer(j), my_c), device_id_type=MESH)
        return c

    lax.fori_loop(1, nr, greet_r, 0)
    pl.semaphore_wait(barrier, nc + nr - 2)

    def c_scatter(p, s):
        return pltpu.make_async_remote_copy(
            src_ref=x_ref.at[p], dst_ref=cpart.at[s], send_sem=cs_send.at[p],
            recv_sem=cs_recv.at[s], device_id=(my_r, p), device_id_type=MESH)

    def start_cs(j, c):
        c_scatter(col_peer(j), my_c).start()
        return c

    lax.fori_loop(1, nc, start_cs, 0)
    cpart[my_c] = x_ref[my_c]

    def wait_cs(j, c):
        c_scatter(my_c, col_peer(j)).wait_recv()
        return c

    lax.fori_loop(1, nc, wait_cs, 0)
    mine[0] = lax.fori_loop(0, nc, lambda s, a: a + cpart[s], jnp.zeros(cpart.shape[1:], jnp.float32))
    own = pltpu.make_async_copy(mine.at[0], rpart.at[my_r], sems.at[0])
    own.start()
    own.wait()

    def r_share(q, s):
        return pltpu.make_async_remote_copy(
            src_ref=rpart.at[s], dst_ref=rpart.at[s], send_sem=r_send.at[q],
            recv_sem=r_recv.at[s], device_id=(q, my_c), device_id_type=MESH)

    def start_r(j, c):
        r_share(row_peer(j), my_r).start()
        return c

    lax.fori_loop(1, nr, start_r, 0)

    def wait_r(j, c):
        r_share(my_r, row_peer(j)).wait_recv()
        return c

    lax.fori_loop(1, nr, wait_r, 0)
    mine[1] = lax.fori_loop(0, nr, lambda s, a: a + rpart[s], jnp.zeros(rpart.shape[1:], jnp.float32))
    own = pltpu.make_async_copy(mine.at[1], o_ref.at[my_c], sems.at[1])
    own.start()
    own.wait()

    def c_gather(p, s):
        return pltpu.make_async_remote_copy(
            src_ref=o_ref.at[s], dst_ref=o_ref.at[s], send_sem=cg_send.at[p],
            recv_sem=cg_recv.at[s], device_id=(my_r, p), device_id_type=MESH)

    def start_cg(j, c):
        c_gather(col_peer(j), my_c).start()
        return c

    lax.fori_loop(1, nc, start_cg, 0)

    def wait_c(j, c):
        c_scatter(col_peer(j), my_c).wait_send()
        c_gather(my_c, col_peer(j)).wait_recv()
        c_gather(col_peer(j), my_c).wait_send()
        return c

    lax.fori_loop(1, nc, wait_c, 0)

    def wait_rs(j, c):
        r_share(row_peer(j), my_r).wait_send()
        return c

    lax.fori_loop(1, nr, wait_rs, 0)


def all_sum(vector, nr, nc):
    length = vector.shape[0]
    rows = -(-length // (nc * 128 * 8)) * 8
    blocks = jnp.pad(vector, (0, nc * rows * 128 - length)).reshape(nc, rows, 128)
    sem = pltpu.SemaphoreType.DMA
    out = pl.pallas_call(
        functools.partial(_sum_kernel, nr, nc),
        out_shape=jax.ShapeDtypeStruct(blocks.shape, jnp.float32),
        in_specs=[pl.BlockSpec(memory_space=pltpu.VMEM)],
        out_specs=pl.BlockSpec(memory_space=pltpu.VMEM),
        scratch_shapes=[
            pltpu.VMEM((nc, rows, 128), jnp.float32),
            pltpu.VMEM((nr, rows, 128), jnp.float32),
            pltpu.VMEM((2, rows, 128), jnp.float32),
            sem((2,)),
            sem((nc,)), sem((nc,)), sem((nr,)), sem((nr,)), sem((nc,)), sem((nc,)),
        ],
        compiler_params=pltpu.CompilerParams(collective_id=0, has_side_effects=True),
    )(blocks)
    return out.reshape(-1)[:length]


def padded_2(cells, sides, width):
    for axis, dim in sides:
        count = lax.axis_size(axis)
        ends = count - 1
        head = lax.slice_in_dim(cells, 0, width, axis=dim)
        tail = lax.slice_in_dim(cells, cells.shape[dim] - width, cells.shape[dim], axis=dim)
        cells = jnp.concatenate(
            [
                lax.ppermute(tail, axis, [(i, (i + 1) % count) for i in range(ends)]),
                cells,
                lax.ppermute(head, axis, [((i + 1) % count, i) for i in range(ends)]),
            ],
            axis=dim,
        )
    return cells


def pointwise(weight, field):
    return jnp.einsum("cm,chw->mhw", weight, field, preferred_element_type=jnp.float32)


def per_channel(vector):
    return vector[:, None, None]


def smooth_act(value):
    return value * jax.nn.sigmoid(value)


def smooth_slope(value):
    sigma = jax.nn.sigmoid(value)
    return sigma * (1.0 + value * (1.0 - sigma))


def spatial_conv(kernel, padded, height, breadth):
    result = jnp.zeros((kernel.shape[2], height, breadth), jnp.float32)
    for tap_row in range(3):
        for tap_col in range(3):
            window = padded[:, tap_row : tap_row + height, tap_col : tap_col + breadth]
            result = result + pointwise(kernel[3 * tap_row + tap_col], window)
    return result


def windows(padded, height, breadth, flip):
    taps = []
    for tap_row in range(3):
        for tap_col in range(3):
            i, j = (2 - tap_row, 2 - tap_col) if flip else (tap_row, tap_col)
            taps.append(padded[:, i : i + height, j : j + breadth])
    return jnp.concatenate(taps, axis=0)


def per_device(
    stem_out,
    tissue,
    w_first,
    w_reduce,
    w_mid,
    w_expand,
    w_short,
    gain_mid,
    shift_mid,
    gain_wide,
    shift_wide,
    upstream,
):
    height, breadth = (stem_out.shape[1], stem_out.shape[2])
    bands, tiles = tissue.shape
    values = tissue.astype(jnp.float32)[:, None, :, None]
    band_keep = jnp.broadcast_to(values, (bands, BLOCK, tiles, BLOCK)).reshape(
        bands * BLOCK, tiles * BLOCK
    )
    row_start = lax.axis_index("rows") * height
    tissue_keep = lax.dynamic_slice_in_dim(band_keep, row_start, height, 0)
    levels = w_mid.shape[0]
    saved_all = []
    feature = stem_out
    for block_index in range(levels):
        w_in = w_first if block_index == 0 else w_reduce[block_index - 1]
        pre_one = pointwise(w_in, feature)
        act_one = smooth_act(
            per_channel(gain_mid[block_index, 0]) * pre_one + per_channel(shift_mid[block_index, 0])
        ).astype(jnp.bfloat16)
        padded = exchange(act_one, lax.axis_size("rows"), lax.axis_size("cols"))
        stacked = windows(padded, height, breadth, False)
        pre_two = jnp.einsum(
            "km,khw->mhw", w_mid[block_index].reshape(-1, w_mid.shape[3]), stacked,
            preferred_element_type=jnp.float32,
        )
        act_two = smooth_act(
            per_channel(gain_mid[block_index, 1]) * pre_two + per_channel(shift_mid[block_index, 1])
        ).astype(jnp.bfloat16)
        pre_three = pointwise(w_expand[block_index], act_two)
        if block_index == 0:
            shortcut = pointwise(w_short, stem_out)
        else:
            shortcut = feature.astype(jnp.float32)
        summed = (
            per_channel(gain_wide[block_index]) * pre_three
            + per_channel(shift_wide[block_index])
            + shortcut
        )
        stored = stacked
        saved_all.append(
            (feature, pre_one, stored, pre_two, act_two, pre_three.astype(jnp.bfloat16), summed.astype(jnp.bfloat16))
        )
        feature = (smooth_act(summed) * tissue_keep).astype(jnp.bfloat16)
    gradient = upstream
    pieces = [None] * levels
    g_short = None
    for block_index in range(levels - 1, -1, -1):
        feature, pre_one, stored, pre_two, act_two, pre_three, summed = saved_all[block_index]
        pre_three, summed = pre_three.astype(jnp.float32), summed.astype(jnp.float32)
        w_in = w_first if block_index == 0 else w_reduce[block_index - 1]
        d_sum = gradient.astype(jnp.float32) * tissue_keep * smooth_slope(summed)
        d_gain3 = jnp.sum(d_sum * pre_three, axis=(1, 2))
        d_shift3 = jnp.sum(d_sum, axis=(1, 2))
        d_pre3 = (per_channel(gain_wide[block_index]) * d_sum).astype(jnp.bfloat16)
        g_expand = jnp.einsum("mhw,ohw->mo", act_two, d_pre3, preferred_element_type=jnp.float32)
        d_act2 = jnp.einsum(
            "mo,ohw->mhw", w_expand[block_index], d_pre3, preferred_element_type=jnp.float32
        )
        d_rel2 = d_act2 * smooth_slope(
            per_channel(gain_mid[block_index, 1]) * pre_two + per_channel(shift_mid[block_index, 1])
        )
        d_gain2 = jnp.sum(d_rel2 * pre_two, axis=(1, 2))
        d_shift2 = jnp.sum(d_rel2, axis=(1, 2))
        d_pre2 = (per_channel(gain_mid[block_index, 1]) * d_rel2).astype(jnp.bfloat16)
        g_mid = jnp.einsum(
            "khw,mhw->km", stored, d_pre2, preferred_element_type=jnp.float32
        ).reshape(w_mid.shape[1:])
        grad_pad = exchange(d_pre2, lax.axis_size("rows"), lax.axis_size("cols"))
        d_act1 = jnp.einsum(
            "km,khw->mhw",
            jnp.swapaxes(w_mid[block_index], 1, 2).reshape(-1, w_mid.shape[2]),
            windows(grad_pad, height, breadth, True),
            preferred_element_type=jnp.float32,
        )
        d_rel1 = d_act1 * smooth_slope(
            per_channel(gain_mid[block_index, 0]) * pre_one + per_channel(shift_mid[block_index, 0])
        )
        d_gain1 = jnp.sum(d_rel1 * pre_one, axis=(1, 2))
        d_shift1 = jnp.sum(d_rel1, axis=(1, 2))
        d_pre1 = (per_channel(gain_mid[block_index, 0]) * d_rel1).astype(jnp.bfloat16)
        g_in = jnp.einsum("chw,mhw->cm", feature, d_pre1, preferred_element_type=jnp.float32)
        d_feature = jnp.einsum("cm,mhw->chw", w_in, d_pre1, preferred_element_type=jnp.float32)
        if block_index == 0:
            d_short = d_sum.astype(jnp.bfloat16)
            g_short = jnp.einsum(
                "chw,ohw->co", feature, d_short, preferred_element_type=jnp.float32
            )
            d_feature = d_feature + jnp.einsum(
                "co,ohw->chw", w_short, d_short, preferred_element_type=jnp.float32
            )
        else:
            d_feature = d_feature + d_sum
        gradient = d_feature.astype(jnp.bfloat16)
        pieces[block_index] = [
            g_in,
            g_mid,
            g_expand,
            d_gain1,
            d_shift1,
            d_gain2,
            d_shift2,
            d_gain3,
            d_shift3,
        ]
    flat = []
    for block_index in range(levels):
        for piece in pieces[block_index]:
            flat.append(piece.reshape(-1))
    flat.append(g_short.reshape(-1))
    partial_vector = jnp.concatenate(flat)
    totals = all_sum(partial_vector, lax.axis_size("rows"), lax.axis_size("cols"))
    pixel_count = height * breadth * lax.axis_size("rows") * lax.axis_size("cols")
    scale = 1.0 / jnp.sqrt(jnp.float32(pixel_count))
    return (gradient, totals * scale)


def solution(mesh):
    in_specs = (
        P(None, "rows", "cols"),
        P(None, "cols"),
        P(),
        P(),
        P(),
        P(),
        P(),
        P(),
        P(),
        P(),
        P(),
        P(None, "rows", "cols"),
    )
    out_specs = (P(None, "rows", "cols"), P())
    return jax.shard_map(
        per_device, mesh=mesh, in_specs=in_specs, out_specs=out_specs, check_vma=False
    )
```

```python
import functools
import jax
import jax.numpy as jnp
from jax import lax
from jax.experimental import pallas as pl
from jax.experimental.pallas import tpu as pltpu
from jax.sharding import PartitionSpec as P

MESH = pl.DeviceIdType.MESH

BLOCK = 64


_TOWARD = ((-1, 0), (1, 0), (0, -1), (0, 1), (-1, -1), (-1, 1), (1, -1), (1, 1))


def _halo_kernel(nr, nc, e_ref, o_ref, send_sem, recv_sem):
    my_r = lax.axis_index("rows")
    my_c = lax.axis_index("cols")

    def present(dr, dc):
        ok = True
        if dr:
            ok = jnp.logical_and(ok, jnp.logical_and(my_r + dr >= 0, my_r + dr < nr))
        if dc:
            ok = jnp.logical_and(ok, jnp.logical_and(my_c + dc >= 0, my_c + dc < nc))
        return ok

    barrier = pltpu.get_barrier_semaphore()
    count = 0
    for dr, dc in _TOWARD:
        there = present(dr, dc)
        count = count + there.astype(jnp.int32)

        @pl.when(there)
        def _():
            pl.semaphore_signal(barrier, inc=1, device_id=(my_r + dr, my_c + dc), device_id_type=MESH)

    pl.semaphore_wait(barrier, count)

    def copy(k, dr, dc):
        return pltpu.make_async_remote_copy(
            src_ref=e_ref.at[k], dst_ref=o_ref.at[k], send_sem=send_sem.at[k],
            recv_sem=recv_sem.at[k], device_id=(my_r + dr, my_c + dc), device_id_type=MESH)

    for k, (dr, dc) in enumerate(_TOWARD):
        @pl.when(present(dr, dc))
        def _():
            copy(k, dr, dc).start()

        @pl.when(jnp.logical_not(present(-dr, -dc)))
        def _():
            o_ref[k] = jnp.zeros(o_ref.shape[1:], o_ref.dtype)

    for k, (dr, dc) in enumerate(_TOWARD):
        @pl.when(present(-dr, -dc))
        def _():
            copy(k, -dr, -dc).wait_recv()

        @pl.when(present(dr, dc))
        def _():
            copy(k, dr, dc).wait_send()


def exchange(cells, nr, nc):
    ch, h, w = cells.shape
    lanes = max(w, -(-h // 128) * 128)

    def wide(v):
        return jnp.pad(v, ((0, 0), (0, lanes - v.shape[1])))

    top, bottom = cells[:, 0, :], cells[:, h - 1, :]
    left, right = cells[:, :, 0], cells[:, :, w - 1]
    pieces = jnp.stack([
        wide(top), wide(bottom), wide(left), wide(right),
        wide(top[:, :1]), wide(top[:, w - 1:]), wide(bottom[:, :1]), wide(bottom[:, w - 1:]),
    ])
    got = pl.pallas_call(
        functools.partial(_halo_kernel, nr, nc),
        out_shape=jax.ShapeDtypeStruct(pieces.shape, pieces.dtype),
        in_specs=[pl.BlockSpec(memory_space=pltpu.VMEM)],
        out_specs=pl.BlockSpec(memory_space=pltpu.VMEM),
        scratch_shapes=[pltpu.SemaphoreType.DMA((8,)), pltpu.SemaphoreType.DMA((8,))],
        compiler_params=pltpu.CompilerParams(collective_id=1, has_side_effects=True),
    )(pieces)
    above = got[1, :, :w]
    below = got[0, :, :w]
    from_left = got[3, :, :h]
    from_right = got[2, :, :h]
    top_row = jnp.concatenate([got[7, :, :1], above, got[6, :, :1]], axis=1)
    bottom_row = jnp.concatenate([got[5, :, :1], below, got[4, :, :1]], axis=1)
    middle = jnp.concatenate([from_left[:, :, None], cells, from_right[:, :, None]], axis=2)
    return jnp.concatenate([top_row[:, None, :], middle, bottom_row[:, None, :]], axis=1)


def _sum_kernel(nr, nc, x_ref, o_ref, cpart, rpart, mine, sems, cs_send, cs_recv, r_send, r_recv, cg_send, cg_recv):
    my_r = lax.axis_index("rows")
    my_c = lax.axis_index("cols")

    def col_peer(j):
        return lax.rem(my_c + j, nc)

    def row_peer(j):
        return lax.rem(my_r + j, nr)

    barrier = pltpu.get_barrier_semaphore()

    def greet_c(j, c):
        pl.semaphore_signal(barrier, inc=1, device_id=(my_r, col_peer(j)), device_id_type=MESH)
        return c

    lax.fori_loop(1, nc, greet_c, 0)

    def greet_r(j, c):
        pl.semaphore_signal(barrier, inc=1, device_id=(row_peer(j), my_c), device_id_type=MESH)
        return c

    lax.fori_loop(1, nr, greet_r, 0)
    pl.semaphore_wait(barrier, nc + nr - 2)

    def c_scatter(p, s):
        return pltpu.make_async_remote_copy(
            src_ref=x_ref.at[p], dst_ref=cpart.at[s], send_sem=cs_send.at[p],
            recv_sem=cs_recv.at[s], device_id=(my_r, p), device_id_type=MESH)

    def start_cs(j, c):
        c_scatter(col_peer(j), my_c).start()
        return c

    lax.fori_loop(1, nc, start_cs, 0)
    cpart[my_c] = x_ref[my_c]

    def wait_cs(j, c):
        c_scatter(my_c, col_peer(j)).wait_recv()
        return c

    lax.fori_loop(1, nc, wait_cs, 0)
    mine[0] = lax.fori_loop(0, nc, lambda s, a: a + cpart[s], jnp.zeros(cpart.shape[1:], jnp.float32))
    own = pltpu.make_async_copy(mine.at[0], rpart.at[my_r], sems.at[0])
    own.start()
    own.wait()

    def r_share(q, s):
        return pltpu.make_async_remote_copy(
            src_ref=rpart.at[s], dst_ref=rpart.at[s], send_sem=r_send.at[q],
            recv_sem=r_recv.at[s], device_id=(q, my_c), device_id_type=MESH)

    def start_r(j, c):
        r_share(row_peer(j), my_r).start()
        return c

    lax.fori_loop(1, nr, start_r, 0)

    def wait_r(j, c):
        r_share(my_r, row_peer(j)).wait_recv()
        return c

    lax.fori_loop(1, nr, wait_r, 0)
    mine[1] = lax.fori_loop(0, nr, lambda s, a: a + rpart[s], jnp.zeros(rpart.shape[1:], jnp.float32))
    own = pltpu.make_async_copy(mine.at[1], o_ref.at[my_c], sems.at[1])
    own.start()
    own.wait()

    def c_gather(p, s):
        return pltpu.make_async_remote_copy(
            src_ref=o_ref.at[s], dst_ref=o_ref.at[s], send_sem=cg_send.at[p],
            recv_sem=cg_recv.at[s], device_id=(my_r, p), device_id_type=MESH)

    def start_cg(j, c):
        c_gather(col_peer(j), my_c).start()
        return c

    lax.fori_loop(1, nc, start_cg, 0)

    def wait_c(j, c):
        c_scatter(col_peer(j), my_c).wait_send()
        c_gather(my_c, col_peer(j)).wait_recv()
        c_gather(col_peer(j), my_c).wait_send()
        return c

    lax.fori_loop(1, nc, wait_c, 0)

    def wait_rs(j, c):
        r_share(row_peer(j), my_r).wait_send()
        return c

    lax.fori_loop(1, nr, wait_rs, 0)


def all_sum(pieces, nr, nc):
    length = sum(piece.size for piece in pieces)
    rows = -(-length // (nc * 128 * 8)) * 8
    tail = jnp.zeros((nc * rows * 128 - length,), jnp.float32)
    blocks = jnp.concatenate([piece.reshape(-1) for piece in pieces] + [tail]).reshape(nc, rows, 128)
    sem = pltpu.SemaphoreType.DMA
    out = pl.pallas_call(
        functools.partial(_sum_kernel, nr, nc),
        out_shape=jax.ShapeDtypeStruct(blocks.shape, jnp.float32),
        in_specs=[pl.BlockSpec(memory_space=pltpu.VMEM)],
        out_specs=pl.BlockSpec(memory_space=pltpu.VMEM),
        scratch_shapes=[
            pltpu.VMEM((nc, rows, 128), jnp.float32),
            pltpu.VMEM((nr, rows, 128), jnp.float32),
            pltpu.VMEM((2, rows, 128), jnp.float32),
            sem((2,)),
            sem((nc,)), sem((nc,)), sem((nr,)), sem((nr,)), sem((nc,)), sem((nc,)),
        ],
        compiler_params=pltpu.CompilerParams(collective_id=0, has_side_effects=True),
    )(blocks)
    return out.reshape(-1)[:length]


def padded_2(cells, sides, width):
    for axis, dim in sides:
        count = lax.axis_size(axis)
        ends = count - 1
        head = lax.slice_in_dim(cells, 0, width, axis=dim)
        tail = lax.slice_in_dim(cells, cells.shape[dim] - width, cells.shape[dim], axis=dim)
        cells = jnp.concatenate(
            [
                lax.ppermute(tail, axis, [(i, (i + 1) % count) for i in range(ends)]),
                cells,
                lax.ppermute(head, axis, [((i + 1) % count, i) for i in range(ends)]),
            ],
            axis=dim,
        )
    return cells


def pointwise(weight, field):
    return jnp.einsum("cm,chw->mhw", weight, field, preferred_element_type=jnp.float32)


def per_channel(vector):
    return vector[:, None, None]


def smooth_act(value):
    return value * jax.nn.sigmoid(value)


def smooth_slope(value):
    sigma = jax.nn.sigmoid(value)
    return sigma * (1.0 + value * (1.0 - sigma))


def spatial_conv(kernel, padded, height, breadth):
    result = jnp.zeros((kernel.shape[2], height, breadth), jnp.float32)
    for tap_row in range(3):
        for tap_col in range(3):
            window = padded[:, tap_row : tap_row + height, tap_col : tap_col + breadth]
            result = result + pointwise(kernel[3 * tap_row + tap_col], window)
    return result


def windows(padded, height, breadth, flip):
    taps = []
    for tap_row in range(3):
        for tap_col in range(3):
            i, j = (2 - tap_row, 2 - tap_col) if flip else (tap_row, tap_col)
            taps.append(padded[:, i : i + height, j : j + breadth])
    return jnp.concatenate(taps, axis=0)


def per_device(
    stem_out,
    tissue,
    w_first,
    w_reduce,
    w_mid,
    w_expand,
    w_short,
    gain_mid,
    shift_mid,
    gain_wide,
    shift_wide,
    upstream,
):
    height, breadth = (stem_out.shape[1], stem_out.shape[2])
    bands, tiles = tissue.shape
    values = tissue.astype(jnp.float32)[:, None, :, None]
    band_keep = jnp.broadcast_to(values, (bands, BLOCK, tiles, BLOCK)).reshape(
        bands * BLOCK, tiles * BLOCK
    )
    row_start = lax.axis_index("rows") * height
    tissue_keep = lax.dynamic_slice_in_dim(band_keep, row_start, height, 0)
    levels = w_mid.shape[0]
    saved_all = []
    feature = stem_out
    for block_index in range(levels):
        w_in = w_first if block_index == 0 else w_reduce[block_index - 1]
        pre_one = pointwise(w_in, feature)
        act_one = smooth_act(
            per_channel(gain_mid[block_index, 0]) * pre_one + per_channel(shift_mid[block_index, 0])
        ).astype(jnp.bfloat16)
        padded = exchange(act_one, lax.axis_size("rows"), lax.axis_size("cols"))
        stacked = windows(padded, height, breadth, False)
        pre_two = jnp.einsum(
            "km,khw->mhw", w_mid[block_index].reshape(-1, w_mid.shape[3]), stacked,
            preferred_element_type=jnp.float32,
        )
        act_two = smooth_act(
            per_channel(gain_mid[block_index, 1]) * pre_two + per_channel(shift_mid[block_index, 1])
        ).astype(jnp.bfloat16)
        pre_three = pointwise(w_expand[block_index], act_two)
        if block_index == 0:
            shortcut = pointwise(w_short, stem_out)
        else:
            shortcut = feature.astype(jnp.float32)
        summed = (
            per_channel(gain_wide[block_index]) * pre_three
            + per_channel(shift_wide[block_index])
            + shortcut
        )
        stored = stacked
        saved_all.append((feature, pre_one, stored, pre_two, act_two, pre_three, summed))
        feature = (smooth_act(summed) * tissue_keep).astype(jnp.bfloat16)
    gradient = upstream
    pieces = [None] * levels
    g_short = None
    for block_index in range(levels - 1, -1, -1):
        feature, pre_one, stored, pre_two, act_two, pre_three, summed = saved_all[block_index]
        w_in = w_first if block_index == 0 else w_reduce[block_index - 1]
        d_sum = gradient.astype(jnp.float32) * tissue_keep * smooth_slope(summed)
        d_gain3 = jnp.sum(d_sum * pre_three, axis=(1, 2))
        d_shift3 = jnp.sum(d_sum, axis=(1, 2))
        d_pre3 = (per_channel(gain_wide[block_index]) * d_sum).astype(jnp.bfloat16)
        g_expand = jnp.einsum("mhw,ohw->mo", act_two, d_pre3, preferred_element_type=jnp.float32)
        d_act2 = jnp.einsum(
            "mo,ohw->mhw", w_expand[block_index], d_pre3, preferred_element_type=jnp.float32
        )
        d_rel2 = d_act2 * smooth_slope(
            per_channel(gain_mid[block_index, 1]) * pre_two + per_channel(shift_mid[block_index, 1])
        )
        d_gain2 = jnp.sum(d_rel2 * pre_two, axis=(1, 2))
        d_shift2 = jnp.sum(d_rel2, axis=(1, 2))
        d_pre2 = (per_channel(gain_mid[block_index, 1]) * d_rel2).astype(jnp.bfloat16)
        g_mid = jnp.einsum(
            "khw,mhw->km", stored, d_pre2, preferred_element_type=jnp.float32
        ).reshape(w_mid.shape[1:])
        grad_pad = exchange(d_pre2, lax.axis_size("rows"), lax.axis_size("cols"))
        d_act1 = jnp.einsum(
            "km,khw->mhw",
            jnp.swapaxes(w_mid[block_index], 1, 2).reshape(-1, w_mid.shape[2]),
            windows(grad_pad, height, breadth, True),
            preferred_element_type=jnp.float32,
        )
        d_rel1 = d_act1 * smooth_slope(
            per_channel(gain_mid[block_index, 0]) * pre_one + per_channel(shift_mid[block_index, 0])
        )
        d_gain1 = jnp.sum(d_rel1 * pre_one, axis=(1, 2))
        d_shift1 = jnp.sum(d_rel1, axis=(1, 2))
        d_pre1 = (per_channel(gain_mid[block_index, 0]) * d_rel1).astype(jnp.bfloat16)
        g_in = jnp.einsum("chw,mhw->cm", feature, d_pre1, preferred_element_type=jnp.float32)
        d_feature = jnp.einsum("cm,mhw->chw", w_in, d_pre1, preferred_element_type=jnp.float32)
        if block_index == 0:
            d_short = d_sum.astype(jnp.bfloat16)
            g_short = jnp.einsum(
                "chw,ohw->co", feature, d_short, preferred_element_type=jnp.float32
            )
            d_feature = d_feature + jnp.einsum(
                "co,ohw->chw", w_short, d_short, preferred_element_type=jnp.float32
            )
        else:
            d_feature = d_feature + d_sum
        gradient = d_feature.astype(jnp.bfloat16)
        pieces[block_index] = [
            g_in,
            g_mid,
            g_expand,
            d_gain1,
            d_shift1,
            d_gain2,
            d_shift2,
            d_gain3,
            d_shift3,
        ]
    flat = []
    for block_index in range(levels):
        for piece in pieces[block_index]:
            flat.append(piece.reshape(-1))
    flat.append(g_short.reshape(-1))
    pixel_count = height * breadth * lax.axis_size("rows") * lax.axis_size("cols")
    scale = 1.0 / jnp.sqrt(jnp.float32(pixel_count))
    totals = all_sum([piece * scale for piece in flat], lax.axis_size("rows"), lax.axis_size("cols"))
    return (gradient, totals)


def solution(mesh):
    in_specs = (
        P(None, "rows", "cols"),
        P(None, "cols"),
        P(),
        P(),
        P(),
        P(),
        P(),
        P(),
        P(),
        P(),
        P(),
        P(None, "rows", "cols"),
    )
    out_specs = (P(None, "rows", "cols"), P())
    return jax.shard_map(
        per_device, mesh=mesh, in_specs=in_specs, out_specs=out_specs, check_vma=False
    )
```

```python
import functools
import jax
import jax.numpy as jnp
from jax import lax
from jax.experimental import pallas as pl
from jax.experimental.pallas import tpu as pltpu
from jax.sharding import PartitionSpec as P

MESH = pl.DeviceIdType.MESH

BLOCK = 64


_TOWARD = ((-1, 0), (1, 0), (0, -1), (0, 1), (-1, -1), (-1, 1), (1, -1), (1, 1))
_FIRST_FAR = (4, 5, 6, 7, 0, 1, 2, 3)


def _halo_kernel(nr, nc, e_ref, o_ref, send_sem, recv_sem):
    my_r = lax.axis_index("rows")
    my_c = lax.axis_index("cols")

    def present(dr, dc):
        ok = True
        if dr:
            ok = jnp.logical_and(ok, jnp.logical_and(my_r + dr >= 0, my_r + dr < nr))
        if dc:
            ok = jnp.logical_and(ok, jnp.logical_and(my_c + dc >= 0, my_c + dc < nc))
        return ok

    barrier = pltpu.get_barrier_semaphore()
    count = 0
    for dr, dc in _TOWARD[4:] + _TOWARD[:4]:
        there = present(dr, dc)
        count = count + there.astype(jnp.int32)

        @pl.when(there)
        def _():
            pl.semaphore_signal(barrier, inc=1, device_id=(my_r + dr, my_c + dc), device_id_type=MESH)

    pl.semaphore_wait(barrier, count)

    def copy(k, dr, dc):
        return pltpu.make_async_remote_copy(
            src_ref=e_ref.at[k], dst_ref=o_ref.at[k], send_sem=send_sem.at[k],
            recv_sem=recv_sem.at[k], device_id=(my_r + dr, my_c + dc), device_id_type=MESH)

    for k in _FIRST_FAR:
        dr, dc = _TOWARD[k]

        @pl.when(present(dr, dc))
        def _():
            copy(k, dr, dc).start()

        @pl.when(jnp.logical_not(present(-dr, -dc)))
        def _():
            o_ref[k] = jnp.zeros(o_ref.shape[1:], o_ref.dtype)

    for k, (dr, dc) in enumerate(_TOWARD):
        @pl.when(present(-dr, -dc))
        def _():
            copy(k, -dr, -dc).wait_recv()

        @pl.when(present(dr, dc))
        def _():
            copy(k, dr, dc).wait_send()


def exchange(cells, nr, nc):
    ch, h, w = cells.shape
    lanes = max(w, -(-h // 128) * 128)

    def wide(v):
        return jnp.pad(v, ((0, 0), (0, lanes - v.shape[1])))

    top, bottom = cells[:, 0, :], cells[:, h - 1, :]
    left, right = cells[:, :, 0], cells[:, :, w - 1]
    pieces = jnp.stack([
        wide(top), wide(bottom), wide(left), wide(right),
        wide(top[:, :1]), wide(top[:, w - 1:]), wide(bottom[:, :1]), wide(bottom[:, w - 1:]),
    ])
    got = pl.pallas_call(
        functools.partial(_halo_kernel, nr, nc),
        out_shape=jax.ShapeDtypeStruct(pieces.shape, pieces.dtype),
        in_specs=[pl.BlockSpec(memory_space=pltpu.VMEM)],
        out_specs=pl.BlockSpec(memory_space=pltpu.VMEM),
        scratch_shapes=[pltpu.SemaphoreType.DMA((8,)), pltpu.SemaphoreType.DMA((8,))],
        compiler_params=pltpu.CompilerParams(collective_id=1, has_side_effects=True),
    )(pieces)
    above = got[1, :, :w]
    below = got[0, :, :w]
    from_left = got[3, :, :h]
    from_right = got[2, :, :h]
    top_row = jnp.concatenate([got[7, :, :1], above, got[6, :, :1]], axis=1)
    bottom_row = jnp.concatenate([got[5, :, :1], below, got[4, :, :1]], axis=1)
    middle = jnp.concatenate([from_left[:, :, None], cells, from_right[:, :, None]], axis=2)
    return jnp.concatenate([top_row[:, None, :], middle, bottom_row[:, None, :]], axis=1)


def _sum_kernel(nr, nc, x_ref, o_ref, cpart, rpart, mine, sems, cs_send, cs_recv, r_send, r_recv, cg_send, cg_recv):
    my_r = lax.axis_index("rows")
    my_c = lax.axis_index("cols")

    def col_peer(j):
        return lax.rem(my_c + j, nc)

    def row_peer(j):
        return lax.rem(my_r + j, nr)

    barrier = pltpu.get_barrier_semaphore()

    def greet_c(j, c):
        pl.semaphore_signal(barrier, inc=1, device_id=(my_r, col_peer(j)), device_id_type=MESH)
        return c

    lax.fori_loop(1, nc, greet_c, 0)

    def greet_r(j, c):
        pl.semaphore_signal(barrier, inc=1, device_id=(row_peer(j), my_c), device_id_type=MESH)
        return c

    lax.fori_loop(1, nr, greet_r, 0)
    pl.semaphore_wait(barrier, nc + nr - 2)

    def c_scatter(p, s):
        return pltpu.make_async_remote_copy(
            src_ref=x_ref.at[p], dst_ref=cpart.at[s], send_sem=cs_send.at[p],
            recv_sem=cs_recv.at[s], device_id=(my_r, p), device_id_type=MESH)

    def start_cs(j, c):
        c_scatter(col_peer(j), my_c).start()
        return c

    lax.fori_loop(1, nc, start_cs, 0)
    cpart[my_c] = x_ref[my_c]

    def wait_cs(j, c):
        c_scatter(my_c, col_peer(j)).wait_recv()
        return c

    lax.fori_loop(1, nc, wait_cs, 0)
    mine[0] = lax.fori_loop(0, nc, lambda s, a: a + cpart[s], jnp.zeros(cpart.shape[1:], jnp.float32))
    own = pltpu.make_async_copy(mine.at[0], rpart.at[my_r], sems.at[0])
    own.start()
    own.wait()

    def r_share(q, s):
        return pltpu.make_async_remote_copy(
            src_ref=rpart.at[s], dst_ref=rpart.at[s], send_sem=r_send.at[q],
            recv_sem=r_recv.at[s], device_id=(q, my_c), device_id_type=MESH)

    def start_r(j, c):
        r_share(row_peer(j), my_r).start()
        return c

    lax.fori_loop(1, nr, start_r, 0)

    def wait_r(j, c):
        r_share(my_r, row_peer(j)).wait_recv()
        return c

    lax.fori_loop(1, nr, wait_r, 0)
    mine[1] = lax.fori_loop(0, nr, lambda s, a: a + rpart[s], jnp.zeros(rpart.shape[1:], jnp.float32))
    own = pltpu.make_async_copy(mine.at[1], o_ref.at[my_c], sems.at[1])
    own.start()
    own.wait()

    def c_gather(p, s):
        return pltpu.make_async_remote_copy(
            src_ref=o_ref.at[s], dst_ref=o_ref.at[s], send_sem=cg_send.at[p],
            recv_sem=cg_recv.at[s], device_id=(my_r, p), device_id_type=MESH)

    def start_cg(j, c):
        c_gather(col_peer(j), my_c).start()
        return c

    lax.fori_loop(1, nc, start_cg, 0)

    def wait_c(j, c):
        c_scatter(col_peer(j), my_c).wait_send()
        c_gather(my_c, col_peer(j)).wait_recv()
        c_gather(col_peer(j), my_c).wait_send()
        return c

    lax.fori_loop(1, nc, wait_c, 0)

    def wait_rs(j, c):
        r_share(row_peer(j), my_r).wait_send()
        return c

    lax.fori_loop(1, nr, wait_rs, 0)


def all_sum(vector, nr, nc):
    length = vector.shape[0]
    rows = -(-length // (nc * 128 * 8)) * 8
    blocks = jnp.pad(vector, (0, nc * rows * 128 - length)).reshape(nc, rows, 128)
    sem = pltpu.SemaphoreType.DMA
    out = pl.pallas_call(
        functools.partial(_sum_kernel, nr, nc),
        out_shape=jax.ShapeDtypeStruct(blocks.shape, jnp.float32),
        in_specs=[pl.BlockSpec(memory_space=pltpu.VMEM)],
        out_specs=pl.BlockSpec(memory_space=pltpu.VMEM),
        scratch_shapes=[
            pltpu.VMEM((nc, rows, 128), jnp.float32),
            pltpu.VMEM((nr, rows, 128), jnp.float32),
            pltpu.VMEM((2, rows, 128), jnp.float32),
            sem((2,)),
            sem((nc,)), sem((nc,)), sem((nr,)), sem((nr,)), sem((nc,)), sem((nc,)),
        ],
        compiler_params=pltpu.CompilerParams(collective_id=0, has_side_effects=True),
    )(blocks)
    return out.reshape(-1)[:length]


def padded_2(cells, sides, width):
    for axis, dim in sides:
        count = lax.axis_size(axis)
        ends = count - 1
        head = lax.slice_in_dim(cells, 0, width, axis=dim)
        tail = lax.slice_in_dim(cells, cells.shape[dim] - width, cells.shape[dim], axis=dim)
        cells = jnp.concatenate(
            [
                lax.ppermute(tail, axis, [(i, (i + 1) % count) for i in range(ends)]),
                cells,
                lax.ppermute(head, axis, [((i + 1) % count, i) for i in range(ends)]),
            ],
            axis=dim,
        )
    return cells


def pointwise(weight, field):
    return jnp.einsum("cm,chw->mhw", weight, field, preferred_element_type=jnp.float32)


def per_channel(vector):
    return vector[:, None, None]


def smooth_act(value):
    return value * jax.nn.sigmoid(value)


def smooth_slope(value):
    sigma = jax.nn.sigmoid(value)
    return sigma * (1.0 + value * (1.0 - sigma))


def spatial_conv(kernel, padded, height, breadth):
    result = jnp.zeros((kernel.shape[2], height, breadth), jnp.float32)
    for tap_row in range(3):
        for tap_col in range(3):
            window = padded[:, tap_row : tap_row + height, tap_col : tap_col + breadth]
            result = result + pointwise(kernel[3 * tap_row + tap_col], window)
    return result


def windows(padded, height, breadth, flip):
    taps = []
    for tap_row in range(3):
        for tap_col in range(3):
            i, j = (2 - tap_row, 2 - tap_col) if flip else (tap_row, tap_col)
            taps.append(padded[:, i : i + height, j : j + breadth])
    return jnp.concatenate(taps, axis=0)


def per_device(
    stem_out,
    tissue,
    w_first,
    w_reduce,
    w_mid,
    w_expand,
    w_short,
    gain_mid,
    shift_mid,
    gain_wide,
    shift_wide,
    upstream,
):
    height, breadth = (stem_out.shape[1], stem_out.shape[2])
    bands, tiles = tissue.shape
    values = tissue.astype(jnp.float32)[:, None, :, None]
    band_keep = jnp.broadcast_to(values, (bands, BLOCK, tiles, BLOCK)).reshape(
        bands * BLOCK, tiles * BLOCK
    )
    row_start = lax.axis_index("rows") * height
    tissue_keep = lax.dynamic_slice_in_dim(band_keep, row_start, height, 0)
    levels = w_mid.shape[0]
    saved_all = []
    feature = stem_out
    for block_index in range(levels):
        w_in = w_first if block_index == 0 else w_reduce[block_index - 1]
        pre_one = pointwise(w_in, feature)
        act_one = smooth_act(
            per_channel(gain_mid[block_index, 0]) * pre_one + per_channel(shift_mid[block_index, 0])
        ).astype(jnp.bfloat16)
        padded = exchange(act_one, lax.axis_size("rows"), lax.axis_size("cols"))
        stacked = windows(padded, height, breadth, False)
        pre_two = jnp.einsum(
            "km,khw->mhw", w_mid[block_index].reshape(-1, w_mid.shape[3]), stacked,
            preferred_element_type=jnp.float32,
        )
        act_two = smooth_act(
            per_channel(gain_mid[block_index, 1]) * pre_two + per_channel(shift_mid[block_index, 1])
        ).astype(jnp.bfloat16)
        pre_three = pointwise(w_expand[block_index], act_two)
        if block_index == 0:
            shortcut = pointwise(w_short, stem_out)
        else:
            shortcut = feature.astype(jnp.float32)
        summed = (
            per_channel(gain_wide[block_index]) * pre_three
            + per_channel(shift_wide[block_index])
            + shortcut
        )
        stored = stacked
        saved_all.append((feature, pre_one, stored, pre_two, act_two, pre_three, summed))
        feature = (smooth_act(summed) * tissue_keep).astype(jnp.bfloat16)
    gradient = upstream
    pieces = [None] * levels
    g_short = None
    for block_index in range(levels - 1, -1, -1):
        feature, pre_one, stored, pre_two, act_two, pre_three, summed = saved_all[block_index]
        w_in = w_first if block_index == 0 else w_reduce[block_index - 1]
        d_sum = gradient.astype(jnp.float32) * tissue_keep * smooth_slope(summed)
        d_gain3 = jnp.sum(d_sum * pre_three, axis=(1, 2))
        d_shift3 = jnp.sum(d_sum, axis=(1, 2))
        d_pre3 = (per_channel(gain_wide[block_index]) * d_sum).astype(jnp.bfloat16)
        g_expand = jnp.einsum("mhw,ohw->mo", act_two, d_pre3, preferred_element_type=jnp.float32)
        d_act2 = jnp.einsum(
            "mo,ohw->mhw", w_expand[block_index], d_pre3, preferred_element_type=jnp.float32
        )
        d_rel2 = d_act2 * smooth_slope(
            per_channel(gain_mid[block_index, 1]) * pre_two + per_channel(shift_mid[block_index, 1])
        )
        d_gain2 = jnp.sum(d_rel2 * pre_two, axis=(1, 2))
        d_shift2 = jnp.sum(d_rel2, axis=(1, 2))
        d_pre2 = (per_channel(gain_mid[block_index, 1]) * d_rel2).astype(jnp.bfloat16)
        g_mid = jnp.einsum(
            "khw,mhw->km", stored, d_pre2, preferred_element_type=jnp.float32
        ).reshape(w_mid.shape[1:])
        grad_pad = exchange(d_pre2, lax.axis_size("rows"), lax.axis_size("cols"))
        d_act1 = jnp.einsum(
            "km,khw->mhw",
            jnp.swapaxes(w_mid[block_index], 1, 2).reshape(-1, w_mid.shape[2]),
            windows(grad_pad, height, breadth, True),
            preferred_element_type=jnp.float32,
        )
        d_rel1 = d_act1 * smooth_slope(
            per_channel(gain_mid[block_index, 0]) * pre_one + per_channel(shift_mid[block_index, 0])
        )
        d_gain1 = jnp.sum(d_rel1 * pre_one, axis=(1, 2))
        d_shift1 = jnp.sum(d_rel1, axis=(1, 2))
        d_pre1 = (per_channel(gain_mid[block_index, 0]) * d_rel1).astype(jnp.bfloat16)
        g_in = jnp.einsum("chw,mhw->cm", feature, d_pre1, preferred_element_type=jnp.float32)
        d_feature = jnp.einsum("cm,mhw->chw", w_in, d_pre1, preferred_element_type=jnp.float32)
        if block_index == 0:
            d_short = d_sum.astype(jnp.bfloat16)
            g_short = jnp.einsum(
                "chw,ohw->co", feature, d_short, preferred_element_type=jnp.float32
            )
            d_feature = d_feature + jnp.einsum(
                "co,ohw->chw", w_short, d_short, preferred_element_type=jnp.float32
            )
        else:
            d_feature = d_feature + d_sum
        gradient = d_feature.astype(jnp.bfloat16)
        pieces[block_index] = [
            g_in,
            g_mid,
            g_expand,
            d_gain1,
            d_shift1,
            d_gain2,
            d_shift2,
            d_gain3,
            d_shift3,
        ]
    flat = []
    for block_index in range(levels):
        for piece in pieces[block_index]:
            flat.append(piece.reshape(-1))
    flat.append(g_short.reshape(-1))
    partial_vector = jnp.concatenate(flat)
    totals = all_sum(partial_vector, lax.axis_size("rows"), lax.axis_size("cols"))
    pixel_count = height * breadth * lax.axis_size("rows") * lax.axis_size("cols")
    scale = 1.0 / jnp.sqrt(jnp.float32(pixel_count))
    return (gradient, totals * scale)


def solution(mesh):
    in_specs = (
        P(None, "rows", "cols"),
        P(None, "cols"),
        P(),
        P(),
        P(),
        P(),
        P(),
        P(),
        P(),
        P(),
        P(),
        P(None, "rows", "cols"),
    )
    out_specs = (P(None, "rows", "cols"), P())
    return jax.shard_map(
        per_device, mesh=mesh, in_specs=in_specs, out_specs=out_specs, check_vma=False
    )
```

```python
import functools
import jax
import jax.numpy as jnp
from jax import lax
from jax.experimental import pallas as pl
from jax.experimental.pallas import tpu as pltpu
from jax.sharding import PartitionSpec as P

MESH = pl.DeviceIdType.MESH

BLOCK = 64


_TOWARD = ((-1, 0), (1, 0), (0, -1), (0, 1), (-1, -1), (-1, 1), (1, -1), (1, 1))
_FIRST_FAR = (4, 5, 6, 7, 0, 1, 2, 3)


def _halo_kernel(nr, nc, e_ref, o_ref, send_sem, recv_sem):
    my_r = lax.axis_index("rows")
    my_c = lax.axis_index("cols")

    def present(dr, dc):
        ok = True
        if dr:
            ok = jnp.logical_and(ok, jnp.logical_and(my_r + dr >= 0, my_r + dr < nr))
        if dc:
            ok = jnp.logical_and(ok, jnp.logical_and(my_c + dc >= 0, my_c + dc < nc))
        return ok

    barrier = pltpu.get_barrier_semaphore()
    count = 0
    for dr, dc in _TOWARD[4:] + _TOWARD[:4]:
        there = present(dr, dc)
        count = count + there.astype(jnp.int32)

        @pl.when(there)
        def _():
            pl.semaphore_signal(barrier, inc=1, device_id=(my_r + dr, my_c + dc), device_id_type=MESH)

    pl.semaphore_wait(barrier, count)

    def copy(k, dr, dc):
        return pltpu.make_async_remote_copy(
            src_ref=e_ref.at[k], dst_ref=o_ref.at[k], send_sem=send_sem.at[k],
            recv_sem=recv_sem.at[k], device_id=(my_r + dr, my_c + dc), device_id_type=MESH)

    for k in _FIRST_FAR:
        dr, dc = _TOWARD[k]

        @pl.when(present(dr, dc))
        def _():
            copy(k, dr, dc).start()

        @pl.when(jnp.logical_not(present(-dr, -dc)))
        def _():
            o_ref[k] = jnp.zeros(o_ref.shape[1:], o_ref.dtype)

    for k, (dr, dc) in enumerate(_TOWARD):
        @pl.when(present(-dr, -dc))
        def _():
            copy(k, -dr, -dc).wait_recv()

        @pl.when(present(dr, dc))
        def _():
            copy(k, dr, dc).wait_send()


def exchange(cells, nr, nc):
    ch, h, w = cells.shape
    lanes = max(w, -(-h // 128) * 128)

    def wide(v):
        return jnp.pad(v, ((0, 0), (0, lanes - v.shape[1])))

    top, bottom = cells[:, 0, :], cells[:, h - 1, :]
    left, right = cells[:, :, 0], cells[:, :, w - 1]
    pieces = jnp.stack([
        wide(top), wide(bottom), wide(left), wide(right),
        wide(top[:, :1]), wide(top[:, w - 1:]), wide(bottom[:, :1]), wide(bottom[:, w - 1:]),
    ])
    got = pl.pallas_call(
        functools.partial(_halo_kernel, nr, nc),
        out_shape=jax.ShapeDtypeStruct(pieces.shape, pieces.dtype),
        in_specs=[pl.BlockSpec(memory_space=pltpu.VMEM)],
        out_specs=pl.BlockSpec(memory_space=pltpu.VMEM),
        scratch_shapes=[pltpu.SemaphoreType.DMA((8,)), pltpu.SemaphoreType.DMA((8,))],
        compiler_params=pltpu.CompilerParams(collective_id=1, has_side_effects=True),
    )(pieces)
    above = got[1, :, :w]
    below = got[0, :, :w]
    from_left = got[3, :, :h]
    from_right = got[2, :, :h]
    top_row = jnp.concatenate([got[7, :, :1], above, got[6, :, :1]], axis=1)
    bottom_row = jnp.concatenate([got[5, :, :1], below, got[4, :, :1]], axis=1)
    middle = jnp.concatenate([from_left[:, :, None], cells, from_right[:, :, None]], axis=2)
    return jnp.concatenate([top_row[:, None, :], middle, bottom_row[:, None, :]], axis=1)


def _sum_kernel(nr, nc, x_ref, o_ref, cpart, rpart, mine, sems, cs_send, cs_recv, r_send, r_recv, cg_send, cg_recv):
    my_r = lax.axis_index("rows")
    my_c = lax.axis_index("cols")

    def col_peer(j):
        return lax.rem(my_c + j, nc)

    def row_peer(j):
        return lax.rem(my_r + j, nr)

    barrier = pltpu.get_barrier_semaphore()

    def greet_c(j, c):
        pl.semaphore_signal(barrier, inc=1, device_id=(my_r, col_peer(j)), device_id_type=MESH)
        return c

    lax.fori_loop(1, nc, greet_c, 0)

    def greet_r(j, c):
        pl.semaphore_signal(barrier, inc=1, device_id=(row_peer(j), my_c), device_id_type=MESH)
        return c

    lax.fori_loop(1, nr, greet_r, 0)
    pl.semaphore_wait(barrier, nc + nr - 2)

    def c_scatter(p, s):
        return pltpu.make_async_remote_copy(
            src_ref=x_ref.at[p], dst_ref=cpart.at[s], send_sem=cs_send.at[p],
            recv_sem=cs_recv.at[s], device_id=(my_r, p), device_id_type=MESH)

    def start_cs(j, c):
        c_scatter(col_peer(j), my_c).start()
        return c

    lax.fori_loop(1, nc, start_cs, 0)
    cpart[my_c] = x_ref[my_c]

    def wait_cs(j, c):
        c_scatter(my_c, col_peer(j)).wait_recv()
        return c

    lax.fori_loop(1, nc, wait_cs, 0)
    mine[0] = lax.fori_loop(0, nc, lambda s, a: a + cpart[s], jnp.zeros(cpart.shape[1:], jnp.float32))
    own = pltpu.make_async_copy(mine.at[0], rpart.at[my_r], sems.at[0])
    own.start()
    own.wait()

    def r_share(q, s):
        return pltpu.make_async_remote_copy(
            src_ref=rpart.at[s], dst_ref=rpart.at[s], send_sem=r_send.at[q],
            recv_sem=r_recv.at[s], device_id=(q, my_c), device_id_type=MESH)

    def start_r(j, c):
        r_share(row_peer(j), my_r).start()
        return c

    lax.fori_loop(1, nr, start_r, 0)

    def wait_r(j, c):
        r_share(my_r, row_peer(j)).wait_recv()
        return c

    lax.fori_loop(1, nr, wait_r, 0)
    mine[1] = lax.fori_loop(0, nr, lambda s, a: a + rpart[s], jnp.zeros(rpart.shape[1:], jnp.float32))
    own = pltpu.make_async_copy(mine.at[1], o_ref.at[my_c], sems.at[1])
    own.start()
    own.wait()

    def c_gather(p, s):
        return pltpu.make_async_remote_copy(
            src_ref=o_ref.at[s], dst_ref=o_ref.at[s], send_sem=cg_send.at[p],
            recv_sem=cg_recv.at[s], device_id=(my_r, p), device_id_type=MESH)

    def start_cg(j, c):
        c_gather(col_peer(j), my_c).start()
        return c

    lax.fori_loop(1, nc, start_cg, 0)

    def wait_c(j, c):
        c_scatter(col_peer(j), my_c).wait_send()
        c_gather(my_c, col_peer(j)).wait_recv()
        c_gather(col_peer(j), my_c).wait_send()
        return c

    lax.fori_loop(1, nc, wait_c, 0)

    def wait_rs(j, c):
        r_share(row_peer(j), my_r).wait_send()
        return c

    lax.fori_loop(1, nr, wait_rs, 0)


def all_sum(pieces, nr, nc):
    length = sum(piece.size for piece in pieces)
    rows = -(-length // (nc * 128 * 8)) * 8
    tail = jnp.zeros((nc * rows * 128 - length,), jnp.float32)
    blocks = jnp.concatenate([piece.reshape(-1) for piece in pieces] + [tail]).reshape(nc, rows, 128)
    sem = pltpu.SemaphoreType.DMA
    out = pl.pallas_call(
        functools.partial(_sum_kernel, nr, nc),
        out_shape=jax.ShapeDtypeStruct(blocks.shape, jnp.float32),
        in_specs=[pl.BlockSpec(memory_space=pltpu.VMEM)],
        out_specs=pl.BlockSpec(memory_space=pltpu.VMEM),
        scratch_shapes=[
            pltpu.VMEM((nc, rows, 128), jnp.float32),
            pltpu.VMEM((nr, rows, 128), jnp.float32),
            pltpu.VMEM((2, rows, 128), jnp.float32),
            sem((2,)),
            sem((nc,)), sem((nc,)), sem((nr,)), sem((nr,)), sem((nc,)), sem((nc,)),
        ],
        compiler_params=pltpu.CompilerParams(collective_id=0, has_side_effects=True),
    )(blocks)
    return out.reshape(-1)[:length]


def padded_2(cells, sides, width):
    for axis, dim in sides:
        count = lax.axis_size(axis)
        ends = count - 1
        head = lax.slice_in_dim(cells, 0, width, axis=dim)
        tail = lax.slice_in_dim(cells, cells.shape[dim] - width, cells.shape[dim], axis=dim)
        cells = jnp.concatenate(
            [
                lax.ppermute(tail, axis, [(i, (i + 1) % count) for i in range(ends)]),
                cells,
                lax.ppermute(head, axis, [((i + 1) % count, i) for i in range(ends)]),
            ],
            axis=dim,
        )
    return cells


def pointwise(weight, field):
    return jnp.einsum("cm,chw->mhw", weight, field, preferred_element_type=jnp.float32)


def per_channel(vector):
    return vector[:, None, None]


def smooth_act(value):
    return value * jax.nn.sigmoid(value)


def smooth_slope(value):
    sigma = jax.nn.sigmoid(value)
    return sigma * (1.0 + value * (1.0 - sigma))


def spatial_conv(kernel, padded, height, breadth):
    result = jnp.zeros((kernel.shape[2], height, breadth), jnp.float32)
    for tap_row in range(3):
        for tap_col in range(3):
            window = padded[:, tap_row : tap_row + height, tap_col : tap_col + breadth]
            result = result + pointwise(kernel[3 * tap_row + tap_col], window)
    return result


def windows(padded, height, breadth, flip):
    taps = []
    for tap_row in range(3):
        for tap_col in range(3):
            i, j = (2 - tap_row, 2 - tap_col) if flip else (tap_row, tap_col)
            taps.append(padded[:, i : i + height, j : j + breadth])
    return jnp.concatenate(taps, axis=0)


def per_device(
    stem_out,
    tissue,
    w_first,
    w_reduce,
    w_mid,
    w_expand,
    w_short,
    gain_mid,
    shift_mid,
    gain_wide,
    shift_wide,
    upstream,
):
    height, breadth = (stem_out.shape[1], stem_out.shape[2])
    bands, tiles = tissue.shape
    values = tissue.astype(jnp.float32)[:, None, :, None]
    band_keep = jnp.broadcast_to(values, (bands, BLOCK, tiles, BLOCK)).reshape(
        bands * BLOCK, tiles * BLOCK
    )
    row_start = lax.axis_index("rows") * height
    tissue_keep = lax.dynamic_slice_in_dim(band_keep, row_start, height, 0)
    levels = w_mid.shape[0]
    saved_all = []
    feature = stem_out
    for block_index in range(levels):
        w_in = w_first if block_index == 0 else w_reduce[block_index - 1]
        pre_one = pointwise(w_in, feature)
        act_one = smooth_act(
            per_channel(gain_mid[block_index, 0]) * pre_one + per_channel(shift_mid[block_index, 0])
        ).astype(jnp.bfloat16)
        padded = exchange(act_one, lax.axis_size("rows"), lax.axis_size("cols"))
        stacked = windows(padded, height, breadth, False)
        pre_two = jnp.einsum(
            "km,khw->mhw", w_mid[block_index].reshape(-1, w_mid.shape[3]), stacked,
            preferred_element_type=jnp.float32,
        )
        act_two = smooth_act(
            per_channel(gain_mid[block_index, 1]) * pre_two + per_channel(shift_mid[block_index, 1])
        ).astype(jnp.bfloat16)
        pre_three = pointwise(w_expand[block_index], act_two)
        if block_index == 0:
            shortcut = pointwise(w_short, stem_out)
        else:
            shortcut = feature.astype(jnp.float32)
        summed = (
            per_channel(gain_wide[block_index]) * pre_three
            + per_channel(shift_wide[block_index])
            + shortcut
        )
        stored = stacked
        saved_all.append((feature, pre_one, stored, pre_two, act_two, pre_three, summed))
        feature = (smooth_act(summed) * tissue_keep).astype(jnp.bfloat16)
    gradient = upstream
    pieces = [None] * levels
    g_short = None
    for block_index in range(levels - 1, -1, -1):
        feature, pre_one, stored, pre_two, act_two, pre_three, summed = saved_all[block_index]
        w_in = w_first if block_index == 0 else w_reduce[block_index - 1]
        d_sum = gradient.astype(jnp.float32) * tissue_keep * smooth_slope(summed)
        d_gain3 = jnp.sum(d_sum * pre_three, axis=(1, 2))
        d_shift3 = jnp.sum(d_sum, axis=(1, 2))
        d_pre3 = (per_channel(gain_wide[block_index]) * d_sum).astype(jnp.bfloat16)
        g_expand = jnp.einsum("mhw,ohw->mo", act_two, d_pre3, preferred_element_type=jnp.float32)
        d_act2 = jnp.einsum(
            "mo,ohw->mhw", w_expand[block_index], d_pre3, preferred_element_type=jnp.float32
        )
        d_rel2 = d_act2 * smooth_slope(
            per_channel(gain_mid[block_index, 1]) * pre_two + per_channel(shift_mid[block_index, 1])
        )
        d_gain2 = jnp.sum(d_rel2 * pre_two, axis=(1, 2))
        d_shift2 = jnp.sum(d_rel2, axis=(1, 2))
        d_pre2 = (per_channel(gain_mid[block_index, 1]) * d_rel2).astype(jnp.bfloat16)
        g_mid = jnp.einsum(
            "khw,mhw->km", stored, d_pre2, preferred_element_type=jnp.float32
        ).reshape(w_mid.shape[1:])
        grad_pad = exchange(d_pre2, lax.axis_size("rows"), lax.axis_size("cols"))
        d_act1 = jnp.einsum(
            "km,khw->mhw",
            jnp.swapaxes(w_mid[block_index], 1, 2).reshape(-1, w_mid.shape[2]),
            windows(grad_pad, height, breadth, True),
            preferred_element_type=jnp.float32,
        )
        d_rel1 = d_act1 * smooth_slope(
            per_channel(gain_mid[block_index, 0]) * pre_one + per_channel(shift_mid[block_index, 0])
        )
        d_gain1 = jnp.sum(d_rel1 * pre_one, axis=(1, 2))
        d_shift1 = jnp.sum(d_rel1, axis=(1, 2))
        d_pre1 = (per_channel(gain_mid[block_index, 0]) * d_rel1).astype(jnp.bfloat16)
        g_in = jnp.einsum("chw,mhw->cm", feature, d_pre1, preferred_element_type=jnp.float32)
        d_feature = jnp.einsum("cm,mhw->chw", w_in, d_pre1, preferred_element_type=jnp.float32)
        if block_index == 0:
            d_short = d_sum.astype(jnp.bfloat16)
            g_short = jnp.einsum(
                "chw,ohw->co", feature, d_short, preferred_element_type=jnp.float32
            )
            d_feature = d_feature + jnp.einsum(
                "co,ohw->chw", w_short, d_short, preferred_element_type=jnp.float32
            )
        else:
            d_feature = d_feature + d_sum
        gradient = d_feature.astype(jnp.bfloat16)
        pieces[block_index] = [
            g_in,
            g_mid,
            g_expand,
            d_gain1,
            d_shift1,
            d_gain2,
            d_shift2,
            d_gain3,
            d_shift3,
        ]
    flat = []
    for block_index in range(levels):
        for piece in pieces[block_index]:
            flat.append(piece.reshape(-1))
    flat.append(g_short.reshape(-1))
    totals = all_sum(flat, lax.axis_size("rows"), lax.axis_size("cols"))
    pixel_count = height * breadth * lax.axis_size("rows") * lax.axis_size("cols")
    scale = 1.0 / jnp.sqrt(jnp.float32(pixel_count))
    return (gradient, totals * scale)


def solution(mesh):
    in_specs = (
        P(None, "rows", "cols"),
        P(None, "cols"),
        P(),
        P(),
        P(),
        P(),
        P(),
        P(),
        P(),
        P(),
        P(),
        P(None, "rows", "cols"),
    )
    out_specs = (P(None, "rows", "cols"), P())
    return jax.shard_map(
        per_device, mesh=mesh, in_specs=in_specs, out_specs=out_specs, check_vma=False
    )
```

```python
import functools
import jax
import jax.numpy as jnp
from jax import lax
from jax.experimental import pallas as pl
from jax.experimental.pallas import tpu as pltpu
from jax.sharding import PartitionSpec as P

MESH = pl.DeviceIdType.MESH

BLOCK = 64


_TOWARD = ((-1, 0), (1, 0), (0, -1), (0, 1), (-1, -1), (-1, 1), (1, -1), (1, 1))
_FIRST_FAR = (4, 5, 6, 7, 0, 1, 2, 3)


def _halo_kernel(nr, nc, e_ref, o_ref, send_sem, recv_sem):
    my_r = lax.axis_index("rows")
    my_c = lax.axis_index("cols")

    def present(dr, dc):
        ok = True
        if dr:
            ok = jnp.logical_and(ok, jnp.logical_and(my_r + dr >= 0, my_r + dr < nr))
        if dc:
            ok = jnp.logical_and(ok, jnp.logical_and(my_c + dc >= 0, my_c + dc < nc))
        return ok

    barrier = pltpu.get_barrier_semaphore()
    count = 0
    for dr, dc in _TOWARD[4:] + _TOWARD[:4]:
        there = present(dr, dc)
        count = count + there.astype(jnp.int32)

        @pl.when(there)
        def _():
            pl.semaphore_signal(barrier, inc=1, device_id=(my_r + dr, my_c + dc), device_id_type=MESH)

    pl.semaphore_wait(barrier, count)

    def copy(k, dr, dc):
        return pltpu.make_async_remote_copy(
            src_ref=e_ref.at[k], dst_ref=o_ref.at[k], send_sem=send_sem.at[k],
            recv_sem=recv_sem.at[k], device_id=(my_r + dr, my_c + dc), device_id_type=MESH)

    for k in _FIRST_FAR:
        dr, dc = _TOWARD[k]

        @pl.when(present(dr, dc))
        def _():
            copy(k, dr, dc).start()

        @pl.when(jnp.logical_not(present(-dr, -dc)))
        def _():
            o_ref[k] = jnp.zeros(o_ref.shape[1:], o_ref.dtype)

    for k, (dr, dc) in enumerate(_TOWARD):
        @pl.when(present(-dr, -dc))
        def _():
            copy(k, -dr, -dc).wait_recv()

        @pl.when(present(dr, dc))
        def _():
            copy(k, dr, dc).wait_send()


def exchange(cells, nr, nc):
    ch, h, w = cells.shape
    lanes = max(w, -(-h // 128) * 128)

    def wide(v):
        return jnp.pad(v, ((0, 0), (0, lanes - v.shape[1])))

    top, bottom = cells[:, 0, :], cells[:, h - 1, :]
    left, right = cells[:, :, 0], cells[:, :, w - 1]
    pieces = jnp.stack([
        wide(top), wide(bottom), wide(left), wide(right),
        wide(top[:, :1]), wide(top[:, w - 1:]), wide(bottom[:, :1]), wide(bottom[:, w - 1:]),
    ])
    got = pl.pallas_call(
        functools.partial(_halo_kernel, nr, nc),
        out_shape=jax.ShapeDtypeStruct(pieces.shape, pieces.dtype),
        in_specs=[pl.BlockSpec(memory_space=pl.ANY)],
        out_specs=pl.BlockSpec(memory_space=pltpu.VMEM),
        scratch_shapes=[pltpu.SemaphoreType.DMA((8,)), pltpu.SemaphoreType.DMA((8,))],
        compiler_params=pltpu.CompilerParams(collective_id=1, has_side_effects=True),
    )(pieces)
    above = got[1, :, :w]
    below = got[0, :, :w]
    from_left = got[3, :, :h]
    from_right = got[2, :, :h]
    top_row = jnp.concatenate([got[7, :, :1], above, got[6, :, :1]], axis=1)
    bottom_row = jnp.concatenate([got[5, :, :1], below, got[4, :, :1]], axis=1)
    middle = jnp.concatenate([from_left[:, :, None], cells, from_right[:, :, None]], axis=2)
    return jnp.concatenate([top_row[:, None, :], middle, bottom_row[:, None, :]], axis=1)


def _sum_kernel(nr, nc, x_ref, o_ref, cpart, rpart, mine, sems, cs_send, cs_recv, r_send, r_recv, cg_send, cg_recv):
    my_r = lax.axis_index("rows")
    my_c = lax.axis_index("cols")

    def col_peer(j):
        return lax.rem(my_c + j, nc)

    def row_peer(j):
        return lax.rem(my_r + j, nr)

    barrier = pltpu.get_barrier_semaphore()

    def greet_c(j, c):
        pl.semaphore_signal(barrier, inc=1, device_id=(my_r, col_peer(j)), device_id_type=MESH)
        return c

    lax.fori_loop(1, nc, greet_c, 0)

    def greet_r(j, c):
        pl.semaphore_signal(barrier, inc=1, device_id=(row_peer(j), my_c), device_id_type=MESH)
        return c

    lax.fori_loop(1, nr, greet_r, 0)
    pl.semaphore_wait(barrier, nc + nr - 2)

    def c_scatter(p, s):
        return pltpu.make_async_remote_copy(
            src_ref=x_ref.at[p], dst_ref=cpart.at[s], send_sem=cs_send.at[p],
            recv_sem=cs_recv.at[s], device_id=(my_r, p), device_id_type=MESH)

    def start_cs(j, c):
        c_scatter(col_peer(j), my_c).start()
        return c

    lax.fori_loop(1, nc, start_cs, 0)
    cpart[my_c] = x_ref[my_c]

    def wait_cs(j, c):
        c_scatter(my_c, col_peer(j)).wait_recv()
        return c

    lax.fori_loop(1, nc, wait_cs, 0)
    mine[0] = lax.fori_loop(0, nc, lambda s, a: a + cpart[s], jnp.zeros(cpart.shape[1:], jnp.float32))
    own = pltpu.make_async_copy(mine.at[0], rpart.at[my_r], sems.at[0])
    own.start()
    own.wait()

    def r_share(q, s):
        return pltpu.make_async_remote_copy(
            src_ref=rpart.at[s], dst_ref=rpart.at[s], send_sem=r_send.at[q],
            recv_sem=r_recv.at[s], device_id=(q, my_c), device_id_type=MESH)

    def start_r(j, c):
        r_share(row_peer(j), my_r).start()
        return c

    lax.fori_loop(1, nr, start_r, 0)

    def wait_r(j, c):
        r_share(my_r, row_peer(j)).wait_recv()
        return c

    lax.fori_loop(1, nr, wait_r, 0)
    mine[1] = lax.fori_loop(0, nr, lambda s, a: a + rpart[s], jnp.zeros(rpart.shape[1:], jnp.float32))
    own = pltpu.make_async_copy(mine.at[1], o_ref.at[my_c], sems.at[1])
    own.start()
    own.wait()

    def c_gather(p, s):
        return pltpu.make_async_remote_copy(
            src_ref=o_ref.at[s], dst_ref=o_ref.at[s], send_sem=cg_send.at[p],
            recv_sem=cg_recv.at[s], device_id=(my_r, p), device_id_type=MESH)

    def start_cg(j, c):
        c_gather(col_peer(j), my_c).start()
        return c

    lax.fori_loop(1, nc, start_cg, 0)

    def wait_c(j, c):
        c_scatter(col_peer(j), my_c).wait_send()
        c_gather(my_c, col_peer(j)).wait_recv()
        c_gather(col_peer(j), my_c).wait_send()
        return c

    lax.fori_loop(1, nc, wait_c, 0)

    def wait_rs(j, c):
        r_share(row_peer(j), my_r).wait_send()
        return c

    lax.fori_loop(1, nr, wait_rs, 0)


def all_sum(vector, nr, nc):
    length = vector.shape[0]
    rows = -(-length // (nc * 128 * 8)) * 8
    blocks = jnp.pad(vector, (0, nc * rows * 128 - length)).reshape(nc, rows, 128)
    sem = pltpu.SemaphoreType.DMA
    out = pl.pallas_call(
        functools.partial(_sum_kernel, nr, nc),
        out_shape=jax.ShapeDtypeStruct(blocks.shape, jnp.float32),
        in_specs=[pl.BlockSpec(memory_space=pltpu.VMEM)],
        out_specs=pl.BlockSpec(memory_space=pltpu.VMEM),
        scratch_shapes=[
            pltpu.VMEM((nc, rows, 128), jnp.float32),
            pltpu.VMEM((nr, rows, 128), jnp.float32),
            pltpu.VMEM((2, rows, 128), jnp.float32),
            sem((2,)),
            sem((nc,)), sem((nc,)), sem((nr,)), sem((nr,)), sem((nc,)), sem((nc,)),
        ],
        compiler_params=pltpu.CompilerParams(collective_id=0, has_side_effects=True),
    )(blocks)
    return out.reshape(-1)[:length]


def padded_2(cells, sides, width):
    for axis, dim in sides:
        count = lax.axis_size(axis)
        ends = count - 1
        head = lax.slice_in_dim(cells, 0, width, axis=dim)
        tail = lax.slice_in_dim(cells, cells.shape[dim] - width, cells.shape[dim], axis=dim)
        cells = jnp.concatenate(
            [
                lax.ppermute(tail, axis, [(i, (i + 1) % count) for i in range(ends)]),
                cells,
                lax.ppermute(head, axis, [((i + 1) % count, i) for i in range(ends)]),
            ],
            axis=dim,
        )
    return cells


def pointwise(weight, field):
    return jnp.einsum("cm,chw->mhw", weight, field, preferred_element_type=jnp.float32)


def per_channel(vector):
    return vector[:, None, None]


def smooth_act(value):
    return value * jax.nn.sigmoid(value)


def smooth_slope(value):
    sigma = jax.nn.sigmoid(value)
    return sigma * (1.0 + value * (1.0 - sigma))


def spatial_conv(kernel, padded, height, breadth):
    result = jnp.zeros((kernel.shape[2], height, breadth), jnp.float32)
    for tap_row in range(3):
        for tap_col in range(3):
            window = padded[:, tap_row : tap_row + height, tap_col : tap_col + breadth]
            result = result + pointwise(kernel[3 * tap_row + tap_col], window)
    return result


def windows(padded, height, breadth, flip):
    taps = []
    for tap_row in range(3):
        for tap_col in range(3):
            i, j = (2 - tap_row, 2 - tap_col) if flip else (tap_row, tap_col)
            taps.append(padded[:, i : i + height, j : j + breadth])
    return jnp.concatenate(taps, axis=0)


def per_device(
    stem_out,
    tissue,
    w_first,
    w_reduce,
    w_mid,
    w_expand,
    w_short,
    gain_mid,
    shift_mid,
    gain_wide,
    shift_wide,
    upstream,
):
    height, breadth = (stem_out.shape[1], stem_out.shape[2])
    bands, tiles = tissue.shape
    values = tissue.astype(jnp.float32)[:, None, :, None]
    band_keep = jnp.broadcast_to(values, (bands, BLOCK, tiles, BLOCK)).reshape(
        bands * BLOCK, tiles * BLOCK
    )
    row_start = lax.axis_index("rows") * height
    tissue_keep = lax.dynamic_slice_in_dim(band_keep, row_start, height, 0)
    levels = w_mid.shape[0]
    saved_all = []
    feature = stem_out
    for block_index in range(levels):
        w_in = w_first if block_index == 0 else w_reduce[block_index - 1]
        pre_one = pointwise(w_in, feature)
        act_one = smooth_act(
            per_channel(gain_mid[block_index, 0]) * pre_one + per_channel(shift_mid[block_index, 0])
        ).astype(jnp.bfloat16)
        padded = exchange(act_one, lax.axis_size("rows"), lax.axis_size("cols"))
        stacked = windows(padded, height, breadth, False)
        pre_two = jnp.einsum(
            "km,khw->mhw", w_mid[block_index].reshape(-1, w_mid.shape[3]), stacked,
            preferred_element_type=jnp.float32,
        )
        act_two = smooth_act(
            per_channel(gain_mid[block_index, 1]) * pre_two + per_channel(shift_mid[block_index, 1])
        ).astype(jnp.bfloat16)
        pre_three = pointwise(w_expand[block_index], act_two)
        if block_index == 0:
            shortcut = pointwise(w_short, stem_out)
        else:
            shortcut = feature.astype(jnp.float32)
        summed = (
            per_channel(gain_wide[block_index]) * pre_three
            + per_channel(shift_wide[block_index])
            + shortcut
        )
        stored = stacked
        saved_all.append((feature, pre_one, stored, pre_two, act_two, pre_three, summed))
        feature = (smooth_act(summed) * tissue_keep).astype(jnp.bfloat16)
    gradient = upstream
    pieces = [None] * levels
    g_short = None
    for block_index in range(levels - 1, -1, -1):
        feature, pre_one, stored, pre_two, act_two, pre_three, summed = saved_all[block_index]
        w_in = w_first if block_index == 0 else w_reduce[block_index - 1]
        d_sum = gradient.astype(jnp.float32) * tissue_keep * smooth_slope(summed)
        d_gain3 = jnp.sum(d_sum * pre_three, axis=(1, 2))
        d_shift3 = jnp.sum(d_sum, axis=(1, 2))
        d_pre3 = (per_channel(gain_wide[block_index]) * d_sum).astype(jnp.bfloat16)
        g_expand = jnp.einsum("mhw,ohw->mo", act_two, d_pre3, preferred_element_type=jnp.float32)
        d_act2 = jnp.einsum(
            "mo,ohw->mhw", w_expand[block_index], d_pre3, preferred_element_type=jnp.float32
        )
        d_rel2 = d_act2 * smooth_slope(
            per_channel(gain_mid[block_index, 1]) * pre_two + per_channel(shift_mid[block_index, 1])
        )
        d_gain2 = jnp.sum(d_rel2 * pre_two, axis=(1, 2))
        d_shift2 = jnp.sum(d_rel2, axis=(1, 2))
        d_pre2 = (per_channel(gain_mid[block_index, 1]) * d_rel2).astype(jnp.bfloat16)
        g_mid = jnp.einsum(
            "khw,mhw->km", stored, d_pre2, preferred_element_type=jnp.float32
        ).reshape(w_mid.shape[1:])
        grad_pad = exchange(d_pre2, lax.axis_size("rows"), lax.axis_size("cols"))
        d_act1 = jnp.einsum(
            "km,khw->mhw",
            jnp.swapaxes(w_mid[block_index], 1, 2).reshape(-1, w_mid.shape[2]),
            windows(grad_pad, height, breadth, True),
            preferred_element_type=jnp.float32,
        )
        d_rel1 = d_act1 * smooth_slope(
            per_channel(gain_mid[block_index, 0]) * pre_one + per_channel(shift_mid[block_index, 0])
        )
        d_gain1 = jnp.sum(d_rel1 * pre_one, axis=(1, 2))
        d_shift1 = jnp.sum(d_rel1, axis=(1, 2))
        d_pre1 = (per_channel(gain_mid[block_index, 0]) * d_rel1).astype(jnp.bfloat16)
        g_in = jnp.einsum("chw,mhw->cm", feature, d_pre1, preferred_element_type=jnp.float32)
        d_feature = jnp.einsum("cm,mhw->chw", w_in, d_pre1, preferred_element_type=jnp.float32)
        if block_index == 0:
            d_short = d_sum.astype(jnp.bfloat16)
            g_short = jnp.einsum(
                "chw,ohw->co", feature, d_short, preferred_element_type=jnp.float32
            )
            d_feature = d_feature + jnp.einsum(
                "co,ohw->chw", w_short, d_short, preferred_element_type=jnp.float32
            )
        else:
            d_feature = d_feature + d_sum
        gradient = d_feature.astype(jnp.bfloat16)
        pieces[block_index] = [
            g_in,
            g_mid,
            g_expand,
            d_gain1,
            d_shift1,
            d_gain2,
            d_shift2,
            d_gain3,
            d_shift3,
        ]
    flat = []
    for block_index in range(levels):
        for piece in pieces[block_index]:
            flat.append(piece.reshape(-1))
    flat.append(g_short.reshape(-1))
    partial_vector = jnp.concatenate(flat)
    totals = all_sum(partial_vector, lax.axis_size("rows"), lax.axis_size("cols"))
    pixel_count = height * breadth * lax.axis_size("rows") * lax.axis_size("cols")
    scale = 1.0 / jnp.sqrt(jnp.float32(pixel_count))
    return (gradient, totals * scale)


def solution(mesh):
    in_specs = (
        P(None, "rows", "cols"),
        P(None, "cols"),
        P(),
        P(),
        P(),
        P(),
        P(),
        P(),
        P(),
        P(),
        P(),
        P(None, "rows", "cols"),
    )
    out_specs = (P(None, "rows", "cols"), P())
    return jax.shard_map(
        per_device, mesh=mesh, in_specs=in_specs, out_specs=out_specs, check_vma=False
    )
```

```python
import functools
import jax
import jax.numpy as jnp
from jax import lax
from jax.experimental import pallas as pl
from jax.experimental.pallas import tpu as pltpu
from jax.sharding import PartitionSpec as P

MESH = pl.DeviceIdType.MESH

BLOCK = 64


_TOWARD = ((-1, 0), (1, 0), (0, -1), (0, 1), (-1, -1), (-1, 1), (1, -1), (1, 1))
_FIRST_FAR = (4, 5, 6, 7, 0, 1, 2, 3)


def _halo_kernel(nr, nc, e_ref, o_ref, send_sem, recv_sem):
    my_r = lax.axis_index("rows")
    my_c = lax.axis_index("cols")

    def present(dr, dc):
        ok = True
        if dr:
            ok = jnp.logical_and(ok, jnp.logical_and(my_r + dr >= 0, my_r + dr < nr))
        if dc:
            ok = jnp.logical_and(ok, jnp.logical_and(my_c + dc >= 0, my_c + dc < nc))
        return ok

    barrier = pltpu.get_barrier_semaphore()
    count = 0
    for dr, dc in _TOWARD[4:] + _TOWARD[:4]:
        there = present(dr, dc)
        count = count + there.astype(jnp.int32)

        @pl.when(there)
        def _():
            pl.semaphore_signal(barrier, inc=1, device_id=(my_r + dr, my_c + dc), device_id_type=MESH)

    pl.semaphore_wait(barrier, count)

    def copy(k, dr, dc):
        return pltpu.make_async_remote_copy(
            src_ref=e_ref.at[k], dst_ref=o_ref.at[k], send_sem=send_sem.at[k],
            recv_sem=recv_sem.at[k], device_id=(my_r + dr, my_c + dc), device_id_type=MESH)

    for k in _FIRST_FAR:
        dr, dc = _TOWARD[k]

        @pl.when(present(dr, dc))
        def _():
            copy(k, dr, dc).start()

        @pl.when(jnp.logical_not(present(-dr, -dc)))
        def _():
            o_ref[k] = jnp.zeros(o_ref.shape[1:], o_ref.dtype)

    for k, (dr, dc) in enumerate(_TOWARD):
        @pl.when(present(-dr, -dc))
        def _():
            copy(k, -dr, -dc).wait_recv()

        @pl.when(present(dr, dc))
        def _():
            copy(k, dr, dc).wait_send()


def exchange(cells, nr, nc):
    ch, h, w = cells.shape
    lanes = max(w, -(-h // 128) * 128)

    def wide(v):
        return jnp.pad(v, ((0, 0), (0, lanes - v.shape[1])))

    top, bottom = cells[:, 0, :], cells[:, h - 1, :]
    left, right = cells[:, :, 0], cells[:, :, w - 1]
    pieces = jnp.stack([
        wide(top), wide(bottom), wide(left), wide(right),
        wide(top[:, :1]), wide(top[:, w - 1:]), wide(bottom[:, :1]), wide(bottom[:, w - 1:]),
    ])
    got = pl.pallas_call(
        functools.partial(_halo_kernel, nr, nc),
        out_shape=jax.ShapeDtypeStruct(pieces.shape, pieces.dtype),
        in_specs=[pl.BlockSpec(memory_space=pl.ANY)],
        out_specs=pl.BlockSpec(memory_space=pltpu.VMEM),
        scratch_shapes=[pltpu.SemaphoreType.DMA((8,)), pltpu.SemaphoreType.DMA((8,))],
        compiler_params=pltpu.CompilerParams(collective_id=1, has_side_effects=True),
    )(pieces)
    above = got[1, :, :w]
    below = got[0, :, :w]
    from_left = got[3, :, :h]
    from_right = got[2, :, :h]
    top_row = jnp.concatenate([got[7, :, :1], above, got[6, :, :1]], axis=1)
    bottom_row = jnp.concatenate([got[5, :, :1], below, got[4, :, :1]], axis=1)
    middle = jnp.concatenate([from_left[:, :, None], cells, from_right[:, :, None]], axis=2)
    return jnp.concatenate([top_row[:, None, :], middle, bottom_row[:, None, :]], axis=1)


def _sum_kernel(nr, nc, x_ref, o_ref, cpart, rpart, mine, sems, cs_send, cs_recv, r_send, r_recv, cg_send, cg_recv):
    my_r = lax.axis_index("rows")
    my_c = lax.axis_index("cols")

    def col_peer(j):
        return lax.rem(my_c + j, nc)

    def row_peer(j):
        return lax.rem(my_r + j, nr)

    barrier = pltpu.get_barrier_semaphore()

    def greet_c(j, c):
        pl.semaphore_signal(barrier, inc=1, device_id=(my_r, col_peer(j)), device_id_type=MESH)
        return c

    lax.fori_loop(1, nc, greet_c, 0)

    def greet_r(j, c):
        pl.semaphore_signal(barrier, inc=1, device_id=(row_peer(j), my_c), device_id_type=MESH)
        return c

    lax.fori_loop(1, nr, greet_r, 0)
    pl.semaphore_wait(barrier, nc + nr - 2)

    def c_scatter(p, s):
        return pltpu.make_async_remote_copy(
            src_ref=x_ref.at[p], dst_ref=cpart.at[s], send_sem=cs_send.at[p],
            recv_sem=cs_recv.at[s], device_id=(my_r, p), device_id_type=MESH)

    def start_cs(j, c):
        c_scatter(col_peer(j), my_c).start()
        return c

    lax.fori_loop(1, nc, start_cs, 0)
    mine_in = pltpu.make_async_copy(x_ref.at[my_c], cpart.at[my_c], sems.at[0])
    mine_in.start()
    mine_in.wait()

    def wait_cs(j, c):
        c_scatter(my_c, col_peer(j)).wait_recv()
        return c

    lax.fori_loop(1, nc, wait_cs, 0)
    mine[0] = lax.fori_loop(0, nc, lambda s, a: a + cpart[s], jnp.zeros(cpart.shape[1:], jnp.float32))
    own = pltpu.make_async_copy(mine.at[0], rpart.at[my_r], sems.at[0])
    own.start()
    own.wait()

    def r_share(q, s):
        return pltpu.make_async_remote_copy(
            src_ref=rpart.at[s], dst_ref=rpart.at[s], send_sem=r_send.at[q],
            recv_sem=r_recv.at[s], device_id=(q, my_c), device_id_type=MESH)

    def start_r(j, c):
        r_share(row_peer(j), my_r).start()
        return c

    lax.fori_loop(1, nr, start_r, 0)

    def wait_r(j, c):
        r_share(my_r, row_peer(j)).wait_recv()
        return c

    lax.fori_loop(1, nr, wait_r, 0)
    mine[1] = lax.fori_loop(0, nr, lambda s, a: a + rpart[s], jnp.zeros(rpart.shape[1:], jnp.float32))
    own = pltpu.make_async_copy(mine.at[1], o_ref.at[my_c], sems.at[1])
    own.start()
    own.wait()

    def c_gather(p, s):
        return pltpu.make_async_remote_copy(
            src_ref=o_ref.at[s], dst_ref=o_ref.at[s], send_sem=cg_send.at[p],
            recv_sem=cg_recv.at[s], device_id=(my_r, p), device_id_type=MESH)

    def start_cg(j, c):
        c_gather(col_peer(j), my_c).start()
        return c

    lax.fori_loop(1, nc, start_cg, 0)

    def wait_c(j, c):
        c_scatter(col_peer(j), my_c).wait_send()
        c_gather(my_c, col_peer(j)).wait_recv()
        c_gather(col_peer(j), my_c).wait_send()
        return c

    lax.fori_loop(1, nc, wait_c, 0)

    def wait_rs(j, c):
        r_share(row_peer(j), my_r).wait_send()
        return c

    lax.fori_loop(1, nr, wait_rs, 0)


def all_sum(vector, nr, nc):
    length = vector.shape[0]
    rows = -(-length // (nc * 128 * 8)) * 8
    blocks = jnp.pad(vector, (0, nc * rows * 128 - length)).reshape(nc, rows, 128)
    sem = pltpu.SemaphoreType.DMA
    out = pl.pallas_call(
        functools.partial(_sum_kernel, nr, nc),
        out_shape=jax.ShapeDtypeStruct(blocks.shape, jnp.float32),
        in_specs=[pl.BlockSpec(memory_space=pl.ANY)],
        out_specs=pl.BlockSpec(memory_space=pltpu.VMEM),
        scratch_shapes=[
            pltpu.VMEM((nc, rows, 128), jnp.float32),
            pltpu.VMEM((nr, rows, 128), jnp.float32),
            pltpu.VMEM((2, rows, 128), jnp.float32),
            sem((2,)),
            sem((nc,)), sem((nc,)), sem((nr,)), sem((nr,)), sem((nc,)), sem((nc,)),
        ],
        compiler_params=pltpu.CompilerParams(collective_id=0, has_side_effects=True),
    )(blocks)
    return out.reshape(-1)[:length]


def padded_2(cells, sides, width):
    for axis, dim in sides:
        count = lax.axis_size(axis)
        ends = count - 1
        head = lax.slice_in_dim(cells, 0, width, axis=dim)
        tail = lax.slice_in_dim(cells, cells.shape[dim] - width, cells.shape[dim], axis=dim)
        cells = jnp.concatenate(
            [
                lax.ppermute(tail, axis, [(i, (i + 1) % count) for i in range(ends)]),
                cells,
                lax.ppermute(head, axis, [((i + 1) % count, i) for i in range(ends)]),
            ],
            axis=dim,
        )
    return cells


def pointwise(weight, field):
    return jnp.einsum("cm,chw->mhw", weight, field, preferred_element_type=jnp.float32)


def per_channel(vector):
    return vector[:, None, None]


def smooth_act(value):
    return value * jax.nn.sigmoid(value)


def smooth_slope(value):
    sigma = jax.nn.sigmoid(value)
    return sigma * (1.0 + value * (1.0 - sigma))


def spatial_conv(kernel, padded, height, breadth):
    result = jnp.zeros((kernel.shape[2], height, breadth), jnp.float32)
    for tap_row in range(3):
        for tap_col in range(3):
            window = padded[:, tap_row : tap_row + height, tap_col : tap_col + breadth]
            result = result + pointwise(kernel[3 * tap_row + tap_col], window)
    return result


def windows(padded, height, breadth, flip):
    taps = []
    for tap_row in range(3):
        for tap_col in range(3):
            i, j = (2 - tap_row, 2 - tap_col) if flip else (tap_row, tap_col)
            taps.append(padded[:, i : i + height, j : j + breadth])
    return jnp.concatenate(taps, axis=0)


def per_device(
    stem_out,
    tissue,
    w_first,
    w_reduce,
    w_mid,
    w_expand,
    w_short,
    gain_mid,
    shift_mid,
    gain_wide,
    shift_wide,
    upstream,
):
    height, breadth = (stem_out.shape[1], stem_out.shape[2])
    bands, tiles = tissue.shape
    values = tissue.astype(jnp.float32)[:, None, :, None]
    band_keep = jnp.broadcast_to(values, (bands, BLOCK, tiles, BLOCK)).reshape(
        bands * BLOCK, tiles * BLOCK
    )
    row_start = lax.axis_index("rows") * height
    tissue_keep = lax.dynamic_slice_in_dim(band_keep, row_start, height, 0)
    levels = w_mid.shape[0]
    saved_all = []
    feature = stem_out
    for block_index in range(levels):
        w_in = w_first if block_index == 0 else w_reduce[block_index - 1]
        pre_one = pointwise(w_in, feature)
        act_one = smooth_act(
            per_channel(gain_mid[block_index, 0]) * pre_one + per_channel(shift_mid[block_index, 0])
        ).astype(jnp.bfloat16)
        padded = exchange(act_one, lax.axis_size("rows"), lax.axis_size("cols"))
        stacked = windows(padded, height, breadth, False)
        pre_two = jnp.einsum(
            "km,khw->mhw", w_mid[block_index].reshape(-1, w_mid.shape[3]), stacked,
            preferred_element_type=jnp.float32,
        )
        act_two = smooth_act(
            per_channel(gain_mid[block_index, 1]) * pre_two + per_channel(shift_mid[block_index, 1])
        ).astype(jnp.bfloat16)
        pre_three = pointwise(w_expand[block_index], act_two)
        if block_index == 0:
            shortcut = pointwise(w_short, stem_out)
        else:
            shortcut = feature.astype(jnp.float32)
        summed = (
            per_channel(gain_wide[block_index]) * pre_three
            + per_channel(shift_wide[block_index])
            + shortcut
        )
        stored = stacked
        saved_all.append((feature, pre_one, stored, pre_two, act_two, pre_three, summed))
        feature = (smooth_act(summed) * tissue_keep).astype(jnp.bfloat16)
    gradient = upstream
    pieces = [None] * levels
    g_short = None
    for block_index in range(levels - 1, -1, -1):
        feature, pre_one, stored, pre_two, act_two, pre_three, summed = saved_all[block_index]
        w_in = w_first if block_index == 0 else w_reduce[block_index - 1]
        d_sum = gradient.astype(jnp.float32) * tissue_keep * smooth_slope(summed)
        d_gain3 = jnp.sum(d_sum * pre_three, axis=(1, 2))
        d_shift3 = jnp.sum(d_sum, axis=(1, 2))
        d_pre3 = (per_channel(gain_wide[block_index]) * d_sum).astype(jnp.bfloat16)
        g_expand = jnp.einsum("mhw,ohw->mo", act_two, d_pre3, preferred_element_type=jnp.float32)
        d_act2 = jnp.einsum(
            "mo,ohw->mhw", w_expand[block_index], d_pre3, preferred_element_type=jnp.float32
        )
        d_rel2 = d_act2 * smooth_slope(
            per_channel(gain_mid[block_index, 1]) * pre_two + per_channel(shift_mid[block_index, 1])
        )
        d_gain2 = jnp.sum(d_rel2 * pre_two, axis=(1, 2))
        d_shift2 = jnp.sum(d_rel2, axis=(1, 2))
        d_pre2 = (per_channel(gain_mid[block_index, 1]) * d_rel2).astype(jnp.bfloat16)
        g_mid = jnp.einsum(
            "khw,mhw->km", stored, d_pre2, preferred_element_type=jnp.float32
        ).reshape(w_mid.shape[1:])
        grad_pad = exchange(d_pre2, lax.axis_size("rows"), lax.axis_size("cols"))
        d_act1 = jnp.einsum(
            "km,khw->mhw",
            jnp.swapaxes(w_mid[block_index], 1, 2).reshape(-1, w_mid.shape[2]),
            windows(grad_pad, height, breadth, True),
            preferred_element_type=jnp.float32,
        )
        d_rel1 = d_act1 * smooth_slope(
            per_channel(gain_mid[block_index, 0]) * pre_one + per_channel(shift_mid[block_index, 0])
        )
        d_gain1 = jnp.sum(d_rel1 * pre_one, axis=(1, 2))
        d_shift1 = jnp.sum(d_rel1, axis=(1, 2))
        d_pre1 = (per_channel(gain_mid[block_index, 0]) * d_rel1).astype(jnp.bfloat16)
        g_in = jnp.einsum("chw,mhw->cm", feature, d_pre1, preferred_element_type=jnp.float32)
        d_feature = jnp.einsum("cm,mhw->chw", w_in, d_pre1, preferred_element_type=jnp.float32)
        if block_index == 0:
            d_short = d_sum.astype(jnp.bfloat16)
            g_short = jnp.einsum(
                "chw,ohw->co", feature, d_short, preferred_element_type=jnp.float32
            )
            d_feature = d_feature + jnp.einsum(
                "co,ohw->chw", w_short, d_short, preferred_element_type=jnp.float32
            )
        else:
            d_feature = d_feature + d_sum
        gradient = d_feature.astype(jnp.bfloat16)
        pieces[block_index] = [
            g_in,
            g_mid,
            g_expand,
            d_gain1,
            d_shift1,
            d_gain2,
            d_shift2,
            d_gain3,
            d_shift3,
        ]
    flat = []
    for block_index in range(levels):
        for piece in pieces[block_index]:
            flat.append(piece.reshape(-1))
    flat.append(g_short.reshape(-1))
    partial_vector = jnp.concatenate(flat)
    totals = all_sum(partial_vector, lax.axis_size("rows"), lax.axis_size("cols"))
    pixel_count = height * breadth * lax.axis_size("rows") * lax.axis_size("cols")
    scale = 1.0 / jnp.sqrt(jnp.float32(pixel_count))
    return (gradient, totals * scale)


def solution(mesh):
    in_specs = (
        P(None, "rows", "cols"),
        P(None, "cols"),
        P(),
        P(),
        P(),
        P(),
        P(),
        P(),
        P(),
        P(),
        P(),
        P(None, "rows", "cols"),
    )
    out_specs = (P(None, "rows", "cols"), P())
    return jax.shard_map(
        per_device, mesh=mesh, in_specs=in_specs, out_specs=out_specs, check_vma=False
    )
```

```python
import functools
import jax
import jax.numpy as jnp
from jax import lax
from jax.experimental import pallas as pl
from jax.experimental.pallas import tpu as pltpu
from jax.sharding import PartitionSpec as P

MESH = pl.DeviceIdType.MESH

BLOCK = 64


_TOWARD = ((-1, 0), (1, 0), (0, -1), (0, 1), (-1, -1), (-1, 1), (1, -1), (1, 1))
_FIRST_FAR = (4, 5, 6, 7, 0, 1, 2, 3)


def _halo_kernel(nr, nc, e_ref, zero_ref, o_ref, send_sem, recv_sem, zero_sem):
    my_r = lax.axis_index("rows")
    my_c = lax.axis_index("cols")

    def present(dr, dc):
        ok = True
        if dr:
            ok = jnp.logical_and(ok, jnp.logical_and(my_r + dr >= 0, my_r + dr < nr))
        if dc:
            ok = jnp.logical_and(ok, jnp.logical_and(my_c + dc >= 0, my_c + dc < nc))
        return ok

    barrier = pltpu.get_barrier_semaphore()
    count = 0
    for dr, dc in _TOWARD[4:] + _TOWARD[:4]:
        there = present(dr, dc)
        count = count + there.astype(jnp.int32)

        @pl.when(there)
        def _():
            pl.semaphore_signal(barrier, inc=1, device_id=(my_r + dr, my_c + dc), device_id_type=MESH)

    pl.semaphore_wait(barrier, count)

    def copy(k, dr, dc):
        return pltpu.make_async_remote_copy(
            src_ref=e_ref.at[k], dst_ref=o_ref.at[k], send_sem=send_sem.at[k],
            recv_sem=recv_sem.at[k], device_id=(my_r + dr, my_c + dc), device_id_type=MESH)

    for k in _FIRST_FAR:
        dr, dc = _TOWARD[k]

        @pl.when(present(dr, dc))
        def _():
            copy(k, dr, dc).start()

        @pl.when(jnp.logical_not(present(-dr, -dc)))
        def _():
            pltpu.make_async_copy(zero_ref, o_ref.at[k], zero_sem.at[k]).start()

    for k, (dr, dc) in enumerate(_TOWARD):
        @pl.when(present(-dr, -dc))
        def _():
            copy(k, -dr, -dc).wait_recv()

        @pl.when(jnp.logical_not(present(-dr, -dc)))
        def _():
            pltpu.make_async_copy(zero_ref, o_ref.at[k], zero_sem.at[k]).wait()

        @pl.when(present(dr, dc))
        def _():
            copy(k, dr, dc).wait_send()


def exchange(cells, nr, nc):
    ch, h, w = cells.shape
    lanes = max(w, -(-h // 128) * 128)

    def wide(v):
        return jnp.pad(v, ((0, 0), (0, lanes - v.shape[1])))

    top, bottom = cells[:, 0, :], cells[:, h - 1, :]
    left, right = cells[:, :, 0], cells[:, :, w - 1]
    pieces = jnp.stack([
        wide(top), wide(bottom), wide(left), wide(right),
        wide(top[:, :1]), wide(top[:, w - 1:]), wide(bottom[:, :1]), wide(bottom[:, w - 1:]),
    ])
    got = pl.pallas_call(
        functools.partial(_halo_kernel, nr, nc),
        out_shape=jax.ShapeDtypeStruct(pieces.shape, pieces.dtype),
        in_specs=[pl.BlockSpec(memory_space=pl.ANY)] * 2,
        out_specs=pl.BlockSpec(memory_space=pl.ANY),
        scratch_shapes=[pltpu.SemaphoreType.DMA((8,))] * 3,
        compiler_params=pltpu.CompilerParams(collective_id=1, has_side_effects=True),
    )(pieces, jnp.zeros(pieces.shape[1:], pieces.dtype))
    above = got[1, :, :w]
    below = got[0, :, :w]
    from_left = got[3, :, :h]
    from_right = got[2, :, :h]
    top_row = jnp.concatenate([got[7, :, :1], above, got[6, :, :1]], axis=1)
    bottom_row = jnp.concatenate([got[5, :, :1], below, got[4, :, :1]], axis=1)
    middle = jnp.concatenate([from_left[:, :, None], cells, from_right[:, :, None]], axis=2)
    return jnp.concatenate([top_row[:, None, :], middle, bottom_row[:, None, :]], axis=1)


def _sum_kernel(nr, nc, x_ref, o_ref, cpart, rpart, mine, sems, cs_send, cs_recv, r_send, r_recv, cg_send, cg_recv):
    my_r = lax.axis_index("rows")
    my_c = lax.axis_index("cols")

    def col_peer(j):
        return lax.rem(my_c + j, nc)

    def row_peer(j):
        return lax.rem(my_r + j, nr)

    barrier = pltpu.get_barrier_semaphore()

    def greet_c(j, c):
        pl.semaphore_signal(barrier, inc=1, device_id=(my_r, col_peer(j)), device_id_type=MESH)
        return c

    lax.fori_loop(1, nc, greet_c, 0)

    def greet_r(j, c):
        pl.semaphore_signal(barrier, inc=1, device_id=(row_peer(j), my_c), device_id_type=MESH)
        return c

    lax.fori_loop(1, nr, greet_r, 0)
    pl.semaphore_wait(barrier, nc + nr - 2)

    def c_scatter(p, s):
        return pltpu.make_async_remote_copy(
            src_ref=x_ref.at[p], dst_ref=cpart.at[s], send_sem=cs_send.at[p],
            recv_sem=cs_recv.at[s], device_id=(my_r, p), device_id_type=MESH)

    def start_cs(j, c):
        c_scatter(col_peer(j), my_c).start()
        return c

    lax.fori_loop(1, nc, start_cs, 0)
    mine_in = pltpu.make_async_copy(x_ref.at[my_c], cpart.at[my_c], sems.at[0])
    mine_in.start()
    mine_in.wait()

    def wait_cs(j, c):
        c_scatter(my_c, col_peer(j)).wait_recv()
        return c

    lax.fori_loop(1, nc, wait_cs, 0)
    mine[0] = lax.fori_loop(0, nc, lambda s, a: a + cpart[s], jnp.zeros(cpart.shape[1:], jnp.float32))
    own = pltpu.make_async_copy(mine.at[0], rpart.at[my_r], sems.at[0])
    own.start()
    own.wait()

    def r_share(q, s):
        return pltpu.make_async_remote_copy(
            src_ref=rpart.at[s], dst_ref=rpart.at[s], send_sem=r_send.at[q],
            recv_sem=r_recv.at[s], device_id=(q, my_c), device_id_type=MESH)

    def start_r(j, c):
        r_share(row_peer(j), my_r).start()
        return c

    lax.fori_loop(1, nr, start_r, 0)

    def wait_r(j, c):
        r_share(my_r, row_peer(j)).wait_recv()
        return c

    lax.fori_loop(1, nr, wait_r, 0)
    mine[1] = lax.fori_loop(0, nr, lambda s, a: a + rpart[s], jnp.zeros(rpart.shape[1:], jnp.float32))
    own = pltpu.make_async_copy(mine.at[1], o_ref.at[my_c], sems.at[1])
    own.start()
    own.wait()

    def c_gather(p, s):
        return pltpu.make_async_remote_copy(
            src_ref=o_ref.at[s], dst_ref=o_ref.at[s], send_sem=cg_send.at[p],
            recv_sem=cg_recv.at[s], device_id=(my_r, p), device_id_type=MESH)

    def start_cg(j, c):
        c_gather(col_peer(j), my_c).start()
        return c

    lax.fori_loop(1, nc, start_cg, 0)

    def wait_c(j, c):
        c_scatter(col_peer(j), my_c).wait_send()
        c_gather(my_c, col_peer(j)).wait_recv()
        c_gather(col_peer(j), my_c).wait_send()
        return c

    lax.fori_loop(1, nc, wait_c, 0)

    def wait_rs(j, c):
        r_share(row_peer(j), my_r).wait_send()
        return c

    lax.fori_loop(1, nr, wait_rs, 0)


def all_sum(vector, nr, nc):
    length = vector.shape[0]
    rows = -(-length // (nc * 128 * 8)) * 8
    blocks = jnp.pad(vector, (0, nc * rows * 128 - length)).reshape(nc, rows, 128)
    sem = pltpu.SemaphoreType.DMA
    out = pl.pallas_call(
        functools.partial(_sum_kernel, nr, nc),
        out_shape=jax.ShapeDtypeStruct(blocks.shape, jnp.float32),
        in_specs=[pl.BlockSpec(memory_space=pl.ANY)],
        out_specs=pl.BlockSpec(memory_space=pltpu.VMEM),
        scratch_shapes=[
            pltpu.VMEM((nc, rows, 128), jnp.float32),
            pltpu.VMEM((nr, rows, 128), jnp.float32),
            pltpu.VMEM((2, rows, 128), jnp.float32),
            sem((2,)),
            sem((nc,)), sem((nc,)), sem((nr,)), sem((nr,)), sem((nc,)), sem((nc,)),
        ],
        compiler_params=pltpu.CompilerParams(collective_id=0, has_side_effects=True),
    )(blocks)
    return out.reshape(-1)[:length]


def padded_2(cells, sides, width):
    for axis, dim in sides:
        count = lax.axis_size(axis)
        ends = count - 1
        head = lax.slice_in_dim(cells, 0, width, axis=dim)
        tail = lax.slice_in_dim(cells, cells.shape[dim] - width, cells.shape[dim], axis=dim)
        cells = jnp.concatenate(
            [
                lax.ppermute(tail, axis, [(i, (i + 1) % count) for i in range(ends)]),
                cells,
                lax.ppermute(head, axis, [((i + 1) % count, i) for i in range(ends)]),
            ],
            axis=dim,
        )
    return cells


def pointwise(weight, field):
    return jnp.einsum("cm,chw->mhw", weight, field, preferred_element_type=jnp.float32)


def per_channel(vector):
    return vector[:, None, None]


def smooth_act(value):
    return value * jax.nn.sigmoid(value)


def smooth_slope(value):
    sigma = jax.nn.sigmoid(value)
    return sigma * (1.0 + value * (1.0 - sigma))


def spatial_conv(kernel, padded, height, breadth):
    result = jnp.zeros((kernel.shape[2], height, breadth), jnp.float32)
    for tap_row in range(3):
        for tap_col in range(3):
            window = padded[:, tap_row : tap_row + height, tap_col : tap_col + breadth]
            result = result + pointwise(kernel[3 * tap_row + tap_col], window)
    return result


def windows(padded, height, breadth, flip):
    taps = []
    for tap_row in range(3):
        for tap_col in range(3):
            i, j = (2 - tap_row, 2 - tap_col) if flip else (tap_row, tap_col)
            taps.append(padded[:, i : i + height, j : j + breadth])
    return jnp.concatenate(taps, axis=0)


def per_device(
    stem_out,
    tissue,
    w_first,
    w_reduce,
    w_mid,
    w_expand,
    w_short,
    gain_mid,
    shift_mid,
    gain_wide,
    shift_wide,
    upstream,
):
    height, breadth = (stem_out.shape[1], stem_out.shape[2])
    bands, tiles = tissue.shape
    values = tissue.astype(jnp.float32)[:, None, :, None]
    band_keep = jnp.broadcast_to(values, (bands, BLOCK, tiles, BLOCK)).reshape(
        bands * BLOCK, tiles * BLOCK
    )
    row_start = lax.axis_index("rows") * height
    tissue_keep = lax.dynamic_slice_in_dim(band_keep, row_start, height, 0)
    levels = w_mid.shape[0]
    saved_all = []
    feature = stem_out
    for block_index in range(levels):
        w_in = w_first if block_index == 0 else w_reduce[block_index - 1]
        pre_one = pointwise(w_in, feature)
        act_one = smooth_act(
            per_channel(gain_mid[block_index, 0]) * pre_one + per_channel(shift_mid[block_index, 0])
        ).astype(jnp.bfloat16)
        padded = exchange(act_one, lax.axis_size("rows"), lax.axis_size("cols"))
        stacked = windows(padded, height, breadth, False)
        pre_two = jnp.einsum(
            "km,khw->mhw", w_mid[block_index].reshape(-1, w_mid.shape[3]), stacked,
            preferred_element_type=jnp.float32,
        )
        act_two = smooth_act(
            per_channel(gain_mid[block_index, 1]) * pre_two + per_channel(shift_mid[block_index, 1])
        ).astype(jnp.bfloat16)
        pre_three = pointwise(w_expand[block_index], act_two)
        if block_index == 0:
            shortcut = pointwise(w_short, stem_out)
        else:
            shortcut = feature.astype(jnp.float32)
        summed = (
            per_channel(gain_wide[block_index]) * pre_three
            + per_channel(shift_wide[block_index])
            + shortcut
        )
        stored = stacked
        saved_all.append((feature, pre_one, stored, pre_two, act_two, pre_three, summed))
        feature = (smooth_act(summed) * tissue_keep).astype(jnp.bfloat16)
    gradient = upstream
    pieces = [None] * levels
    g_short = None
    for block_index in range(levels - 1, -1, -1):
        feature, pre_one, stored, pre_two, act_two, pre_three, summed = saved_all[block_index]
        w_in = w_first if block_index == 0 else w_reduce[block_index - 1]
        d_sum = gradient.astype(jnp.float32) * tissue_keep * smooth_slope(summed)
        d_gain3 = jnp.sum(d_sum * pre_three, axis=(1, 2))
        d_shift3 = jnp.sum(d_sum, axis=(1, 2))
        d_pre3 = (per_channel(gain_wide[block_index]) * d_sum).astype(jnp.bfloat16)
        g_expand = jnp.einsum("mhw,ohw->mo", act_two, d_pre3, preferred_element_type=jnp.float32)
        d_act2 = jnp.einsum(
            "mo,ohw->mhw", w_expand[block_index], d_pre3, preferred_element_type=jnp.float32
        )
        d_rel2 = d_act2 * smooth_slope(
            per_channel(gain_mid[block_index, 1]) * pre_two + per_channel(shift_mid[block_index, 1])
        )
        d_gain2 = jnp.sum(d_rel2 * pre_two, axis=(1, 2))
        d_shift2 = jnp.sum(d_rel2, axis=(1, 2))
        d_pre2 = (per_channel(gain_mid[block_index, 1]) * d_rel2).astype(jnp.bfloat16)
        g_mid = jnp.einsum(
            "khw,mhw->km", stored, d_pre2, preferred_element_type=jnp.float32
        ).reshape(w_mid.shape[1:])
        grad_pad = exchange(d_pre2, lax.axis_size("rows"), lax.axis_size("cols"))
        d_act1 = jnp.einsum(
            "km,khw->mhw",
            jnp.swapaxes(w_mid[block_index], 1, 2).reshape(-1, w_mid.shape[2]),
            windows(grad_pad, height, breadth, True),
            preferred_element_type=jnp.float32,
        )
        d_rel1 = d_act1 * smooth_slope(
            per_channel(gain_mid[block_index, 0]) * pre_one + per_channel(shift_mid[block_index, 0])
        )
        d_gain1 = jnp.sum(d_rel1 * pre_one, axis=(1, 2))
        d_shift1 = jnp.sum(d_rel1, axis=(1, 2))
        d_pre1 = (per_channel(gain_mid[block_index, 0]) * d_rel1).astype(jnp.bfloat16)
        g_in = jnp.einsum("chw,mhw->cm", feature, d_pre1, preferred_element_type=jnp.float32)
        d_feature = jnp.einsum("cm,mhw->chw", w_in, d_pre1, preferred_element_type=jnp.float32)
        if block_index == 0:
            d_short = d_sum.astype(jnp.bfloat16)
            g_short = jnp.einsum(
                "chw,ohw->co", feature, d_short, preferred_element_type=jnp.float32
            )
            d_feature = d_feature + jnp.einsum(
                "co,ohw->chw", w_short, d_short, preferred_element_type=jnp.float32
            )
        else:
            d_feature = d_feature + d_sum
        gradient = d_feature.astype(jnp.bfloat16)
        pieces[block_index] = [
            g_in,
            g_mid,
            g_expand,
            d_gain1,
            d_shift1,
            d_gain2,
            d_shift2,
            d_gain3,
            d_shift3,
        ]
    flat = []
    for block_index in range(levels):
        for piece in pieces[block_index]:
            flat.append(piece.reshape(-1))
    flat.append(g_short.reshape(-1))
    partial_vector = jnp.concatenate(flat)
    totals = all_sum(partial_vector, lax.axis_size("rows"), lax.axis_size("cols"))
    pixel_count = height * breadth * lax.axis_size("rows") * lax.axis_size("cols")
    scale = 1.0 / jnp.sqrt(jnp.float32(pixel_count))
    return (gradient, totals * scale)


def solution(mesh):
    in_specs = (
        P(None, "rows", "cols"),
        P(None, "cols"),
        P(),
        P(),
        P(),
        P(),
        P(),
        P(),
        P(),
        P(),
        P(),
        P(None, "rows", "cols"),
    )
    out_specs = (P(None, "rows", "cols"), P())
    return jax.shard_map(
        per_device, mesh=mesh, in_specs=in_specs, out_specs=out_specs, check_vma=False
    )
```

```python
import functools
import jax
import jax.numpy as jnp
from jax import lax
from jax.experimental import pallas as pl
from jax.experimental.pallas import tpu as pltpu
from jax.sharding import PartitionSpec as P

MESH = pl.DeviceIdType.MESH

BLOCK = 64


_TOWARD = ((-1, 0), (1, 0), (0, -1), (0, 1), (-1, -1), (-1, 1), (1, -1), (1, 1))
_FIRST_FAR = (4, 5, 6, 7, 0, 1, 2, 3)


def _halo_kernel(nr, nc, e_ref, zero_ref, o_ref, send_sem, recv_sem, zero_sem):
    my_r = lax.axis_index("rows")
    my_c = lax.axis_index("cols")

    def present(dr, dc):
        ok = True
        if dr:
            ok = jnp.logical_and(ok, jnp.logical_and(my_r + dr >= 0, my_r + dr < nr))
        if dc:
            ok = jnp.logical_and(ok, jnp.logical_and(my_c + dc >= 0, my_c + dc < nc))
        return ok

    barrier = pltpu.get_barrier_semaphore()
    count = 0
    for dr, dc in _TOWARD[4:] + _TOWARD[:4]:
        there = present(dr, dc)
        count = count + there.astype(jnp.int32)

        @pl.when(there)
        def _():
            pl.semaphore_signal(barrier, inc=1, device_id=(my_r + dr, my_c + dc), device_id_type=MESH)

    pl.semaphore_wait(barrier, count)

    def copy(k, dr, dc):
        return pltpu.make_async_remote_copy(
            src_ref=e_ref.at[k], dst_ref=o_ref.at[k], send_sem=send_sem.at[k],
            recv_sem=recv_sem.at[k], device_id=(my_r + dr, my_c + dc), device_id_type=MESH)

    for k in _FIRST_FAR:
        dr, dc = _TOWARD[k]

        @pl.when(present(dr, dc))
        def _():
            copy(k, dr, dc).start()

        @pl.when(jnp.logical_not(present(-dr, -dc)))
        def _():
            pltpu.make_async_copy(zero_ref, o_ref.at[k], zero_sem.at[k]).start()

    for k, (dr, dc) in enumerate(_TOWARD):
        @pl.when(present(-dr, -dc))
        def _():
            copy(k, -dr, -dc).wait_recv()

        @pl.when(jnp.logical_not(present(-dr, -dc)))
        def _():
            pltpu.make_async_copy(zero_ref, o_ref.at[k], zero_sem.at[k]).wait()

        @pl.when(present(dr, dc))
        def _():
            copy(k, dr, dc).wait_send()


def exchange(cells, nr, nc):
    ch, h, w = cells.shape
    lanes = max(w, -(-h // 128) * 128)

    def wide(v):
        return jnp.pad(v, ((0, 0), (0, lanes - v.shape[1])))

    top, bottom = cells[:, 0, :], cells[:, h - 1, :]
    left, right = cells[:, :, 0], cells[:, :, w - 1]
    pieces = jnp.stack([
        wide(top), wide(bottom), wide(left), wide(right),
        wide(top[:, :1]), wide(top[:, w - 1:]), wide(bottom[:, :1]), wide(bottom[:, w - 1:]),
    ])
    got = pl.pallas_call(
        functools.partial(_halo_kernel, nr, nc),
        out_shape=jax.ShapeDtypeStruct(pieces.shape, pieces.dtype),
        in_specs=[pl.BlockSpec(memory_space=pl.ANY)] * 2,
        out_specs=pl.BlockSpec(memory_space=pl.ANY),
        scratch_shapes=[pltpu.SemaphoreType.DMA((8,))] * 3,
        compiler_params=pltpu.CompilerParams(collective_id=1, has_side_effects=True),
    )(pieces, jnp.zeros(pieces.shape[1:], pieces.dtype))
    above = got[1, :, :w]
    below = got[0, :, :w]
    from_left = got[3, :, :h]
    from_right = got[2, :, :h]
    top_row = jnp.concatenate([got[7, :, :1], above, got[6, :, :1]], axis=1)
    bottom_row = jnp.concatenate([got[5, :, :1], below, got[4, :, :1]], axis=1)
    middle = jnp.concatenate([from_left[:, :, None], cells, from_right[:, :, None]], axis=2)
    return jnp.concatenate([top_row[:, None, :], middle, bottom_row[:, None, :]], axis=1)


def _sum_kernel(nr, nc, x_ref, o_ref, cpart, rpart, mine, sems, cs_send, cs_recv, r_send, r_recv, cg_send, cg_recv):
    my_r = lax.axis_index("rows")
    my_c = lax.axis_index("cols")

    def col_peer(j):
        return lax.rem(my_c + j, nc)

    def row_peer(j):
        return lax.rem(my_r + j, nr)

    barrier = pltpu.get_barrier_semaphore()

    def greet_c(j, c):
        pl.semaphore_signal(barrier, inc=1, device_id=(my_r, col_peer(j)), device_id_type=MESH)
        return c

    lax.fori_loop(1, nc, greet_c, 0)

    def greet_r(j, c):
        pl.semaphore_signal(barrier, inc=1, device_id=(row_peer(j), my_c), device_id_type=MESH)
        return c

    lax.fori_loop(1, nr, greet_r, 0)
    pl.semaphore_wait(barrier, nc + nr - 2)

    def c_scatter(p, s):
        return pltpu.make_async_remote_copy(
            src_ref=x_ref.at[p], dst_ref=cpart.at[s], send_sem=cs_send.at[p],
            recv_sem=cs_recv.at[s], device_id=(my_r, p), device_id_type=MESH)

    def start_cs(j, c):
        c_scatter(col_peer(j), my_c).start()
        return c

    lax.fori_loop(1, nc, start_cs, 0)
    mine_in = pltpu.make_async_copy(x_ref.at[my_c], cpart.at[my_c], sems.at[0])
    mine_in.start()
    mine_in.wait()

    def wait_cs(j, c):
        c_scatter(my_c, col_peer(j)).wait_recv()
        return c

    lax.fori_loop(1, nc, wait_cs, 0)
    mine[0] = lax.fori_loop(0, nc, lambda s, a: a + cpart[s], jnp.zeros(cpart.shape[1:], jnp.float32))
    own = pltpu.make_async_copy(mine.at[0], rpart.at[my_r], sems.at[0])
    own.start()
    own.wait()

    def r_share(q, s):
        return pltpu.make_async_remote_copy(
            src_ref=rpart.at[s], dst_ref=rpart.at[s], send_sem=r_send.at[q],
            recv_sem=r_recv.at[s], device_id=(q, my_c), device_id_type=MESH)

    def start_r(j, c):
        r_share(row_peer(j), my_r).start()
        return c

    lax.fori_loop(1, nr, start_r, 0)

    def wait_r(j, c):
        r_share(my_r, row_peer(j)).wait_recv()
        return c

    lax.fori_loop(1, nr, wait_r, 0)
    mine[1] = lax.fori_loop(0, nr, lambda s, a: a + rpart[s], jnp.zeros(rpart.shape[1:], jnp.float32))
    own = pltpu.make_async_copy(mine.at[1], o_ref.at[my_c], sems.at[1])
    own.start()
    own.wait()

    def c_gather(p, s):
        return pltpu.make_async_remote_copy(
            src_ref=o_ref.at[s], dst_ref=o_ref.at[s], send_sem=cg_send.at[p],
            recv_sem=cg_recv.at[s], device_id=(my_r, p), device_id_type=MESH)

    def start_cg(j, c):
        c_gather(col_peer(j), my_c).start()
        return c

    lax.fori_loop(1, nc, start_cg, 0)

    def wait_c(j, c):
        c_scatter(col_peer(j), my_c).wait_send()
        c_gather(my_c, col_peer(j)).wait_recv()
        c_gather(col_peer(j), my_c).wait_send()
        return c

    lax.fori_loop(1, nc, wait_c, 0)

    def wait_rs(j, c):
        r_share(row_peer(j), my_r).wait_send()
        return c

    lax.fori_loop(1, nr, wait_rs, 0)


def all_sum(vector, nr, nc):
    length = vector.shape[0]
    rows = -(-length // (nc * 128 * 8)) * 8
    blocks = jnp.pad(vector, (0, nc * rows * 128 - length)).reshape(nc, rows, 128)
    sem = pltpu.SemaphoreType.DMA
    out = pl.pallas_call(
        functools.partial(_sum_kernel, nr, nc),
        out_shape=jax.ShapeDtypeStruct(blocks.shape, jnp.float32),
        in_specs=[pl.BlockSpec(memory_space=pl.ANY)],
        out_specs=pl.BlockSpec(memory_space=pl.ANY),
        scratch_shapes=[
            pltpu.VMEM((nc, rows, 128), jnp.float32),
            pltpu.VMEM((nr, rows, 128), jnp.float32),
            pltpu.VMEM((2, rows, 128), jnp.float32),
            sem((2,)),
            sem((nc,)), sem((nc,)), sem((nr,)), sem((nr,)), sem((nc,)), sem((nc,)),
        ],
        compiler_params=pltpu.CompilerParams(collective_id=0, has_side_effects=True),
    )(blocks)
    return out.reshape(-1)[:length]


def padded_2(cells, sides, width):
    for axis, dim in sides:
        count = lax.axis_size(axis)
        ends = count - 1
        head = lax.slice_in_dim(cells, 0, width, axis=dim)
        tail = lax.slice_in_dim(cells, cells.shape[dim] - width, cells.shape[dim], axis=dim)
        cells = jnp.concatenate(
            [
                lax.ppermute(tail, axis, [(i, (i + 1) % count) for i in range(ends)]),
                cells,
                lax.ppermute(head, axis, [((i + 1) % count, i) for i in range(ends)]),
            ],
            axis=dim,
        )
    return cells


def pointwise(weight, field):
    return jnp.einsum("cm,chw->mhw", weight, field, preferred_element_type=jnp.float32)


def per_channel(vector):
    return vector[:, None, None]


def smooth_act(value):
    return value * jax.nn.sigmoid(value)


def smooth_slope(value):
    sigma = jax.nn.sigmoid(value)
    return sigma * (1.0 + value * (1.0 - sigma))


def spatial_conv(kernel, padded, height, breadth):
    result = jnp.zeros((kernel.shape[2], height, breadth), jnp.float32)
    for tap_row in range(3):
        for tap_col in range(3):
            window = padded[:, tap_row : tap_row + height, tap_col : tap_col + breadth]
            result = result + pointwise(kernel[3 * tap_row + tap_col], window)
    return result


def windows(padded, height, breadth, flip):
    taps = []
    for tap_row in range(3):
        for tap_col in range(3):
            i, j = (2 - tap_row, 2 - tap_col) if flip else (tap_row, tap_col)
            taps.append(padded[:, i : i + height, j : j + breadth])
    return jnp.concatenate(taps, axis=0)


def per_device(
    stem_out,
    tissue,
    w_first,
    w_reduce,
    w_mid,
    w_expand,
    w_short,
    gain_mid,
    shift_mid,
    gain_wide,
    shift_wide,
    upstream,
):
    height, breadth = (stem_out.shape[1], stem_out.shape[2])
    bands, tiles = tissue.shape
    values = tissue.astype(jnp.float32)[:, None, :, None]
    band_keep = jnp.broadcast_to(values, (bands, BLOCK, tiles, BLOCK)).reshape(
        bands * BLOCK, tiles * BLOCK
    )
    row_start = lax.axis_index("rows") * height
    tissue_keep = lax.dynamic_slice_in_dim(band_keep, row_start, height, 0)
    levels = w_mid.shape[0]
    saved_all = []
    feature = stem_out
    for block_index in range(levels):
        w_in = w_first if block_index == 0 else w_reduce[block_index - 1]
        pre_one = pointwise(w_in, feature)
        act_one = smooth_act(
            per_channel(gain_mid[block_index, 0]) * pre_one + per_channel(shift_mid[block_index, 0])
        ).astype(jnp.bfloat16)
        padded = exchange(act_one, lax.axis_size("rows"), lax.axis_size("cols"))
        stacked = windows(padded, height, breadth, False)
        pre_two = jnp.einsum(
            "km,khw->mhw", w_mid[block_index].reshape(-1, w_mid.shape[3]), stacked,
            preferred_element_type=jnp.float32,
        )
        act_two = smooth_act(
            per_channel(gain_mid[block_index, 1]) * pre_two + per_channel(shift_mid[block_index, 1])
        ).astype(jnp.bfloat16)
        pre_three = pointwise(w_expand[block_index], act_two)
        if block_index == 0:
            shortcut = pointwise(w_short, stem_out)
        else:
            shortcut = feature.astype(jnp.float32)
        summed = (
            per_channel(gain_wide[block_index]) * pre_three
            + per_channel(shift_wide[block_index])
            + shortcut
        )
        stored = stacked
        saved_all.append((feature, pre_one, stored, pre_two, act_two, pre_three, summed))
        feature = (smooth_act(summed) * tissue_keep).astype(jnp.bfloat16)
    gradient = upstream
    pieces = [None] * levels
    g_short = None
    for block_index in range(levels - 1, -1, -1):
        feature, pre_one, stored, pre_two, act_two, pre_three, summed = saved_all[block_index]
        w_in = w_first if block_index == 0 else w_reduce[block_index - 1]
        d_sum = gradient.astype(jnp.float32) * tissue_keep * smooth_slope(summed)
        d_gain3 = jnp.sum(d_sum * pre_three, axis=(1, 2))
        d_shift3 = jnp.sum(d_sum, axis=(1, 2))
        d_pre3 = (per_channel(gain_wide[block_index]) * d_sum).astype(jnp.bfloat16)
        g_expand = jnp.einsum("mhw,ohw->mo", act_two, d_pre3, preferred_element_type=jnp.float32)
        d_act2 = jnp.einsum(
            "mo,ohw->mhw", w_expand[block_index], d_pre3, preferred_element_type=jnp.float32
        )
        d_rel2 = d_act2 * smooth_slope(
            per_channel(gain_mid[block_index, 1]) * pre_two + per_channel(shift_mid[block_index, 1])
        )
        d_gain2 = jnp.sum(d_rel2 * pre_two, axis=(1, 2))
        d_shift2 = jnp.sum(d_rel2, axis=(1, 2))
        d_pre2 = (per_channel(gain_mid[block_index, 1]) * d_rel2).astype(jnp.bfloat16)
        g_mid = jnp.einsum(
            "khw,mhw->km", stored, d_pre2, preferred_element_type=jnp.float32
        ).reshape(w_mid.shape[1:])
        grad_pad = exchange(d_pre2, lax.axis_size("rows"), lax.axis_size("cols"))
        d_act1 = jnp.einsum(
            "km,khw->mhw",
            jnp.swapaxes(w_mid[block_index], 1, 2).reshape(-1, w_mid.shape[2]),
            windows(grad_pad, height, breadth, True),
            preferred_element_type=jnp.float32,
        )
        d_rel1 = d_act1 * smooth_slope(
            per_channel(gain_mid[block_index, 0]) * pre_one + per_channel(shift_mid[block_index, 0])
        )
        d_gain1 = jnp.sum(d_rel1 * pre_one, axis=(1, 2))
        d_shift1 = jnp.sum(d_rel1, axis=(1, 2))
        d_pre1 = (per_channel(gain_mid[block_index, 0]) * d_rel1).astype(jnp.bfloat16)
        g_in = jnp.einsum("chw,mhw->cm", feature, d_pre1, preferred_element_type=jnp.float32)
        d_feature = jnp.einsum("cm,mhw->chw", w_in, d_pre1, preferred_element_type=jnp.float32)
        if block_index == 0:
            d_short = d_sum.astype(jnp.bfloat16)
            g_short = jnp.einsum(
                "chw,ohw->co", feature, d_short, preferred_element_type=jnp.float32
            )
            d_feature = d_feature + jnp.einsum(
                "co,ohw->chw", w_short, d_short, preferred_element_type=jnp.float32
            )
        else:
            d_feature = d_feature + d_sum
        gradient = d_feature.astype(jnp.bfloat16)
        pieces[block_index] = [
            g_in,
            g_mid,
            g_expand,
            d_gain1,
            d_shift1,
            d_gain2,
            d_shift2,
            d_gain3,
            d_shift3,
        ]
    flat = []
    for block_index in range(levels):
        for piece in pieces[block_index]:
            flat.append(piece.reshape(-1))
    flat.append(g_short.reshape(-1))
    partial_vector = jnp.concatenate(flat)
    totals = all_sum(partial_vector, lax.axis_size("rows"), lax.axis_size("cols"))
    pixel_count = height * breadth * lax.axis_size("rows") * lax.axis_size("cols")
    scale = 1.0 / jnp.sqrt(jnp.float32(pixel_count))
    return (gradient, totals * scale)


def solution(mesh):
    in_specs = (
        P(None, "rows", "cols"),
        P(None, "cols"),
        P(),
        P(),
        P(),
        P(),
        P(),
        P(),
        P(),
        P(),
        P(),
        P(None, "rows", "cols"),
    )
    out_specs = (P(None, "rows", "cols"), P())
    return jax.shard_map(
        per_device, mesh=mesh, in_specs=in_specs, out_specs=out_specs, check_vma=False
    )
```

```python
import functools

import numpy as np
import jax
import jax.numpy as jnp
from jax import lax
from jax.experimental import pallas as pl
from jax.experimental.pallas import tpu as pltpu
from jax.sharding import PartitionSpec as P

MESH = pl.DeviceIdType.MESH

BLOCK = 64


_TOWARD = ((-1, 0), (1, 0), (0, -1), (0, 1), (-1, -1), (-1, 1), (1, -1), (1, 1))
_FIRST_FAR = (4, 5, 6, 7, 0, 1, 2, 3)


def _halo_kernel(nr, nc, e_ref, zero_ref, o_ref, send_sem, recv_sem, zero_sem):
    my_r = lax.axis_index("rows")
    my_c = lax.axis_index("cols")

    def present(dr, dc):
        ok = True
        if dr:
            ok = jnp.logical_and(ok, jnp.logical_and(my_r + dr >= 0, my_r + dr < nr))
        if dc:
            ok = jnp.logical_and(ok, jnp.logical_and(my_c + dc >= 0, my_c + dc < nc))
        return ok

    barrier = pltpu.get_barrier_semaphore()
    count = 0
    for dr, dc in _TOWARD[4:] + _TOWARD[:4]:
        there = present(dr, dc)
        count = count + there.astype(jnp.int32)

        @pl.when(there)
        def _():
            pl.semaphore_signal(barrier, inc=1, device_id=(my_r + dr, my_c + dc), device_id_type=MESH)

    pl.semaphore_wait(barrier, count)

    def copy(k, dr, dc):
        return pltpu.make_async_remote_copy(
            src_ref=e_ref.at[k], dst_ref=o_ref.at[k], send_sem=send_sem.at[k],
            recv_sem=recv_sem.at[k], device_id=(my_r + dr, my_c + dc), device_id_type=MESH)

    for k in _FIRST_FAR:
        dr, dc = _TOWARD[k]

        @pl.when(present(dr, dc))
        def _():
            copy(k, dr, dc).start()

        @pl.when(jnp.logical_not(present(-dr, -dc)))
        def _():
            pltpu.make_async_copy(zero_ref, o_ref.at[k], zero_sem.at[k]).start()

    for k, (dr, dc) in enumerate(_TOWARD):
        @pl.when(present(-dr, -dc))
        def _():
            copy(k, -dr, -dc).wait_recv()

        @pl.when(jnp.logical_not(present(-dr, -dc)))
        def _():
            pltpu.make_async_copy(zero_ref, o_ref.at[k], zero_sem.at[k]).wait()

        @pl.when(present(dr, dc))
        def _():
            copy(k, dr, dc).wait_send()


def exchange(cells, nr, nc):
    ch, h, w = cells.shape
    lanes = max(w, -(-h // 128) * 128)

    def wide(v):
        return jnp.pad(v, ((0, 0), (0, lanes - v.shape[1])))

    top, bottom = cells[:, 0, :], cells[:, h - 1, :]
    left, right = cells[:, :, 0], cells[:, :, w - 1]
    pieces = jnp.stack([
        wide(top), wide(bottom), wide(left), wide(right),
        wide(top[:, :1]), wide(top[:, w - 1:]), wide(bottom[:, :1]), wide(bottom[:, w - 1:]),
    ])
    got = pl.pallas_call(
        functools.partial(_halo_kernel, nr, nc),
        out_shape=jax.ShapeDtypeStruct(pieces.shape, pieces.dtype),
        in_specs=[pl.BlockSpec(memory_space=pl.ANY)] * 2,
        out_specs=pl.BlockSpec(memory_space=pl.ANY),
        scratch_shapes=[pltpu.SemaphoreType.DMA((8,))] * 3,
        compiler_params=pltpu.CompilerParams(collective_id=1, has_side_effects=True),
    )(pieces, jnp.zeros(pieces.shape[1:], pieces.dtype))
    above = got[1, :, :w]
    below = got[0, :, :w]
    from_left = got[3, :, :h]
    from_right = got[2, :, :h]
    top_row = jnp.concatenate([got[7, :, :1], above, got[6, :, :1]], axis=1)
    bottom_row = jnp.concatenate([got[5, :, :1], below, got[4, :, :1]], axis=1)
    middle = jnp.concatenate([from_left[:, :, None], cells, from_right[:, :, None]], axis=2)
    return jnp.concatenate([top_row[:, None, :], middle, bottom_row[:, None, :]], axis=1)


def _sum_kernel(nr, nc, scale, x_ref, o_ref, cpart, rpart, mine, sems, cs_send, cs_recv, r_send, r_recv, cg_send, cg_recv):
    my_r = lax.axis_index("rows")
    my_c = lax.axis_index("cols")

    def col_peer(j):
        return lax.rem(my_c + j, nc)

    def row_peer(j):
        return lax.rem(my_r + j, nr)

    barrier = pltpu.get_barrier_semaphore()

    def greet_c(j, c):
        pl.semaphore_signal(barrier, inc=1, device_id=(my_r, col_peer(j)), device_id_type=MESH)
        return c

    lax.fori_loop(1, nc, greet_c, 0)

    def greet_r(j, c):
        pl.semaphore_signal(barrier, inc=1, device_id=(row_peer(j), my_c), device_id_type=MESH)
        return c

    lax.fori_loop(1, nr, greet_r, 0)
    pl.semaphore_wait(barrier, nc + nr - 2)

    def c_scatter(p, s):
        return pltpu.make_async_remote_copy(
            src_ref=x_ref.at[p], dst_ref=cpart.at[s], send_sem=cs_send.at[p],
            recv_sem=cs_recv.at[s], device_id=(my_r, p), device_id_type=MESH)

    def start_cs(j, c):
        c_scatter(col_peer(j), my_c).start()
        return c

    lax.fori_loop(1, nc, start_cs, 0)
    mine_in = pltpu.make_async_copy(x_ref.at[my_c], cpart.at[my_c], sems.at[0])
    mine_in.start()
    mine_in.wait()

    def wait_cs(j, c):
        c_scatter(my_c, col_peer(j)).wait_recv()
        return c

    lax.fori_loop(1, nc, wait_cs, 0)
    mine[0] = lax.fori_loop(0, nc, lambda s, a: a + cpart[s], jnp.zeros(cpart.shape[1:], jnp.float32))
    own = pltpu.make_async_copy(mine.at[0], rpart.at[my_r], sems.at[0])
    own.start()
    own.wait()

    def r_share(q, s):
        return pltpu.make_async_remote_copy(
            src_ref=rpart.at[s], dst_ref=rpart.at[s], send_sem=r_send.at[q],
            recv_sem=r_recv.at[s], device_id=(q, my_c), device_id_type=MESH)

    def start_r(j, c):
        r_share(row_peer(j), my_r).start()
        return c

    lax.fori_loop(1, nr, start_r, 0)

    def wait_r(j, c):
        r_share(my_r, row_peer(j)).wait_recv()
        return c

    lax.fori_loop(1, nr, wait_r, 0)
    mine[1] = scale * lax.fori_loop(0, nr, lambda s, a: a + rpart[s], jnp.zeros(rpart.shape[1:], jnp.float32))
    own = pltpu.make_async_copy(mine.at[1], o_ref.at[my_c], sems.at[1])
    own.start()
    own.wait()

    def c_gather(p, s):
        return pltpu.make_async_remote_copy(
            src_ref=o_ref.at[s], dst_ref=o_ref.at[s], send_sem=cg_send.at[p],
            recv_sem=cg_recv.at[s], device_id=(my_r, p), device_id_type=MESH)

    def start_cg(j, c):
        c_gather(col_peer(j), my_c).start()
        return c

    lax.fori_loop(1, nc, start_cg, 0)

    def wait_c(j, c):
        c_scatter(col_peer(j), my_c).wait_send()
        c_gather(my_c, col_peer(j)).wait_recv()
        c_gather(col_peer(j), my_c).wait_send()
        return c

    lax.fori_loop(1, nc, wait_c, 0)

    def wait_rs(j, c):
        r_share(row_peer(j), my_r).wait_send()
        return c

    lax.fori_loop(1, nr, wait_rs, 0)


def all_sum(vector, nr, nc, scale):
    length = vector.shape[0]
    rows = -(-length // (nc * 128 * 8)) * 8
    blocks = jnp.pad(vector, (0, nc * rows * 128 - length)).reshape(nc, rows, 128)
    sem = pltpu.SemaphoreType.DMA
    out = pl.pallas_call(
        functools.partial(_sum_kernel, nr, nc, scale),
        out_shape=jax.ShapeDtypeStruct(blocks.shape, jnp.float32),
        in_specs=[pl.BlockSpec(memory_space=pl.ANY)],
        out_specs=pl.BlockSpec(memory_space=pltpu.VMEM),
        scratch_shapes=[
            pltpu.VMEM((nc, rows, 128), jnp.float32),
            pltpu.VMEM((nr, rows, 128), jnp.float32),
            pltpu.VMEM((2, rows, 128), jnp.float32),
            sem((2,)),
            sem((nc,)), sem((nc,)), sem((nr,)), sem((nr,)), sem((nc,)), sem((nc,)),
        ],
        compiler_params=pltpu.CompilerParams(collective_id=0, has_side_effects=True),
    )(blocks)
    return out.reshape(-1)[:length]


def padded_2(cells, sides, width):
    for axis, dim in sides:
        count = lax.axis_size(axis)
        ends = count - 1
        head = lax.slice_in_dim(cells, 0, width, axis=dim)
        tail = lax.slice_in_dim(cells, cells.shape[dim] - width, cells.shape[dim], axis=dim)
        cells = jnp.concatenate(
            [
                lax.ppermute(tail, axis, [(i, (i + 1) % count) for i in range(ends)]),
                cells,
                lax.ppermute(head, axis, [((i + 1) % count, i) for i in range(ends)]),
            ],
            axis=dim,
        )
    return cells


def pointwise(weight, field):
    return jnp.einsum("cm,chw->mhw", weight, field, preferred_element_type=jnp.float32)


def per_channel(vector):
    return vector[:, None, None]


def smooth_act(value):
    return value * jax.nn.sigmoid(value)


def smooth_slope(value):
    sigma = jax.nn.sigmoid(value)
    return sigma * (1.0 + value * (1.0 - sigma))


def spatial_conv(kernel, padded, height, breadth):
    result = jnp.zeros((kernel.shape[2], height, breadth), jnp.float32)
    for tap_row in range(3):
        for tap_col in range(3):
            window = padded[:, tap_row : tap_row + height, tap_col : tap_col + breadth]
            result = result + pointwise(kernel[3 * tap_row + tap_col], window)
    return result


def windows(padded, height, breadth, flip):
    taps = []
    for tap_row in range(3):
        for tap_col in range(3):
            i, j = (2 - tap_row, 2 - tap_col) if flip else (tap_row, tap_col)
            taps.append(padded[:, i : i + height, j : j + breadth])
    return jnp.concatenate(taps, axis=0)


def per_device(
    stem_out,
    tissue,
    w_first,
    w_reduce,
    w_mid,
    w_expand,
    w_short,
    gain_mid,
    shift_mid,
    gain_wide,
    shift_wide,
    upstream,
):
    height, breadth = (stem_out.shape[1], stem_out.shape[2])
    bands, tiles = tissue.shape
    values = tissue.astype(jnp.float32)[:, None, :, None]
    band_keep = jnp.broadcast_to(values, (bands, BLOCK, tiles, BLOCK)).reshape(
        bands * BLOCK, tiles * BLOCK
    )
    row_start = lax.axis_index("rows") * height
    tissue_keep = lax.dynamic_slice_in_dim(band_keep, row_start, height, 0)
    levels = w_mid.shape[0]
    saved_all = []
    feature = stem_out
    for block_index in range(levels):
        w_in = w_first if block_index == 0 else w_reduce[block_index - 1]
        pre_one = pointwise(w_in, feature)
        act_one = smooth_act(
            per_channel(gain_mid[block_index, 0]) * pre_one + per_channel(shift_mid[block_index, 0])
        ).astype(jnp.bfloat16)
        padded = exchange(act_one, lax.axis_size("rows"), lax.axis_size("cols"))
        stacked = windows(padded, height, breadth, False)
        pre_two = jnp.einsum(
            "km,khw->mhw", w_mid[block_index].reshape(-1, w_mid.shape[3]), stacked,
            preferred_element_type=jnp.float32,
        )
        act_two = smooth_act(
            per_channel(gain_mid[block_index, 1]) * pre_two + per_channel(shift_mid[block_index, 1])
        ).astype(jnp.bfloat16)
        pre_three = pointwise(w_expand[block_index], act_two)
        if block_index == 0:
            shortcut = pointwise(w_short, stem_out)
        else:
            shortcut = feature.astype(jnp.float32)
        summed = (
            per_channel(gain_wide[block_index]) * pre_three
            + per_channel(shift_wide[block_index])
            + shortcut
        )
        stored = stacked
        saved_all.append((feature, pre_one, stored, pre_two, act_two, pre_three, summed))
        feature = (smooth_act(summed) * tissue_keep).astype(jnp.bfloat16)
    gradient = upstream
    pieces = [None] * levels
    g_short = None
    for block_index in range(levels - 1, -1, -1):
        feature, pre_one, stored, pre_two, act_two, pre_three, summed = saved_all[block_index]
        w_in = w_first if block_index == 0 else w_reduce[block_index - 1]
        d_sum = gradient.astype(jnp.float32) * tissue_keep * smooth_slope(summed)
        d_gain3 = jnp.sum(d_sum * pre_three, axis=(1, 2))
        d_shift3 = jnp.sum(d_sum, axis=(1, 2))
        d_pre3 = (per_channel(gain_wide[block_index]) * d_sum).astype(jnp.bfloat16)
        g_expand = jnp.einsum("mhw,ohw->mo", act_two, d_pre3, preferred_element_type=jnp.float32)
        d_act2 = jnp.einsum(
            "mo,ohw->mhw", w_expand[block_index], d_pre3, preferred_element_type=jnp.float32
        )
        d_rel2 = d_act2 * smooth_slope(
            per_channel(gain_mid[block_index, 1]) * pre_two + per_channel(shift_mid[block_index, 1])
        )
        d_gain2 = jnp.sum(d_rel2 * pre_two, axis=(1, 2))
        d_shift2 = jnp.sum(d_rel2, axis=(1, 2))
        d_pre2 = (per_channel(gain_mid[block_index, 1]) * d_rel2).astype(jnp.bfloat16)
        g_mid = jnp.einsum(
            "khw,mhw->km", stored, d_pre2, preferred_element_type=jnp.float32
        ).reshape(w_mid.shape[1:])
        grad_pad = exchange(d_pre2, lax.axis_size("rows"), lax.axis_size("cols"))
        d_act1 = jnp.einsum(
            "km,khw->mhw",
            jnp.swapaxes(w_mid[block_index], 1, 2).reshape(-1, w_mid.shape[2]),
            windows(grad_pad, height, breadth, True),
            preferred_element_type=jnp.float32,
        )
        d_rel1 = d_act1 * smooth_slope(
            per_channel(gain_mid[block_index, 0]) * pre_one + per_channel(shift_mid[block_index, 0])
        )
        d_gain1 = jnp.sum(d_rel1 * pre_one, axis=(1, 2))
        d_shift1 = jnp.sum(d_rel1, axis=(1, 2))
        d_pre1 = (per_channel(gain_mid[block_index, 0]) * d_rel1).astype(jnp.bfloat16)
        g_in = jnp.einsum("chw,mhw->cm", feature, d_pre1, preferred_element_type=jnp.float32)
        d_feature = jnp.einsum("cm,mhw->chw", w_in, d_pre1, preferred_element_type=jnp.float32)
        if block_index == 0:
            d_short = d_sum.astype(jnp.bfloat16)
            g_short = jnp.einsum(
                "chw,ohw->co", feature, d_short, preferred_element_type=jnp.float32
            )
            d_feature = d_feature + jnp.einsum(
                "co,ohw->chw", w_short, d_short, preferred_element_type=jnp.float32
            )
        else:
            d_feature = d_feature + d_sum
        gradient = d_feature.astype(jnp.bfloat16)
        pieces[block_index] = [
            g_in,
            g_mid,
            g_expand,
            d_gain1,
            d_shift1,
            d_gain2,
            d_shift2,
            d_gain3,
            d_shift3,
        ]
    flat = []
    for block_index in range(levels):
        for piece in pieces[block_index]:
            flat.append(piece.reshape(-1))
    flat.append(g_short.reshape(-1))
    partial_vector = jnp.concatenate(flat)
    pixel_count = height * breadth * lax.axis_size("rows") * lax.axis_size("cols")
    scale = float(1.0 / np.sqrt(np.float32(pixel_count)))
    totals = all_sum(partial_vector, lax.axis_size("rows"), lax.axis_size("cols"), scale)
    return (gradient, totals)


def solution(mesh):
    in_specs = (
        P(None, "rows", "cols"),
        P(None, "cols"),
        P(),
        P(),
        P(),
        P(),
        P(),
        P(),
        P(),
        P(),
        P(),
        P(None, "rows", "cols"),
    )
    out_specs = (P(None, "rows", "cols"), P())
    return jax.shard_map(
        per_device, mesh=mesh, in_specs=in_specs, out_specs=out_specs, check_vma=False
    )
```
